32 devices in a mesh: section: 4 (over z), st: 4 (over y, core), dp: 2 (over x).
Axes of the slice: x: 2, y: 2, z: 4, core: 2. Of those that a mesh axis runs over, the one named last changes fastest.
Arguments:
- saved_qkv: bfloat16 [4, 2, 3, 128, 48, 128], P('section', 'dp', None, None, 'st'), may hold values from -9 to 9
- positions: int32 [4, 2, 128], P('section', 'dp'), may hold values from 0 to 127, as said below
- w_out: bfloat16 [4, 6144, 6144], P('section', None, 'st'), may hold values from -0.078125 to 0.078125
- grad_out: bfloat16 [4, 2, 128, 6144], P('section', 'dp', None, 'st'), may hold values from -6 to 6
Outputs:
- grad_weight: bfloat16 [4, 6144, 6144], P('section', 'dp', 'st')
- upstream: bfloat16 [4, 2, 3, 128, 48, 128], P('section', 'dp', None, None, 'st')
The draws below stay inside these ranges and needn't reach their ends.
Inputs may be any that keep to these rules, and one draw needn't show every extreme that they name: `positions`: each row holds every number 0 to 127 once.
All inputs are finite; a program needn't handle non-finite values.
Results may differ from the reference program's by a relative error of at most 0.0095.
Values may be sent and summed in bfloat16 or wider, within the bound.
No kernel may reach another device: no remote copies, remote signals or barrier semaphores. Data moves between devices by JAX's collectives and lax.ppermute only.
A program may use at most 128 MiB of HBM per device.

```python
import math
import jax
import jax.numpy as jnp
from jax import lax

D = 6144
HEADS = 48
DH = 128
SEQ = 128
SECTIONS = 4
REPLICAS = 2


def order_tables(key):
    row_count = SECTIONS * REPLICAS
    row_keys = jax.random.split(jax.random.fold_in(key, 17), row_count)
    permuted = jax.vmap(lambda single: jax.random.permutation(single, SEQ))(row_keys)
    return permuted.reshape(SECTIONS, REPLICAS, SEQ).astype(jnp.int32)


def draw_positions(key, part):
    return order_tables(key)


def draw_saved_qkv(key, part):
    dims_all = (SECTIONS, REPLICAS, 3, SEQ, HEADS, DH)
    base_key = jax.random.fold_in(key, 29)
    return jnp.clip(jax.random.normal(base_key, dims_all, jnp.float32), -4.0, 4.0).astype(jnp.bfloat16)


def spiked(values, rng, source, target, parts, factor):
    def block_of(dim):
        return (jnp.arange(values.shape[dim]) // (values.shape[dim] // parts)).reshape((-1,) + (1,) * (values.ndim - 1 - dim))

    near = jax.random.permutation(rng, parts)[block_of(target)]
    other_side = (block_of(target) + parts // 2) % parts
    return jnp.where((block_of(source) == near) | (block_of(source) == other_side), factor * values, values)


def block_levels(stream_key, shape, shards, low, high):
    def one(position, shards_of):
        heights = jax.random.uniform(jax.random.fold_in(jax.random.fold_in(stream_key, 6), position), (shards_of,), jnp.float32, low / len(shards), high / len(shards))
        return jnp.repeat(jnp.exp(heights), shape[position] // shards_of).reshape((-1,) + (1,) * (len(shape) - position - 1))

    loudness = one(*shards[0])
    for cut in shards[1:]:
        loudness = loudness * one(*cut)
    return loudness


def bell_draw(own_key, dims, scale, bound, cuts=(), held_as=jnp.bfloat16):
    result = scale * jax.random.normal(own_key, dims, jnp.float32)
    if cuts:
        result = result * block_levels(own_key, dims, cuts, -0.22, 0.18)
    return jnp.clip(result, -bound, bound).astype(held_as)


def gaussian_with(rng, dims, deviation, bound, cuts, heavy, dtype=jnp.bfloat16):
    drawn = deviation * jax.random.normal(rng, dims, jnp.float32)
    if cuts:
        drawn = drawn * block_levels(rng, dims, cuts, -0.22, 0.18)
    return jnp.clip(spiked(drawn, jax.random.fold_in(rng, 3), *heavy), -bound, bound).astype(dtype)


def setup_inputs(seed: int = 0) -> dict:
    splits = jax.random.split(jax.random.key(seed), 5)
    saved_qkv = draw_saved_qkv(jax.random.fold_in(splits[4], 71), 0)
    positions = draw_positions(jax.random.fold_in(splits[4], 71), 0)
    w_out = bell_draw(splits[2], (SECTIONS, D, HEADS * DH), (HEADS * DH) ** -0.5, 0.078125, ((0, 4), (2, 4)))
    grad_out = gaussian_with(splits[3], (SECTIONS, REPLICAS, SEQ, D), 1.0, 6.0, ((0, 4), (1, 2), (3, 4)), (1, 3, 2, 2.0))
    return dict(saved_qkv=saved_qkv, positions=positions, w_out=w_out, grad_out=grad_out)


def attend_backward(qkv_rows, token_pos, w_section, grad_rows):
    inv_root = 1.0 / math.sqrt(qkv_rows.shape[-1])
    queries = qkv_rows[0].astype(jnp.float32)
    key_rows = qkv_rows[1].astype(jnp.float32)
    values = qkv_rows[2].astype(jnp.float32)
    scores = jnp.einsum('qhd,khd->hqk', queries, key_rows) * inv_root
    visible = token_pos[None, :] <= token_pos[:, None]
    scores = jnp.where(visible[None], scores, -1e+30)
    highest = lax.optimization_barrier(jnp.max(scores, axis=2, keepdims=True))
    exponent = jnp.exp(scores - highest)
    softmax_out = exponent / lax.optimization_barrier(jnp.sum(exponent, axis=2, keepdims=True))
    weights_bf = softmax_out.astype(jnp.bfloat16)
    attended = jnp.einsum('hqk,khd->qhd', weights_bf.astype(jnp.float32), values).astype(jnp.bfloat16)
    seq_len = attended.shape[0]
    flat_att = attended.reshape(seq_len, -1)
    d_flat = jnp.dot(grad_rows, w_section, preferred_element_type=jnp.float32).astype(jnp.bfloat16)
    d_heads = d_flat.reshape(attended.shape).astype(jnp.float32)
    d_values = jnp.einsum('hqk,qhd->khd', weights_bf.astype(jnp.float32), d_heads).astype(jnp.bfloat16)
    d_weights = jnp.einsum('qhd,khd->hqk', d_heads, values)
    row_dot = lax.optimization_barrier(jnp.sum(softmax_out * d_weights, axis=2, keepdims=True))
    d_scores = (softmax_out * (d_weights - row_dot)).astype(jnp.bfloat16).astype(jnp.float32)
    d_queries = (jnp.einsum('hqk,khd->qhd', d_scores, key_rows) * inv_root).astype(jnp.bfloat16)
    d_keys = (jnp.einsum('hqk,qhd->khd', d_scores, queries) * inv_root).astype(jnp.bfloat16)
    return (flat_att, jnp.stack([d_queries, d_keys, d_values]))

def reference(saved_qkv, positions, w_out, grad_out):

    def per_section(section_items):
        qkv_section, pos_section, w_section, grad_section = section_items

        def per_replica(running, replica_items):
            qkv_rows, token_pos, grad_rows = replica_items
            flat_att, grad_qkv = attend_backward(qkv_rows, token_pos, w_section, grad_rows)
            partial_term = jnp.dot(grad_rows.T, flat_att, preferred_element_type=jnp.float32)
            rounded = lax.optimization_barrier(partial_term.astype(jnp.bfloat16))
            return (running + rounded.astype(jnp.float32), grad_qkv)
        start_sum = jnp.zeros((w_section.shape[0], w_section.shape[1]), jnp.float32)
        running, grad_all = lax.scan(per_replica, start_sum, (qkv_section, pos_section, grad_section))
        return (running.astype(jnp.bfloat16), grad_all)
    grad_weight, grad_all = lax.map(per_section, (saved_qkv, positions, w_out, grad_out))
    upstream = jnp.concatenate([grad_all[1:], jnp.zeros_like(grad_all[:1])], axis=0)
    return (grad_weight, upstream)
```

```python
import functools
import math

import jax
import jax.numpy as jnp
from jax import lax
from jax.experimental import pallas as pl
from jax.experimental.pallas import tpu as pltpu
from jax.sharding import PartitionSpec as P

F32 = jnp.float32
BF16 = jnp.bfloat16


def dot(a, b, dims):
    return lax.dot_general(a, b, ((dims[0], dims[1]), ((), ())), preferred_element_type=F32)


def rotate(value, axis, steps):
    count = lax.axis_size(axis)
    return lax.ppermute(value, axis, [(i, (i + steps) % count) for i in range(count)])


def swap(value, axis):
    count = lax.axis_size(axis)
    return lax.ppermute(value, axis, [(i, i ^ 1) for i in range(count)])


def down(value, axis):
    count = lax.axis_size(axis)
    return lax.ppermute(value, axis, [(i, i - 1) for i in range(1, count)])


def pick(index, options):
    result = options[0]
    for number, option in enumerate(options[1:], 1):
        result = jnp.where(index == number, option, result)
    return result


def rows_as_lanes(pos_ref):
    seq = pos_ref.shape[-1]
    lanes = jnp.broadcast_to(pos_ref[...].astype(F32), (seq, seq))
    return lanes, lanes.T


def forward_kernel(pos_ref, qkv_ref, out_ref):
    _, heads, _, width = qkv_ref.shape
    scale = 1.0 / math.sqrt(width)
    across, along = rows_as_lanes(pos_ref)
    visible = across <= along
    for head in range(heads):
        scores = dot(qkv_ref[0, head], qkv_ref[1, head], ((1,), (1,))) * scale
        scores = jnp.where(visible, scores, -1e30)
        exponent = jnp.exp(scores - jnp.max(scores, axis=1, keepdims=True))
        probs = exponent / jnp.sum(exponent, axis=1, keepdims=True)
        attended = dot(probs.astype(BF16), qkv_ref[2, head], ((1,), (0,)))
        out_ref[:, head * width : (head + 1) * width] = attended.astype(BF16)


def head_block(heads, most=4):
    return max(size for size in range(1, most + 1) if heads % size == 0)


def forward(pos, qkv):
    _, heads, seq, width = qkv.shape
    block = head_block(heads)
    return pl.pallas_call(
        forward_kernel,
        name="forward",
        grid=(heads // block,),
        in_specs=[
            pl.BlockSpec((1, seq), lambda h: (0, 0)),
            pl.BlockSpec((3, block, seq, width), lambda h: (0, h, 0, 0)),
        ],
        out_specs=pl.BlockSpec((seq, block * width), lambda h: (0, h)),
        out_shape=jax.ShapeDtypeStruct((seq, heads * width), BF16),
    )(pos, qkv)


def backward_kernel(pos_ref, qkv_ref, grad_ref, out_ref):
    _, heads, _, width = qkv_ref.shape
    scale = 1.0 / math.sqrt(width)
    across, along = rows_as_lanes(pos_ref)
    visible = along <= across
    for head in range(heads):
        query, key, value = qkv_ref[0, head], qkv_ref[1, head], qkv_ref[2, head]
        grad = grad_ref[:, head * width : (head + 1) * width]
        scores = dot(key, query, ((1,), (1,))) * scale
        scores = jnp.where(visible, scores, -1e30)
        exponent = jnp.exp(scores - jnp.max(scores, axis=0, keepdims=True))
        probs = exponent / jnp.sum(exponent, axis=0, keepdims=True)
        d_value = dot(probs.astype(BF16), grad, ((1,), (0,)))
        d_probs = dot(value, grad, ((1,), (1,)))
        row_dot = jnp.sum(probs * d_probs, axis=0, keepdims=True)
        d_scores = (probs * (d_probs - row_dot)).astype(BF16)
        d_key = dot(d_scores, query, ((1,), (0,))) * scale
        d_query = dot(d_scores, key, ((0,), (0,))) * scale
        out_ref[0, head] = d_query.astype(BF16)
        out_ref[1, head] = d_key.astype(BF16)
        out_ref[2, head] = d_value.astype(BF16)


def backward(pos, qkv, grad, first, count, total):
    _, _, seq, width = qkv.shape
    block = head_block(math.gcd(count, first) if first else count)
    start = first // block
    return pl.pallas_call(
        backward_kernel,
        name="backward",
        grid=(count // block,),
        in_specs=[
            pl.BlockSpec((1, seq), lambda h: (0, 0)),
            pl.BlockSpec((3, block, seq, width), lambda h: (0, h + start, 0, 0)),
            pl.BlockSpec((seq, block * width), lambda h: (0, h)),
        ],
        out_specs=pl.BlockSpec((3, block, seq, width), lambda h: (0, h, 0, 0)),
        out_shape=jax.ShapeDtypeStruct((3, total, seq, width), BF16),
    )(pos, qkv, grad)


def fill_kernel(late_ref, whole_ref, out_ref, sem):
    first = out_ref.shape[1] - late_ref.shape[1]
    copies = [
        pltpu.make_async_copy(late_ref.at[i], out_ref.at[i, pl.ds(first, late_ref.shape[1])], sem.at[i])
        for i in range(3)
    ]
    for copy in copies:
        copy.start()
    for copy in copies:
        copy.wait()


def fill(late, whole):
    return pl.pallas_call(
        fill_kernel,
        name="fill",
        in_specs=[pl.BlockSpec(memory_space=pl.ANY)] * 2,
        out_specs=pl.BlockSpec(memory_space=pl.ANY),
        out_shape=jax.ShapeDtypeStruct(whole.shape, whole.dtype),
        scratch_shapes=[pltpu.SemaphoreType.DMA((3,))],
        input_output_aliases={1: 0},
    )(late, whole)


def project_kernel(has_total, splits, shard_ref, *refs):
    refs = list(refs)
    grad_ref, weight_ref = refs[:2]
    total_ref = refs[2] if has_total else None
    outs = refs[3:] if has_total else refs[2:]
    scratch = None
    if splits:
        scratch = outs.pop()
    acc_ref = scratch if splits else outs[0]
    step = pl.program_id(0)
    product = jnp.dot(grad_ref[...], weight_ref[...], preferred_element_type=F32)

    @pl.when(step == 0)
    def _():
        acc_ref[...] = product + total_ref[...] if has_total else product

    @pl.when(step > 0)
    def _():
        acc_ref[...] += product

    if splits:

        @pl.when(step == pl.num_programs(0) - 1)
        def _():
            at = 0
            for out, size in zip(outs, splits):
                out[...] = acc_ref[:, at : at + size].astype(BF16)
                at += size


def project(shard, grad, weight, total, splits):
    seq, features = grad.shape
    columns = weight.shape[1]
    steps = max(1, features // 512)
    while features % steps or (features // steps) % 128:
        steps -= 1
    depth = features // steps
    whole = lambda k, s: (0, 0)
    in_specs = [
        pl.BlockSpec((seq, depth), lambda k, s: (0, k)),
        pl.BlockSpec((depth, columns), lambda k, s: (s[0] * steps + k, 0)),
    ]
    args = [grad, weight]
    if total is not None:
        in_specs.append(pl.BlockSpec((seq, columns), whole))
        args.append(total)
    if splits:
        out_specs = [pl.BlockSpec((seq, size), whole) for size in splits]
        out_shape = [jax.ShapeDtypeStruct((seq, size), BF16) for size in splits]
        scratch = [pltpu.VMEM((seq, columns), F32)]
    else:
        out_specs = pl.BlockSpec((seq, columns), whole)
        out_shape = jax.ShapeDtypeStruct((seq, columns), F32)
        scratch = []
    return pl.pallas_call(
        functools.partial(project_kernel, total is not None, splits),
        name="project",
        grid_spec=pltpu.PrefetchScalarGridSpec(
            num_scalar_prefetch=1,
            grid=(steps,),
            in_specs=in_specs,
            out_specs=out_specs,
            scratch_shapes=scratch,
        ),
        out_shape=out_shape,
    )(shard.reshape(1).astype(jnp.int32), *args)


def weight_kernel(slots, replicas, blocks, rows_ref, *refs):
    acts = refs[:replicas]
    grads = refs[replicas : replicas * (1 + slots)]
    out_ref, stacked = refs[-2:]
    step = pl.program_id(0)
    seq = acts[0].shape[0]

    @pl.when(step == 0)
    def _():
        for number, act in enumerate(acts):
            stacked[number * seq : (number + 1) * seq] = act[...]

    for slot in range(slots):

        @pl.when(step // blocks == slot)
        def _():
            own = grads[slot * replicas : (slot + 1) * replicas]
            left = jnp.concatenate([ref[...] for ref in own], axis=0)
            out_ref[...] = dot(left, stacked[...], ((0,), (0,))).astype(BF16)


def weight_gradient(rows, acts, grads):
    replicas = len(acts)
    slots = len(grads)
    seq, columns = acts[0].shape
    features = grads[0][0].shape[1]
    blocks = max(1, features // 512)
    while features % blocks or (features // blocks) % 128:
        blocks -= 1
    size = features // blocks
    in_specs = [pl.BlockSpec((seq, columns), lambda s, p: (0, 0))] * replicas
    for slot in range(slots):
        spec = pl.BlockSpec(
            (seq, size),
            lambda s, p, slot=slot: (0, jnp.clip(s - slot * blocks, 0, blocks - 1)),
        )
        in_specs += [spec] * replicas
    return pl.pallas_call(
        functools.partial(weight_kernel, slots, replicas, blocks),
        name="weight_gradient",
        grid_spec=pltpu.PrefetchScalarGridSpec(
            num_scalar_prefetch=1,
            grid=(slots * blocks,),
            in_specs=in_specs,
            out_specs=pl.BlockSpec(
                (size, columns), lambda s, p: (p[s // blocks] * blocks + s % blocks, 0)
            ),
            scratch_shapes=[pltpu.VMEM((replicas * seq, columns), BF16)],
        ),
        out_shape=jax.ShapeDtypeStruct((slots * features, columns), BF16),
    )(rows, *acts, *[ref for slot in grads for ref in slot])


def local(saved_qkv, positions, w_out, grad_out):
    qkv = saved_qkv[0, 0].transpose(0, 2, 1, 3)
    pos = positions[0]
    weight = w_out[0]
    heads, seq, width = qkv.shape[1:]
    early = max(1, (heads * 7) // 12)
    late = heads - early
    shards = lax.axis_size("st")
    replicas = lax.axis_size("dp")
    chips = shards // 2
    me = lax.axis_index("st")
    chip, core = me // 2, me % 2
    replica = lax.axis_index("dp")
    per_replica = chips // replicas

    qkv_above = down(qkv[:, :early], "section")
    pos_above = down(pos, "section")

    same = [grad_out[0, 0]]
    for step in range(1, chips):
        same.append(rotate(same[0], "st", 2 * step))
    other = [swap(value, "st") for value in same]

    attended = forward(pos, qkv)
    acts = [attended] + [rotate(attended, "dp", step) for step in range(1, replicas)]

    total = None
    for step in range(chips):
        source = 2 * ((chip - step) % chips)
        for shard, value in ((source + core, same[step]), (source + 1 - core, other[step])):
            last = step == chips - 1 and value is other[step]
            splits = (early * width, late * width) if last else None
            total = project(shard, value, weight, total, splits)
    d_early, d_late = total
    d_above = down(d_early, "section")
    grads_late = backward(pos, qkv[:, early:], d_late, 0, late, late)
    late_above = down(grads_late, "section")

    slots = []
    rows = []
    for number in range(per_replica):
        mine = (chip - (replica * per_replica + number)) % chips
        own_core, other_core = [pick(mine, same)], [pick(mine, other)]
        for step in range(1, replicas):
            target = (replica + step) % replicas
            theirs = (chip - (target * per_replica + number)) % chips
            got = rotate(pick(theirs, same), "dp", step)
            own_core.append(got)
            other_core.append(swap(got, "st"))
        slots += [own_core, other_core]
        rows += [2 * number + core, 2 * number + 1 - core]
    grad_weight = weight_gradient(jnp.stack(rows).astype(jnp.int32), acts, slots)

    whole = backward(pos_above, qkv_above, d_above, 0, early, heads)
    upstream = fill(late_above, whole)
    return (grad_weight[None], upstream.transpose(0, 2, 1, 3)[None, None])


def solution(mesh):
    in_specs = (
        P("section", "dp", None, None, "st", None),
        P("section", "dp", None),
        P("section", None, "st"),
        P("section", "dp", None, "st"),
    )
    out_specs = (P("section", "dp", "st"), P("section", "dp", None, None, "st", None))
    return jax.shard_map(local, mesh=mesh, in_specs=in_specs, out_specs=out_specs, check_vma=False)
```

```python
import functools
import math

import jax
import jax.numpy as jnp
from jax import lax
from jax.experimental import pallas as pl
from jax.experimental.pallas import tpu as pltpu
from jax.sharding import PartitionSpec as P


F32 = jnp.float32
BF16 = jnp.bfloat16
VMEM = pl.BlockSpec(memory_space=pltpu.VMEM)
SMEM = pl.BlockSpec(memory_space=pltpu.SMEM)
ANY = pl.BlockSpec(memory_space=pl.ANY)
HBM = pl.BlockSpec(memory_space=pltpu.HBM)
PARAMS = pltpu.CompilerParams(vmem_limit_bytes=24 * 2**20)


def dot(a, b, dims):
    return lax.dot_general(a, b, ((dims[0], dims[1]), ((), ())), preferred_element_type=F32)


def rotate(value, axis, steps):
    count = lax.axis_size(axis)
    return lax.ppermute(value, axis, [(i, (i + steps) % count) for i in range(count)])


def swap(value, axis):
    count = lax.axis_size(axis)
    return lax.ppermute(value, axis, [(i, i ^ 1) for i in range(count)])


def down(value, axis):
    count = lax.axis_size(axis)
    return lax.ppermute(value, axis, [(i, i - 1) for i in range(1, count)])


def masked_softmax(pos_ref, qkv_ref, heads):
    width = qkv_ref.shape[-1]
    seq = pos_ref.shape[-1]
    scale = 1.0 / math.sqrt(width)
    queries = jnp.broadcast_to(pos_ref[...].astype(F32), (seq, seq))
    visible = queries.T <= queries
    probs = []
    for head in heads:
        scores = dot(qkv_ref[1, head], qkv_ref[0, head], ((1,), (1,))) * scale
        scores = jnp.where(visible, scores, -1e30)
        exponent = jnp.exp(scores - jnp.max(scores, axis=0, keepdims=True))
        probs.append(exponent * (1.0 / jnp.sum(exponent, axis=0, keepdims=True)))
    return probs


def place():
    me = lax.axis_index("st")
    return lax.div(me, 2), lax.rem(me, 2)


def rows_of(weight_ref, depth, chips, step, crossed):
    chip, core = place()
    owner = 2 * lax.rem(chip - step + chips, chips) + (1 - core if crossed else core)
    return weight_ref.at[pl.ds(pl.multiple_of(owner * depth, depth), depth)]


def forward_kernel(chips, pos_ref, qkv_ref, weight_ref, out_ref, *refs):
    heads, _, width = qkv_ref.shape[1:]
    kept, sems = refs[:-1], refs[-1]
    gets = [
        pltpu.make_async_copy(
            rows_of(weight_ref, ref.shape[0], chips, step, False), ref, sems.at[step]
        )
        for step, ref in enumerate(kept, 1)
    ]
    for get in gets:
        get.start()
    for head, probs in enumerate(masked_softmax(pos_ref, qkv_ref, range(heads))):
        attended = dot(probs.astype(BF16), qkv_ref[2, head], ((0,), (0,)))
        out_ref[:, head * width : (head + 1) * width] = attended.astype(BF16)
    for get in gets:
        get.wait()


def forward(chips, depth, pos, qkv, weight):
    _, heads, seq, width = qkv.shape
    kept = [pltpu.VMEM((depth, weight.shape[1]), BF16)] * (chips - 1)
    return pl.pallas_call(
        functools.partial(forward_kernel, chips),
        name="forward",
        in_specs=[VMEM, VMEM, HBM],
        out_specs=[VMEM] * chips,
        out_shape=[jax.ShapeDtypeStruct((seq, heads * width), BF16)] + kept,
        scratch_shapes=[pltpu.SemaphoreType.DMA((chips,))],
        compiler_params=PARAMS,
    )(pos, qkv, weight)


def backward_kernel(first, pos_ref, qkv_ref, grad_ref, out_ref, buffer, sems):
    heads, _, width = buffer.shape[1:]
    scale = 1.0 / math.sqrt(width)
    copies = []
    all_probs = masked_softmax(pos_ref, qkv_ref, range(first, first + heads))
    for number, probs in enumerate(all_probs):
        head = first + number
        query, key, value = qkv_ref[0, head], qkv_ref[1, head], qkv_ref[2, head]
        grad = grad_ref[:, number * width : (number + 1) * width]
        d_value = dot(probs.astype(BF16), grad, ((1,), (0,)))
        d_probs = dot(value, grad, ((1,), (1,)))
        row_dot = jnp.sum(probs * d_probs, axis=0, keepdims=True)
        d_scores = (probs * (d_probs - row_dot)).astype(BF16)
        d_key = dot(d_scores, query, ((1,), (0,))) * scale
        d_query = dot(d_scores, key, ((0,), (0,))) * scale
        buffer[0, number] = d_query.astype(BF16)
        buffer[1, number] = d_key.astype(BF16)
        buffer[2, number] = d_value.astype(BF16)
        copy = pltpu.make_async_copy(
            buffer.at[:, number], out_ref.at[:, number], sems.at[number]
        )
        copy.start()
        copies.append(copy)
    for copy in copies:
        copy.wait()


def backward(pos, qkv, grad, first, total):
    _, _, seq, width = qkv.shape
    heads = grad.shape[1] // width
    return pl.pallas_call(
        functools.partial(backward_kernel, first),
        name="backward",
        in_specs=[VMEM, VMEM, VMEM],
        out_specs=ANY,
        out_shape=jax.ShapeDtypeStruct((3, total, seq, width), BF16),
        scratch_shapes=[
            pltpu.VMEM((3, heads, seq, width), BF16),
            pltpu.SemaphoreType.DMA((heads,)),
        ],
        compiler_params=PARAMS,
    )(pos, qkv, grad)


def fill_kernel(late_ref, whole_ref, out_ref, buffer, in_sems, out_sems):
    late = late_ref.shape[1]
    first = out_ref.shape[1] - late
    gets = [
        pltpu.make_async_copy(late_ref.at[i], buffer.at[i], in_sems.at[i]) for i in range(3)
    ]
    puts = [
        pltpu.make_async_copy(buffer.at[i], out_ref.at[i, pl.ds(first, late)], out_sems.at[i])
        for i in range(3)
    ]
    for get in gets:
        get.start()
    for get, put in zip(gets, puts):
        get.wait()
        put.start()
    for put in puts:
        put.wait()


def fill(late, whole):
    return pl.pallas_call(
        fill_kernel,
        name="fill",
        in_specs=[ANY, ANY],
        out_specs=ANY,
        out_shape=jax.ShapeDtypeStruct(whole.shape, whole.dtype),
        scratch_shapes=[
            pltpu.VMEM(late.shape, late.dtype),
            pltpu.SemaphoreType.DMA((3,)),
            pltpu.SemaphoreType.DMA((3,)),
        ],
        input_output_aliases={1: 0},
        compiler_params=PARAMS,
    )(late, whole)


def open_kernel(chips, weight_ref, own_ref, mate_ref, total_ref, *refs):
    kept, (buffer, sems) = refs[:-2], refs[-2:]
    depth = own_ref.shape[1]
    gets = [
        pltpu.make_async_copy(
            rows_of(weight_ref, depth, chips, 0, crossed), buffer.at[crossed], sems.at[chips + crossed]
        )
        for crossed in range(2)
    ]
    gets += [
        pltpu.make_async_copy(
            rows_of(weight_ref, depth, chips, step, True), ref, sems.at[step]
        )
        for step, ref in enumerate(kept, 1)
    ]
    for get in gets:
        get.start()
    gets[0].wait()
    total_ref[...] = jnp.dot(own_ref[...], buffer[0], preferred_element_type=F32)
    gets[1].wait()
    total_ref[...] += jnp.dot(mate_ref[...], buffer[1], preferred_element_type=F32)
    for get in gets[2:]:
        get.wait()


def open_project(chips, weight, own, mate):
    seq, depth = own.shape
    columns = weight.shape[1]
    kept = [pltpu.VMEM((depth, columns), BF16)] * (chips - 1)
    return pl.pallas_call(
        functools.partial(open_kernel, chips),
        name="open_project",
        in_specs=[HBM, VMEM, VMEM],
        out_specs=[VMEM] * chips,
        out_shape=[jax.ShapeDtypeStruct((seq, columns), F32)] + kept,
        scratch_shapes=[
            pltpu.VMEM((2, depth, columns), BF16),
            pltpu.SemaphoreType.DMA((chips + 2,)),
        ],
        compiler_params=PARAMS,
    )(weight, own, mate)


def project_kernel(splits, weight_ref, grad_ref, carried_ref, *outs):
    total = carried_ref[...] + jnp.dot(
        grad_ref[...], weight_ref[...], preferred_element_type=F32
    )
    at = 0
    for out, size in zip(outs, splits):
        out[...] = total[:, at : at + size].astype(out.dtype)
        at += size


def project(weight, grad, total, splits, dtype):
    seq = grad.shape[0]
    return pl.pallas_call(
        functools.partial(project_kernel, splits),
        name="project",
        in_specs=[VMEM] * 3,
        out_specs=[VMEM] * len(splits),
        out_shape=[jax.ShapeDtypeStruct((seq, size), dtype) for size in splits],
        compiler_params=PARAMS,
    )(weight, grad, total)


def choose_kernel(chips, per_replica, number, step, replicas, *refs):
    chip, _ = place()
    target = lax.rem(lax.axis_index("dp") + step, replicas)
    index = lax.rem(chip - (target * per_replica + number) + chips, chips)
    out_ref = refs[-1]
    for option, ref in enumerate(refs[:-1]):

        @pl.when(index == option)
        def _():
            out_ref[...] = ref[...]


def choose(replicas, number, step, options):
    chips = len(options)
    return pl.pallas_call(
        functools.partial(choose_kernel, chips, chips // replicas, number, step, replicas),
        name="choose",
        in_specs=[VMEM] * chips,
        out_specs=VMEM,
        out_shape=jax.ShapeDtypeStruct(options[0].shape, options[0].dtype),
        compiler_params=PARAMS,
    )(*options)


def weight_kernel(replicas, chips, slots, blocks, *refs):
    acts = refs[:replicas]
    same = refs[replicas : replicas + chips]
    other = refs[replicas + chips : replicas + 2 * chips]
    far = refs[replicas + 2 * chips : -2]
    out_ref, stacked = refs[-2:]
    step = pl.program_id(0)
    seq = acts[0].shape[0]
    size = out_ref.shape[0]
    chip, _ = place()

    @pl.when(step == 0)
    def _():
        for number, act in enumerate(acts):
            stacked[number * seq : (number + 1) * seq] = act[...]

    columns = pl.ds(pl.multiple_of(lax.rem(step, blocks) * size, size), size)
    for slot in range(slots):

        @pl.when(lax.div(step, blocks) == slot)
        def _():
            options = other if slot % 2 else same
            index = lax.rem(
                chip - (lax.axis_index("dp") * (slots // 2) + slot // 2) + chips, chips
            )
            near = options[0][:, columns]
            for number in range(1, chips):
                near = jnp.where(index == number, options[number][:, columns], near)
            ours = far[slot * (replicas - 1) : (slot + 1) * (replicas - 1)]
            left = jnp.concatenate([near] + [ref[:, columns] for ref in ours], axis=0)
            out_ref[...] = dot(left, stacked[...], ((0,), (0,))).astype(BF16)


def weight_gradient(acts, same, other, far):
    replicas, chips, slots = len(acts), len(same), len(far)
    seq, columns = acts[0].shape
    features = same[0].shape[1]
    blocks = max(1, features // 768)
    while features % blocks or (features // blocks) % 128:
        blocks -= 1
    size = features // blocks

    def target(step):
        slot = lax.div(step, blocks)
        core = lax.rem(lax.axis_index("st") + slot, 2)
        return (2 * lax.div(slot, 2) + core) * blocks + lax.rem(step, blocks), 0

    args = [*acts, *same, *other, *[ref for slot in far for ref in slot]]
    return pl.pallas_call(
        functools.partial(weight_kernel, replicas, chips, slots, blocks),
        name="weight_gradient",
        grid=(slots * blocks,),
        in_specs=[VMEM] * len(args),
        out_specs=pl.BlockSpec((size, columns), target),
        scratch_shapes=[pltpu.VMEM((replicas * seq, columns), BF16)],
        out_shape=jax.ShapeDtypeStruct((slots * features, columns), BF16),
        compiler_params=PARAMS,
    )(*args)


def local(saved_qkv, positions, w_out, grad_out):
    qkv = saved_qkv[0, 0].transpose(0, 2, 1, 3)
    pos = positions[0]
    weight = pltpu.with_memory_space_constraint(w_out[0], pltpu.HBM)
    heads, _, width = qkv.shape[1:]
    early = max(1, heads // 2)
    late = heads - early
    shards = lax.axis_size("st")
    replicas = lax.axis_size("dp")
    chips = shards // 2
    per_replica = chips // replicas

    qkv_above = down(qkv[:, :early], "section")
    same = [grad_out[0, 0]]
    for step in range(1, chips):
        same.append(rotate(same[0], "st", 2 * step))
    other = []
    for step in range(chips):
        other.append(swap(same[step], "st"))

    attended, *straight_rows = forward(chips, grad_out.shape[-1], pos, qkv, weight)
    acts = [attended]
    for step in range(1, replicas):
        acts.append(rotate(attended, "dp", step))
    pos_above = down(pos, "section")

    whole = (heads * width,)
    halves = (early * width, late * width)
    total, *crossed_rows = open_project(chips, weight, same[0], other[0])
    for step in range(1, chips):
        last = step == chips - 1
        (total,) = project(straight_rows[step - 1], same[step], total, whole, F32)
        total = project(
            crossed_rows[step - 1],
            other[step],
            total,
            halves if last else whole,
            BF16 if last else F32,
        )
        if not last:
            (total,) = total
    d_early, d_late = total
    d_above = down(d_early, "section")
    grads_late = backward(pos, qkv, d_late, early, late)
    late_above = down(grads_late, "section")

    far = []
    for number in range(per_replica):
        direct, crossed = [], []
        for step in range(1, replicas):
            chosen = choose(replicas, number, step, same)
            direct.append(rotate(chosen, "dp", step))
            crossed.append(swap(direct[-1], "st"))
        far += [direct, crossed]

    begun = backward(pos_above, qkv_above, d_above, 0, heads)
    grad_weight = weight_gradient(acts, same, other, far)
    upstream = fill(late_above, begun)
    return (grad_weight[None], upstream.transpose(0, 2, 1, 3)[None, None])


def solution(mesh):
    in_specs = (
        P("section", "dp", None, None, "st", None),
        P("section", "dp", None),
        P("section", None, "st"),
        P("section", "dp", None, "st"),
    )
    out_specs = (P("section", "dp", "st"), P("section", "dp", None, None, "st", None))

    return jax.shard_map(local, mesh=mesh, in_specs=in_specs, out_specs=out_specs, check_vma=False)
```

```python
import functools
import math

import jax
import jax.numpy as jnp
from jax import lax
from jax.experimental import pallas as pl
from jax.experimental.pallas import tpu as pltpu
from jax.sharding import PartitionSpec as P


F32 = jnp.float32
BF16 = jnp.bfloat16
VMEM = pl.BlockSpec(memory_space=pltpu.VMEM)
SMEM = pl.BlockSpec(memory_space=pltpu.SMEM)
ANY = pl.BlockSpec(memory_space=pl.ANY)
PARAMS = pltpu.CompilerParams(vmem_limit_bytes=24 * 2**20)


def in_hbm(value):
    return pltpu.with_memory_space_constraint(value, pltpu.HBM)


def dot(a, b, dims):
    return lax.dot_general(a, b, ((dims[0], dims[1]), ((), ())), preferred_element_type=F32)


def rotate(value, axis, steps):
    count = lax.axis_size(axis)
    return lax.ppermute(value, axis, [(i, (i + steps) % count) for i in range(count)])


def swap(value, axis):
    count = lax.axis_size(axis)
    return lax.ppermute(value, axis, [(i, i ^ 1) for i in range(count)])


def down(value, axis):
    count = lax.axis_size(axis)
    return lax.ppermute(value, axis, [(i, i - 1) for i in range(1, count)])


def visibility(positions):
    seq = positions.shape[-1]
    queries = jnp.broadcast_to(positions.astype(F32), (seq, seq))
    return queries.T <= queries


def softmax(visible, query, key):
    scores = dot(key, query, ((1,), (1,))) * (1.0 / math.sqrt(query.shape[-1]))
    scores = jnp.where(visible, scores, -1e30)
    exponent = jnp.exp(scores - jnp.max(scores, axis=0, keepdims=True))
    return exponent * (1.0 / jnp.sum(exponent, axis=0, keepdims=True))


def pack_kernel(rows, pos_ref, qkv_ref, out_ref, held, sems):
    gets = [
        pltpu.make_async_copy(
            qkv_ref.at[i, pl.ds(0, rows)], out_ref.at[pl.ds(i * rows, rows)], sems.at[i]
        )
        for i in range(3)
    ]
    pos_get = pltpu.make_async_copy(pos_ref, held, sems.at[3])
    pos_get.start()
    for get in gets:
        get.start()
    pos_get.wait()
    spare = (out_ref.shape[0] - 3 * rows, out_ref.shape[1])
    out_ref[3 * rows :] = jnp.broadcast_to(held[...].astype(F32), spare).astype(BF16)
    for get in gets:
        get.wait()


def pack(pos, qkv, early):
    _, _, seq, width = qkv.shape
    rows = early * seq
    return pl.pallas_call(
        functools.partial(pack_kernel, rows),
        name="pack",
        in_specs=[ANY, ANY],
        out_specs=VMEM,
        out_shape=pltpu.VMEM((3 * rows + 16, width), BF16),
        scratch_shapes=[pltpu.VMEM(pos.shape, pos.dtype), pltpu.SemaphoreType.DMA((4,))],
        compiler_params=PARAMS,
    )(in_hbm(pos), in_hbm(qkv.reshape(3, -1, width)))


def place():
    me = lax.axis_index("st")
    return lax.div(me, 2), lax.rem(me, 2)


def rows_of(weight_ref, depth, chips, step, crossed):
    chip, core = place()
    owner = 2 * lax.rem(chip - step + chips, chips) + (1 - core if crossed else core)
    return weight_ref.at[pl.ds(pl.multiple_of(owner * depth, depth), depth)]


def forward_kernel(chips, groups, pos_ref, qkv_ref, weight_ref, out_ref, *refs):
    kept, (buffer, head_sems, sems) = refs[:-3], refs[-3:]
    heads, _, width = buffer.shape[1:]
    size = heads // groups
    fetches = []
    for group in range(groups):
        part = pl.ds(group * size, size)
        fetches.append(
            pltpu.make_async_copy(qkv_ref.at[:, part], buffer.at[:, part], head_sems.at[group])
        )
    gets = [
        pltpu.make_async_copy(
            rows_of(weight_ref, ref.shape[0], chips, 1 + number // 2, number % 2),
            ref,
            sems.at[number],
        )
        for number, ref in enumerate(kept)
    ]
    for get in fetches + gets:
        get.start()
    visible = visibility(pos_ref[...])
    for head in range(heads):
        if head % size == 0:
            fetches[head // size].wait()
        probs = softmax(visible, buffer[0, head], buffer[1, head])
        attended = dot(probs.astype(BF16), buffer[2, head], ((0,), (0,)))
        out_ref[:, head * width : (head + 1) * width] = attended.astype(BF16)
    for get in gets:
        get.wait()


def forward(chips, depth, pos, qkv, weight):
    _, heads, seq, width = qkv.shape
    count = 2 * (chips - 1)
    groups = max(size for size in (1, 2, 3) if heads % size == 0)
    return pl.pallas_call(
        functools.partial(forward_kernel, chips, groups),
        name="forward",
        in_specs=[VMEM, ANY, ANY],
        out_specs=[VMEM] * (1 + count),
        out_shape=[jax.ShapeDtypeStruct((seq, heads * width), BF16)]
        + [pltpu.VMEM((depth, weight.shape[1]), BF16)] * count,
        scratch_shapes=[
            pltpu.VMEM(qkv.shape, BF16),
            pltpu.SemaphoreType.DMA((groups,)),
            pltpu.SemaphoreType.DMA((count,)),
        ],
        compiler_params=PARAMS,
    )(pos, in_hbm(qkv), weight)


def backward_kernel(first, packed, *refs):
    if packed:
        packed_ref, grad_ref, out_ref, buffer, sems = refs
    else:
        pos_ref, qkv_ref, grad_ref, out_ref, buffer, sems = refs
    heads, seq, width = buffer.shape[1:]
    scale = 1.0 / math.sqrt(width)
    positions = packed_ref[3 * heads * seq :][:1] if packed else pos_ref[...]
    visible = visibility(positions)
    copies = []
    for head in range(heads):
        if packed:
            query, key, value = (
                packed_ref[(i * heads + head) * seq : (i * heads + head + 1) * seq]
                for i in range(3)
            )
        else:
            query, key, value = (qkv_ref[i, first + head] for i in range(3))
        grad = grad_ref[:, head * width : (head + 1) * width]
        probs = softmax(visible, query, key)
        d_value = dot(probs.astype(BF16), grad, ((1,), (0,)))
        d_probs = dot(value, grad, ((1,), (1,)))
        row_dot = jnp.sum(probs * d_probs, axis=0, keepdims=True)
        d_scores = (probs * (d_probs - row_dot)).astype(BF16)
        d_key = dot(d_scores, query, ((1,), (0,))) * scale
        d_query = dot(d_scores, key, ((0,), (0,))) * scale
        buffer[0, head] = d_query.astype(BF16)
        buffer[1, head] = d_key.astype(BF16)
        buffer[2, head] = d_value.astype(BF16)
        copy = pltpu.make_async_copy(buffer.at[:, head], out_ref.at[:, head], sems.at[head])
        copy.start()
        copies.append(copy)
    for copy in copies:
        copy.wait()


def backward(args, grad, first, total, seq):
    width = args[-1].shape[-1]
    heads = grad.shape[1] // width
    return pl.pallas_call(
        functools.partial(backward_kernel, first, len(args) == 1),
        name="backward",
        in_specs=[VMEM] * (len(args) + 1),
        out_specs=ANY,
        out_shape=jax.ShapeDtypeStruct((3, total, seq, width), BF16),
        scratch_shapes=[
            pltpu.VMEM((3, heads, seq, width), BF16),
            pltpu.SemaphoreType.DMA((heads,)),
        ],
        compiler_params=PARAMS,
    )(*args, grad)


def fill_kernel(late_ref, whole_ref, out_ref, sems):
    late = late_ref.shape[1]
    first = out_ref.shape[1] - late
    puts = [
        pltpu.make_async_copy(late_ref.at[i], out_ref.at[i, pl.ds(first, late)], sems.at[i])
        for i in range(3)
    ]
    for put in puts:
        put.start()
    for put in puts:
        put.wait()


def fill(late, whole):
    return pl.pallas_call(
        fill_kernel,
        name="fill",
        in_specs=[VMEM, ANY],
        out_specs=ANY,
        out_shape=jax.ShapeDtypeStruct(whole.shape, whole.dtype),
        scratch_shapes=[pltpu.SemaphoreType.DMA((3,))],
        input_output_aliases={1: 0},
        compiler_params=PARAMS,
    )(late, whole)


def open_kernel(chips, weight_ref, own_ref, mate_ref, total_ref, buffer, sems):
    depth = own_ref.shape[1]
    gets = [
        pltpu.make_async_copy(
            rows_of(weight_ref, depth, chips, 0, crossed), buffer.at[crossed], sems.at[crossed]
        )
        for crossed in range(2)
    ]
    for get in gets:
        get.start()
    gets[0].wait()
    product = jnp.dot(own_ref[...], buffer[0], preferred_element_type=F32)
    gets[1].wait()
    total_ref[...] = product + jnp.dot(mate_ref[...], buffer[1], preferred_element_type=F32)


def open_project(chips, weight, own, mate):
    seq, depth = own.shape
    columns = weight.shape[1]
    return pl.pallas_call(
        functools.partial(open_kernel, chips),
        name="open_project",
        in_specs=[ANY, VMEM, VMEM],
        out_specs=VMEM,
        out_shape=jax.ShapeDtypeStruct((seq, columns), F32),
        scratch_shapes=[
            pltpu.VMEM((2, depth, columns), BF16),
            pltpu.SemaphoreType.DMA((2,)),
        ],
        compiler_params=PARAMS,
    )(weight, own, mate)


def project_kernel(splits, weight_ref, grad_ref, carried_ref, *outs):
    total = carried_ref[...] + jnp.dot(
        grad_ref[...], weight_ref[...], preferred_element_type=F32
    )
    at = 0
    for out, size in zip(outs, splits):
        out[...] = total[:, at : at + size].astype(out.dtype)
        at += size


def project(weight, grad, total, splits, dtype):
    seq = grad.shape[0]
    return pl.pallas_call(
        functools.partial(project_kernel, splits),
        name="project",
        in_specs=[VMEM] * 3,
        out_specs=[VMEM] * len(splits),
        out_shape=[jax.ShapeDtypeStruct((seq, size), dtype) for size in splits],
        compiler_params=PARAMS,
    )(weight, grad, total)


def choose_kernel(chips, per_replica, number, step, replicas, *refs):
    chip, _ = place()
    target = lax.rem(lax.axis_index("dp") + step, replicas)
    index = lax.rem(chip - (target * per_replica + number) + chips, chips)
    out_ref = refs[-1]
    for option, ref in enumerate(refs[:-1]):

        @pl.when(index == option)
        def _():
            out_ref[...] = ref[...]


def choose(replicas, number, step, options):
    chips = len(options)
    return pl.pallas_call(
        functools.partial(choose_kernel, chips, chips // replicas, number, step, replicas),
        name="choose",
        in_specs=[VMEM] * chips,
        out_specs=VMEM,
        out_shape=jax.ShapeDtypeStruct(options[0].shape, options[0].dtype),
        compiler_params=PARAMS,
    )(*options)


def weight_kernel(replicas, chips, slots, blocks, *refs):
    acts = refs[:replicas]
    same = refs[replicas : replicas + chips]
    other = refs[replicas + chips : replicas + 2 * chips]
    far = refs[replicas + 2 * chips : -2]
    out_ref, stacked = refs[-2:]
    step = pl.program_id(0)
    seq = acts[0].shape[0]
    size = out_ref.shape[0]
    chip, _ = place()

    @pl.when(step == 0)
    def _():
        for number, act in enumerate(acts):
            stacked[number * seq : (number + 1) * seq] = act[...]

    columns = pl.ds(pl.multiple_of(lax.rem(step, blocks) * size, size), size)
    for slot in range(slots):

        @pl.when(lax.div(step, blocks) == slot)
        def _():
            options = other if slot % 2 else same
            index = lax.rem(
                chip - (lax.axis_index("dp") * (slots // 2) + slot // 2) + chips, chips
            )
            near = options[0][:, columns]
            for number in range(1, chips):
                near = jnp.where(index == number, options[number][:, columns], near)
            ours = far[slot * (replicas - 1) : (slot + 1) * (replicas - 1)]
            left = jnp.concatenate([near] + [ref[:, columns] for ref in ours], axis=0)
            out_ref[...] = dot(left, stacked[...], ((0,), (0,))).astype(BF16)


def weight_gradient(acts, same, other, far):
    replicas, chips, slots = len(acts), len(same), len(far)
    seq, columns = acts[0].shape
    features = same[0].shape[1]
    blocks = max(1, features // 768)
    while features % blocks or (features // blocks) % 128:
        blocks -= 1
    size = features // blocks

    def target(step):
        slot = lax.div(step, blocks)
        core = lax.rem(lax.axis_index("st") + slot, 2)
        return (2 * lax.div(slot, 2) + core) * blocks + lax.rem(step, blocks), 0

    args = [*acts, *same, *other, *[ref for slot in far for ref in slot]]
    return pl.pallas_call(
        functools.partial(weight_kernel, replicas, chips, slots, blocks),
        name="weight_gradient",
        grid=(slots * blocks,),
        in_specs=[VMEM] * len(args),
        out_specs=pl.BlockSpec((size, columns), target),
        scratch_shapes=[pltpu.VMEM((replicas * seq, columns), BF16)],
        out_shape=jax.ShapeDtypeStruct((slots * features, columns), BF16),
        compiler_params=PARAMS,
    )(*args)


def local(saved_qkv, positions, w_out, grad_out):
    qkv = saved_qkv[0, 0].transpose(0, 2, 1, 3)
    pos = positions[0]
    weight = in_hbm(w_out[0])
    heads, seq, width = qkv.shape[1:]
    early = max(1, heads // 2)
    late = heads - early
    shards = lax.axis_size("st")
    replicas = lax.axis_size("dp")
    chips = shards // 2
    per_replica = chips // replicas

    packed_above = down(pack(pos, qkv, early), "section")
    same = [grad_out[0, 0]]
    for step in range(1, chips):
        same.append(rotate(same[0], "st", 2 * step))
    other = []
    for step in range(chips):
        other.append(swap(same[step], "st"))

    attended, *far_rows = forward(chips, grad_out.shape[-1], pos, qkv, weight)
    acts = [attended]
    for step in range(1, replicas):
        acts.append(rotate(attended, "dp", step))

    whole = (heads * width,)
    halves = (early * width, late * width)
    total = open_project(chips, weight, same[0], other[0])
    for step in range(1, chips):
        last = step == chips - 1
        (total,) = project(far_rows[2 * step - 2], same[step], total, whole, F32)
        total = project(
            far_rows[2 * step - 1],
            other[step],
            total,
            halves if last else whole,
            BF16 if last else F32,
        )
        if not last:
            (total,) = total
    d_early, d_late = total
    d_above = down(d_early, "section")
    grads_late = backward((pos, qkv), d_late, early, late, seq)
    late_above = down(grads_late, "section")

    far = []
    for number in range(per_replica):
        direct, crossed = [], []
        for step in range(1, replicas):
            chosen = choose(replicas, number, step, same)
            direct.append(rotate(chosen, "dp", step))
            crossed.append(swap(direct[-1], "st"))
        far += [direct, crossed]

    begun = backward((packed_above,), d_above, 0, heads, seq)
    grad_weight = weight_gradient(acts, same, other, far)
    upstream = fill(late_above, begun)
    return (grad_weight[None], upstream.transpose(0, 2, 1, 3)[None, None])


def solution(mesh):
    in_specs = (
        P("section", "dp", None, None, "st", None),
        P("section", "dp", None),
        P("section", None, "st"),
        P("section", "dp", None, "st"),
    )
    out_specs = (P("section", "dp", "st"), P("section", "dp", None, None, "st", None))

    return jax.shard_map(local, mesh=mesh, in_specs=in_specs, out_specs=out_specs, check_vma=False)
```

```python
import functools
import math

import jax
import jax.numpy as jnp
from jax import lax
from jax.experimental import pallas as pl
from jax.experimental.pallas import tpu as pltpu
from jax.sharding import PartitionSpec as P


F32 = jnp.float32
BF16 = jnp.bfloat16
VMEM = pl.BlockSpec(memory_space=pltpu.VMEM)
SMEM = pl.BlockSpec(memory_space=pltpu.SMEM)
ANY = pl.BlockSpec(memory_space=pl.ANY)
PARAMS = pltpu.CompilerParams(vmem_limit_bytes=24 * 2**20)


def in_hbm(value):
    return pltpu.with_memory_space_constraint(value, pltpu.HBM)


def dot(a, b, dims):
    return lax.dot_general(a, b, ((dims[0], dims[1]), ((), ())), preferred_element_type=F32)


def rotate(value, axis, steps):
    count = lax.axis_size(axis)
    return lax.ppermute(value, axis, [(i, (i + steps) % count) for i in range(count)])


def swap(value, axis):
    count = lax.axis_size(axis)
    return lax.ppermute(value, axis, [(i, i ^ 1) for i in range(count)])


def down(value, axis):
    count = lax.axis_size(axis)
    return lax.ppermute(value, axis, [(i, i - 1) for i in range(1, count)])


def visibility(positions):
    seq = positions.shape[-1]
    queries = jnp.broadcast_to(positions.astype(F32), (seq, seq))
    return queries.T <= queries


def softmax(visible, query, key):
    scores = dot(key, query, ((1,), (1,))) * (1.0 / math.sqrt(query.shape[-1]))
    scores = jnp.where(visible, scores, -1e30)
    exponent = jnp.exp(scores - jnp.max(scores, axis=0, keepdims=True))
    return exponent * (1.0 / jnp.sum(exponent, axis=0, keepdims=True))


def pack_kernel(rows, pos_ref, qkv_ref, out_ref, held, sems):
    gets = [
        pltpu.make_async_copy(
            qkv_ref.at[i, pl.ds(0, rows)], out_ref.at[pl.ds(i * rows, rows)], sems.at[i]
        )
        for i in range(3)
    ]
    pos_get = pltpu.make_async_copy(pos_ref, held, sems.at[3])
    pos_get.start()
    for get in gets:
        get.start()
    pos_get.wait()
    spare = (out_ref.shape[0] - 3 * rows, out_ref.shape[1])
    out_ref[3 * rows :] = jnp.broadcast_to(held[...].astype(F32), spare).astype(BF16)
    for get in gets:
        get.wait()


def pack(pos, qkv, early):
    _, _, seq, width = qkv.shape
    rows = early * seq
    return pl.pallas_call(
        functools.partial(pack_kernel, rows),
        name="pack",
        in_specs=[ANY, ANY],
        out_specs=VMEM,
        out_shape=pltpu.VMEM((3 * rows + 16, width), BF16),
        scratch_shapes=[pltpu.VMEM(pos.shape, pos.dtype), pltpu.SemaphoreType.DMA((4,))],
        compiler_params=PARAMS,
    )(in_hbm(pos), in_hbm(qkv.reshape(3, -1, width)))


def place():
    me = lax.axis_index("st")
    return lax.div(me, 2), lax.rem(me, 2)


def rows_of(weight_ref, depth, chips, step, crossed):
    chip, core = place()
    owner = 2 * lax.rem(chip - step + chips, chips) + (1 - core if crossed else core)
    return weight_ref.at[pl.ds(pl.multiple_of(owner * depth, depth), depth)]


def forward_kernel(chips, groups, pos_ref, qkv_ref, weight_ref, own_ref, out_ref, total_ref, *refs):
    kept, (held, shard, buffer, rows, head_sems, sems) = refs[:-6], refs[-6:]
    heads, _, width = buffer.shape[1:]
    size = heads // groups
    gets = [pltpu.make_async_copy(pos_ref, held, head_sems.at[groups])]
    for group in range(groups):
        part = pl.ds(group * size, size)
        gets.append(
            pltpu.make_async_copy(qkv_ref.at[:, part], buffer.at[:, part], head_sems.at[group])
        )
    fetches = [
        pltpu.make_async_copy(
            rows_of(weight_ref, rows.shape[0], chips, number // 2, number % 2),
            target,
            sems.at[number],
        )
        for number, target in enumerate((rows, *kept))
    ]
    gets.append(pltpu.make_async_copy(own_ref, shard, head_sems.at[groups + 1]))
    for get in gets + fetches:
        get.start()
    gets[0].wait()
    visible = visibility(held[...])
    for head in range(heads):
        if head % size == 0:
            gets[1 + head // size].wait()
        probs = softmax(visible, buffer[0, head], buffer[1, head])
        attended = dot(probs.astype(BF16), buffer[2, head], ((0,), (0,)))
        out_ref[:, head * width : (head + 1) * width] = attended.astype(BF16)
    gets[-1].wait()
    fetches[0].wait()
    total_ref[...] = jnp.dot(shard[...], rows[...], preferred_element_type=F32)
    for fetch in fetches[1:]:
        fetch.wait()


def forward(chips, pos, qkv, weight, own):
    _, heads, seq, width = qkv.shape
    depth, columns = own.shape[1], weight.shape[1]
    count = 2 * chips - 1
    groups = max(size for size in (1, 2, 3) if heads % size == 0)
    return pl.pallas_call(
        functools.partial(forward_kernel, chips, groups),
        name="forward",
        in_specs=[ANY] * 4,
        out_specs=[VMEM] * (2 + count),
        out_shape=[
            jax.ShapeDtypeStruct((seq, heads * width), BF16),
            jax.ShapeDtypeStruct((seq, columns), F32),
        ]
        + [pltpu.VMEM((depth, columns), BF16)] * count,
        scratch_shapes=[
            pltpu.VMEM(pos.shape, pos.dtype),
            pltpu.VMEM(own.shape, BF16),
            pltpu.VMEM(qkv.shape, BF16),
            pltpu.VMEM((depth, columns), BF16),
            pltpu.SemaphoreType.DMA((groups + 2,)),
            pltpu.SemaphoreType.DMA((count + 1,)),
        ],
        compiler_params=PARAMS,
    )(in_hbm(pos), in_hbm(qkv), weight, in_hbm(own))


def head_gradients(visible, query, key, value, grad):
    scale = 1.0 / math.sqrt(query.shape[-1])
    probs = softmax(visible, query, key)
    d_value = dot(probs.astype(BF16), grad, ((1,), (0,)))
    d_probs = dot(value, grad, ((1,), (1,)))
    row_dot = jnp.sum(probs * d_probs, axis=0, keepdims=True)
    d_scores = (probs * (d_probs - row_dot)).astype(BF16)
    d_key = dot(d_scores, query, ((1,), (0,))) * scale
    d_query = dot(d_scores, key, ((0,), (0,))) * scale
    return d_query.astype(BF16), d_key.astype(BF16), d_value.astype(BF16)


def late_kernel(pos_ref, qkv_ref, grad_ref, out_ref):
    heads, _, width = out_ref.shape[1:]
    first = qkv_ref.shape[1] - heads
    visible = visibility(pos_ref[...])
    for head in range(heads):
        query, key, value = (qkv_ref[i, first + head] for i in range(3))
        grad = grad_ref[:, head * width : (head + 1) * width]
        for i, result in enumerate(head_gradients(visible, query, key, value, grad)):
            out_ref[i, head] = result


def late_backward(pos, qkv, grad):
    _, _, seq, width = qkv.shape
    heads = grad.shape[1] // width
    return pl.pallas_call(
        late_kernel,
        name="late_backward",
        in_specs=[VMEM] * 3,
        out_specs=VMEM,
        out_shape=pltpu.VMEM((3, heads, seq, width), BF16),
        compiler_params=PARAMS,
    )(pos, qkv, grad)


def early_kernel(packed_ref, grad_ref, out_ref, buffer, sems):
    heads, seq, width = buffer.shape[1:]
    visible = visibility(packed_ref[3 * heads * seq :][:1])
    copies = []
    for head in range(heads):
        query, key, value = (
            packed_ref[(i * heads + head) * seq : (i * heads + head + 1) * seq] for i in range(3)
        )
        grad = grad_ref[:, head * width : (head + 1) * width]
        for i, result in enumerate(head_gradients(visible, query, key, value, grad)):
            buffer[i, head] = result
        copy = pltpu.make_async_copy(buffer.at[:, head], out_ref.at[:, head], sems.at[head])
        copy.start()
        copies.append(copy)
    for copy in copies:
        copy.wait()


def early_backward(packed, grad, total):
    seq, width = grad.shape[0], packed.shape[1]
    heads = grad.shape[1] // width
    return pl.pallas_call(
        early_kernel,
        name="early_backward",
        in_specs=[VMEM] * 2,
        out_specs=ANY,
        out_shape=jax.ShapeDtypeStruct((3, total, seq, width), BF16),
        scratch_shapes=[
            pltpu.VMEM((3, heads, seq, width), BF16),
            pltpu.SemaphoreType.DMA((heads,)),
        ],
        compiler_params=PARAMS,
    )(packed, grad)


def fill_kernel(late_ref, whole_ref, out_ref, sems):
    late = late_ref.shape[1]
    first = out_ref.shape[1] - late
    puts = [
        pltpu.make_async_copy(late_ref.at[i], out_ref.at[i, pl.ds(first, late)], sems.at[i])
        for i in range(3)
    ]
    for put in puts:
        put.start()
    for put in puts:
        put.wait()


def fill(late, whole):
    return pl.pallas_call(
        fill_kernel,
        name="fill",
        in_specs=[VMEM, ANY],
        out_specs=ANY,
        out_shape=jax.ShapeDtypeStruct(whole.shape, whole.dtype),
        scratch_shapes=[pltpu.SemaphoreType.DMA((3,))],
        input_output_aliases={1: 0},
        compiler_params=PARAMS,
    )(late, whole)


def project_kernel(splits, weight_ref, grad_ref, carried_ref, *outs):
    total = carried_ref[...] + jnp.dot(
        grad_ref[...], weight_ref[...], preferred_element_type=F32
    )
    at = 0
    for out, size in zip(outs, splits):
        out[...] = total[:, at : at + size].astype(out.dtype)
        at += size


def project(weight, grad, total, splits, dtype):
    seq = grad.shape[0]
    return pl.pallas_call(
        functools.partial(project_kernel, splits),
        name="project",
        in_specs=[VMEM] * 3,
        out_specs=[VMEM] * len(splits),
        out_shape=[jax.ShapeDtypeStruct((seq, size), dtype) for size in splits],
        compiler_params=PARAMS,
    )(weight, grad, total)


def choose_kernel(chips, per_replica, number, step, replicas, *refs):
    chip, _ = place()
    target = lax.rem(lax.axis_index("dp") + step, replicas)
    index = lax.rem(chip - (target * per_replica + number) + chips, chips)
    out_ref = refs[-1]
    for option, ref in enumerate(refs[:-1]):

        @pl.when(index == option)
        def _():
            out_ref[...] = ref[...]


def choose(replicas, number, step, options):
    chips = len(options)
    return pl.pallas_call(
        functools.partial(choose_kernel, chips, chips // replicas, number, step, replicas),
        name="choose",
        in_specs=[VMEM] * chips,
        out_specs=VMEM,
        out_shape=jax.ShapeDtypeStruct(options[0].shape, options[0].dtype),
        compiler_params=PARAMS,
    )(*options)


def weight_kernel(replicas, chips, blocks, *refs):
    acts = refs[:replicas]
    options = refs[replicas : replicas + chips]
    out_ref, stacked = refs[-2:]
    step = pl.program_id(0)
    slots = pl.num_programs(0) // blocks
    far = refs[replicas + chips : replicas + chips + slots * (replicas - 1)]
    seq = acts[0].shape[0]
    size = out_ref.shape[0]

    @pl.when(step == 0)
    def _():
        for number, act in enumerate(acts):
            stacked[number * seq : (number + 1) * seq] = act[...]

    chip, _ = place()
    columns = pl.ds(pl.multiple_of(lax.rem(step, blocks) * size, size), size)
    for slot in range(slots):

        @pl.when(lax.div(step, blocks) == slot)
        def _():
            index = lax.rem(chip - (lax.axis_index("dp") * slots + slot) + chips, chips)
            near = options[0][:, columns]
            for number in range(1, chips):
                near = jnp.where(index == number, options[number][:, columns], near)
            ours = far[slot * (replicas - 1) : (slot + 1) * (replicas - 1)]
            left = jnp.concatenate([near] + [ref[:, columns] for ref in ours], axis=0)
            out_ref[...] = dot(left, stacked[...], ((0,), (0,))).astype(BF16)


def weight_gradient(parity, acts, options, far, begun):
    replicas, chips, slots = len(acts), len(options), len(far)
    seq, columns = acts[0].shape
    features = options[0].shape[1]
    blocks = max(1, features // 768)
    while features % blocks or (features // blocks) % 128:
        blocks -= 1
    size = features // blocks

    def target(step):
        core = lax.rem(lax.axis_index("st") + parity, 2)
        return (2 * lax.div(step, blocks) + core) * blocks + lax.rem(step, blocks), 0

    args = [*acts, *options, *[ref for slot in far for ref in slot]]
    specs = [VMEM] * len(args)
    aliases = {}
    if begun is not None:
        aliases = {len(args): 0}
        args.append(begun)
        specs.append(ANY)
    return pl.pallas_call(
        functools.partial(weight_kernel, replicas, chips, blocks),
        name="weight_gradient",
        grid=(slots * blocks,),
        in_specs=specs,
        out_specs=pl.BlockSpec((size, columns), target),
        scratch_shapes=[pltpu.VMEM((replicas * seq, columns), BF16)],
        out_shape=jax.ShapeDtypeStruct((2 * slots * features, columns), BF16),
        input_output_aliases=aliases,
        compiler_params=PARAMS,
    )(*args)


def local(saved_qkv, positions, w_out, grad_out):
    qkv = saved_qkv[0, 0].transpose(0, 2, 1, 3)
    pos = positions[0]
    weight = in_hbm(w_out[0])
    heads, _, width = qkv.shape[1:]
    early = max(1, heads // 2)
    late = heads - early
    shards = lax.axis_size("st")
    replicas = lax.axis_size("dp")
    chips = shards // 2
    per_replica = chips // replicas

    packed_above = down(pack(pos, qkv, early), "section")
    same = [grad_out[0, 0]]
    for step in range(1, chips):
        same.append(rotate(same[0], "st", 2 * step))
    other = []
    for step in range(chips):
        other.append(swap(same[step], "st"))

    attended, total, *far_rows = forward(chips, pos, qkv, weight, same[0])
    acts = [attended]
    for step in range(1, replicas):
        acts.append(rotate(attended, "dp", step))

    whole = (heads * width,)
    halves = (early * width, late * width)
    (total,) = project(far_rows[0], other[0], total, whole, F32)
    for step in range(1, chips):
        last = step == chips - 1
        (total,) = project(far_rows[2 * step - 1], same[step], total, whole, F32)
        total = project(
            far_rows[2 * step],
            other[step],
            total,
            halves if last else whole,
            BF16 if last else F32,
        )
        if not last:
            (total,) = total
    d_early, d_late = total
    d_above = down(d_early, "section")
    grads_late = late_backward(pos, qkv, d_late)
    late_above = down(grads_late, "section")

    near_far, cross_far = [], []
    for number in range(per_replica):
        direct, crossed = [], []
        for step in range(1, replicas):
            chosen = choose(replicas, number, step, same)
            direct.append(rotate(chosen, "dp", step))
            crossed.append(swap(direct[-1], "st"))
        near_far.append(direct)
        cross_far.append(crossed)

    begun = early_backward(packed_above, d_above, heads)
    grad_weight = weight_gradient(0, acts, same, near_far, None)
    grad_weight = weight_gradient(1, acts, other, cross_far, grad_weight)
    upstream = fill(late_above, begun)
    return (grad_weight[None], upstream.transpose(0, 2, 1, 3)[None, None])


def solution(mesh):
    in_specs = (
        P("section", "dp", None, None, "st", None),
        P("section", "dp", None),
        P("section", None, "st"),
        P("section", "dp", None, "st"),
    )
    out_specs = (P("section", "dp", "st"), P("section", "dp", None, None, "st", None))

    return jax.shard_map(local, mesh=mesh, in_specs=in_specs, out_specs=out_specs, check_vma=False)
```

```python
import functools
import math

import jax
import jax.numpy as jnp
from jax import lax
from jax.experimental import pallas as pl
from jax.experimental.pallas import tpu as pltpu
from jax.sharding import PartitionSpec as P


F32 = jnp.float32
BF16 = jnp.bfloat16
VMEM = pl.BlockSpec(memory_space=pltpu.VMEM)
SMEM = pl.BlockSpec(memory_space=pltpu.SMEM)
ANY = pl.BlockSpec(memory_space=pl.ANY)
PARAMS = pltpu.CompilerParams(vmem_limit_bytes=24 * 2**20)


def in_hbm(value):
    return pltpu.with_memory_space_constraint(value, pltpu.HBM)


def dot(a, b, dims):
    return lax.dot_general(a, b, ((dims[0], dims[1]), ((), ())), preferred_element_type=F32)


def rotate(value, axis, steps):
    count = lax.axis_size(axis)
    return lax.ppermute(value, axis, [(i, (i + steps) % count) for i in range(count)])


def swap(value, axis):
    count = lax.axis_size(axis)
    return lax.ppermute(value, axis, [(i, i ^ 1) for i in range(count)])


def down(value, axis):
    count = lax.axis_size(axis)
    return lax.ppermute(value, axis, [(i, i - 1) for i in range(1, count)])


def visibility(positions):
    seq = positions.shape[-1]
    queries = jnp.broadcast_to(positions.astype(F32), (seq, seq))
    return queries.T <= queries


def softmax(visible, query, key):
    scores = dot(key, query, ((1,), (1,))) * (1.0 / math.sqrt(query.shape[-1]))
    scores = jnp.where(visible, scores, -1e30)
    exponent = jnp.exp(scores - jnp.max(scores, axis=0, keepdims=True))
    return exponent * (1.0 / jnp.sum(exponent, axis=0, keepdims=True))


def pack_kernel(rows, pos_ref, qkv_ref, own_ref, out_ref, *refs):
    parts, (held, sems) = refs[:-2], refs[-2:]
    gets = [pltpu.make_async_copy(pos_ref, held, sems.at[3])]
    gets += [
        pltpu.make_async_copy(
            qkv_ref.at[i, pl.ds(0, rows)], out_ref.at[pl.ds(i * rows, rows)], sems.at[i]
        )
        for i in range(3)
    ]
    for number, part in enumerate(parts):
        size = part.shape[1]
        gets.append(
            pltpu.make_async_copy(
                own_ref.at[:, pl.ds(number * size, size)], part, sems.at[4 + number]
            )
        )
    for get in gets:
        get.start()
    gets[0].wait()
    spare = (out_ref.shape[0] - 3 * rows, out_ref.shape[1])
    out_ref[3 * rows :] = jnp.broadcast_to(held[...].astype(F32), spare).astype(BF16)
    for get in gets[1:]:
        get.wait()


def pack(pos, qkv, own, early, pieces):
    _, _, seq, width = qkv.shape
    rows = early * seq
    part = pltpu.VMEM((seq, own.shape[1] // pieces), BF16)
    return pl.pallas_call(
        functools.partial(pack_kernel, rows),
        name="pack",
        in_specs=[ANY] * 3,
        out_specs=[VMEM] * (1 + pieces),
        out_shape=[pltpu.VMEM((3 * rows + 16, width), BF16)] + [part] * pieces,
        scratch_shapes=[
            pltpu.VMEM(pos.shape, pos.dtype),
            pltpu.SemaphoreType.DMA((4 + pieces,)),
        ],
        compiler_params=PARAMS,
    )(in_hbm(pos), in_hbm(qkv.reshape(3, -1, width)), in_hbm(own))


def place():
    me = lax.axis_index("st")
    return lax.div(me, 2), lax.rem(me, 2)


def rows_of(weight_ref, depth, chips, step, crossed):
    chip, core = place()
    owner = 2 * lax.rem(chip - step + chips, chips) + (1 - core if crossed else core)
    return weight_ref.at[pl.ds(pl.multiple_of(owner * depth, depth), depth)]


def forward_kernel(chips, groups, pos_ref, qkv_ref, weight_ref, own_ref, out_ref, total_ref, *refs):
    kept, (held, shard, buffer, rows, head_sems, sems) = refs[:-6], refs[-6:]
    heads, _, width = buffer.shape[1:]
    size = heads // groups
    gets = [pltpu.make_async_copy(pos_ref, held, head_sems.at[groups])]
    for group in range(groups):
        part = pl.ds(group * size, size)
        gets.append(
            pltpu.make_async_copy(qkv_ref.at[:, part], buffer.at[:, part], head_sems.at[group])
        )
    fetches = [
        pltpu.make_async_copy(
            rows_of(weight_ref, rows.shape[0], chips, number // 2, number % 2),
            target,
            sems.at[number],
        )
        for number, target in enumerate((rows, *kept))
    ]
    gets.append(pltpu.make_async_copy(own_ref, shard, head_sems.at[groups + 1]))
    for get in gets + fetches:
        get.start()
    gets[0].wait()
    visible = visibility(held[...])
    for head in range(heads):
        if head % size == 0:
            gets[1 + head // size].wait()
        probs = softmax(visible, buffer[0, head], buffer[1, head])
        attended = dot(probs.astype(BF16), buffer[2, head], ((0,), (0,)))
        out_ref[:, head * width : (head + 1) * width] = attended.astype(BF16)
    gets[-1].wait()
    fetches[0].wait()
    total_ref[...] = jnp.dot(shard[...], rows[...], preferred_element_type=F32)
    for fetch in fetches[1:]:
        fetch.wait()


def forward(chips, pos, qkv, weight, own):
    _, heads, seq, width = qkv.shape
    depth, columns = own.shape[1], weight.shape[1]
    count = 2 * chips - 1
    groups = max(size for size in (1, 2, 3) if heads % size == 0)
    return pl.pallas_call(
        functools.partial(forward_kernel, chips, groups),
        name="forward",
        in_specs=[ANY] * 4,
        out_specs=[VMEM] * (2 + count),
        out_shape=[
            jax.ShapeDtypeStruct((seq, heads * width), BF16),
            jax.ShapeDtypeStruct((seq, columns), F32),
        ]
        + [pltpu.VMEM((depth, columns), BF16)] * count,
        scratch_shapes=[
            pltpu.VMEM(pos.shape, pos.dtype),
            pltpu.VMEM(own.shape, BF16),
            pltpu.VMEM(qkv.shape, BF16),
            pltpu.VMEM((depth, columns), BF16),
            pltpu.SemaphoreType.DMA((groups + 2,)),
            pltpu.SemaphoreType.DMA((count + 1,)),
        ],
        compiler_params=PARAMS,
    )(in_hbm(pos), in_hbm(qkv), weight, in_hbm(own))


def head_gradients(visible, query, key, value, grad):
    scale = 1.0 / math.sqrt(query.shape[-1])
    probs = softmax(visible, query, key)
    d_value = dot(probs.astype(BF16), grad, ((1,), (0,)))
    d_probs = dot(value, grad, ((1,), (1,)))
    row_dot = jnp.sum(probs * d_probs, axis=0, keepdims=True)
    d_scores = (probs * (d_probs - row_dot)).astype(BF16)
    d_key = dot(d_scores, query, ((1,), (0,))) * scale
    d_query = dot(d_scores, key, ((0,), (0,))) * scale
    return d_query.astype(BF16), d_key.astype(BF16), d_value.astype(BF16)


def late_kernel(pos_ref, qkv_ref, grad_ref, out_ref):
    heads, _, width = out_ref.shape[1:]
    first = qkv_ref.shape[1] - heads
    visible = visibility(pos_ref[...])
    for head in range(heads):
        query, key, value = (qkv_ref[i, first + head] for i in range(3))
        grad = grad_ref[:, head * width : (head + 1) * width]
        for i, result in enumerate(head_gradients(visible, query, key, value, grad)):
            out_ref[i, head] = result


def late_backward(pos, qkv, grad):
    _, _, seq, width = qkv.shape
    heads = grad.shape[1] // width
    return pl.pallas_call(
        late_kernel,
        name="late_backward",
        in_specs=[VMEM] * 3,
        out_specs=VMEM,
        out_shape=pltpu.VMEM((3, heads, seq, width), BF16),
        compiler_params=PARAMS,
    )(pos, qkv, grad)


def early_kernel(packed_ref, grad_ref, out_ref, buffer, sems):
    heads, seq, width = buffer.shape[1:]
    visible = visibility(packed_ref[3 * heads * seq :][:1])
    copies = []
    for head in range(heads):
        query, key, value = (
            packed_ref[(i * heads + head) * seq : (i * heads + head + 1) * seq] for i in range(3)
        )
        grad = grad_ref[:, head * width : (head + 1) * width]
        for i, result in enumerate(head_gradients(visible, query, key, value, grad)):
            buffer[i, head] = result
        copy = pltpu.make_async_copy(buffer.at[:, head], out_ref.at[:, head], sems.at[head])
        copy.start()
        copies.append(copy)
    for copy in copies:
        copy.wait()


def early_backward(packed, grad, total):
    seq, width = grad.shape[0], packed.shape[1]
    heads = grad.shape[1] // width
    return pl.pallas_call(
        early_kernel,
        name="early_backward",
        in_specs=[VMEM] * 2,
        out_specs=ANY,
        out_shape=jax.ShapeDtypeStruct((3, total, seq, width), BF16),
        scratch_shapes=[
            pltpu.VMEM((3, heads, seq, width), BF16),
            pltpu.SemaphoreType.DMA((heads,)),
        ],
        compiler_params=PARAMS,
    )(packed, grad)


def fill_kernel(late_ref, whole_ref, out_ref, sems):
    late = late_ref.shape[1]
    first = out_ref.shape[1] - late
    puts = [
        pltpu.make_async_copy(late_ref.at[i], out_ref.at[i, pl.ds(first, late)], sems.at[i])
        for i in range(3)
    ]
    for put in puts:
        put.start()
    for put in puts:
        put.wait()


def fill(late, whole):
    return pl.pallas_call(
        fill_kernel,
        name="fill",
        in_specs=[VMEM, ANY],
        out_specs=ANY,
        out_shape=jax.ShapeDtypeStruct(whole.shape, whole.dtype),
        scratch_shapes=[pltpu.SemaphoreType.DMA((3,))],
        input_output_aliases={1: 0},
        compiler_params=PARAMS,
    )(late, whole)


def project_kernel(terms, splits, *refs):
    count = 1 + max(number for number, _ in terms)
    weights, grads = refs[:count], refs[count : count + len(terms)]
    refs = refs[count + len(terms) :]
    total = refs[0][...]
    for (number, start), grad in zip(terms, grads):
        rows = weights[number][start : start + grad.shape[1]]
        total = total + jnp.dot(grad[...], rows, preferred_element_type=F32)
    at = 0
    for out, size in zip(refs[1:], splits):
        out[...] = total[:, at : at + size].astype(out.dtype)
        at += size


def project(items, total, splits, dtype):
    weights, terms = [], []
    for weight, start, _ in items:
        found = [number for number, known in enumerate(weights) if known is weight]
        if not found:
            weights.append(weight)
        terms.append((found[0] if found else len(weights) - 1, start))
    grads = [grad for _, _, grad in items]
    seq = grads[0].shape[0]
    return pl.pallas_call(
        functools.partial(project_kernel, tuple(terms), splits),
        name="project",
        in_specs=[VMEM] * (len(weights) + len(grads) + 1),
        out_specs=[VMEM] * len(splits),
        out_shape=[jax.ShapeDtypeStruct((seq, size), dtype) for size in splits],
        compiler_params=PARAMS,
    )(*weights, *grads, total)


def counts(options):
    return tuple(len(pieces) for pieces in options)


def grouped(refs, sizes):
    refs = list(refs)
    return [[refs.pop(0) for _ in range(size)] for size in sizes]


def choose_kernel(sizes, per_replica, number, step, replicas, *refs):
    chips = len(sizes)
    chip, _ = place()
    target = lax.rem(lax.axis_index("dp") + step, replicas)
    index = lax.rem(chip - (target * per_replica + number) + chips, chips)
    out_ref = refs[-1]
    for option, pieces in enumerate(grouped(refs[:-1], sizes)):

        @pl.when(index == option)
        def _():
            at = 0
            for piece in pieces:
                out_ref[:, at : at + piece.shape[1]] = piece[...]
                at += piece.shape[1]


def choose(replicas, number, step, options):
    chips = len(options)
    args = [piece for pieces in options for piece in pieces]
    return pl.pallas_call(
        functools.partial(
            choose_kernel, counts(options), chips // replicas, number, step, replicas
        ),
        name="choose",
        in_specs=[VMEM] * len(args),
        out_specs=VMEM,
        out_shape=jax.ShapeDtypeStruct(options[0][0].shape, options[0][0].dtype),
        compiler_params=PARAMS,
    )(*args)


def weight_kernel(replicas, sizes, slots, blocks, *refs):
    acts = refs[:replicas]
    args = sum(sizes)
    options = grouped(refs[replicas : replicas + args], sizes)
    far = refs[replicas + args : replicas + args + slots * (replicas - 1)]
    out_ref, stacked = refs[-2:]
    step = pl.program_id(0)
    chips = len(sizes)
    seq = acts[0].shape[0]
    size = out_ref.shape[0]

    @pl.when(step == 0)
    def _():
        for number, act in enumerate(acts):
            stacked[number * seq : (number + 1) * seq] = act[...]

    chip, _ = place()
    for slot in range(slots):
        ours = far[slot * (replicas - 1) : (slot + 1) * (replicas - 1)]
        index = lax.rem(chip - (lax.axis_index("dp") * slots + slot) + chips, chips)
        for block in range(blocks):

            @pl.when(step == slot * blocks + block)
            def _():
                near = None
                for number, pieces in enumerate(options):
                    piece, at = divmod(block * size, pieces[0].shape[1])
                    part = pieces[piece][:, at : at + size]
                    near = part if near is None else jnp.where(index == number, part, near)
                columns = slice(block * size, (block + 1) * size)
                left = jnp.concatenate([near] + [ref[:, columns] for ref in ours], axis=0)
                out_ref[...] = dot(left, stacked[...], ((0,), (0,))).astype(BF16)


def weight_gradient(parity, acts, options, far, begun):
    replicas, slots = len(acts), len(far)
    seq, columns = acts[0].shape
    features = far[0][0].shape[1]
    blocks = max(counts(options))
    size = features // blocks

    def target(step):
        core = lax.rem(lax.axis_index("st") + parity, 2)
        return (2 * lax.div(step, blocks) + core) * blocks + lax.rem(step, blocks), 0

    args = [*acts, *[piece for pieces in options for piece in pieces]]
    args += [ref for slot in far for ref in slot]
    specs = [VMEM] * len(args)
    aliases = {}
    if begun is not None:
        aliases = {len(args): 0}
        args.append(begun)
        specs.append(ANY)
    return pl.pallas_call(
        functools.partial(weight_kernel, replicas, counts(options), slots, blocks),
        name="weight_gradient",
        grid=(slots * blocks,),
        in_specs=specs,
        out_specs=pl.BlockSpec((size, columns), target),
        scratch_shapes=[pltpu.VMEM((replicas * seq, columns), BF16)],
        out_shape=jax.ShapeDtypeStruct((2 * slots * features, columns), BF16),
        input_output_aliases=aliases,
        compiler_params=PARAMS,
    )(*args)


def pieces_of(features):
    return 2 if features % 256 == 0 else 1


def local(saved_qkv, positions, w_out, grad_out):
    qkv = saved_qkv[0, 0].transpose(0, 2, 1, 3)
    pos = positions[0]
    weight = in_hbm(w_out[0])
    heads, _, width = qkv.shape[1:]
    early = max(1, heads // 2)
    late = heads - early
    shards = lax.axis_size("st")
    replicas = lax.axis_size("dp")
    chips = shards // 2
    per_replica = chips // replicas

    own = grad_out[0, 0]
    pieces = pieces_of(own.shape[1])
    packed, *parts = pack(pos, qkv, own, early, pieces)
    packed_above = down(packed, "section")
    same = [[own]]
    other = []
    for step in range(1, chips):
        same.append([])
        for piece in range(pieces):
            same[-1].append(rotate(parts[piece], "st", 2 * step))
    other.append([swap(own, "st")])
    for step in range(1, chips):
        other.append([])
        for piece in range(pieces):
            other[-1].append(swap(same[step][piece], "st"))

    attended, total, *far_rows = forward(chips, pos, qkv, weight, own)
    acts = [attended]
    for step in range(1, replicas):
        acts.append(rotate(attended, "dp", step))

    whole = (heads * width,)
    halves = (early * width, late * width)
    depth = own.shape[1] // pieces
    direct, crossed = [], []
    for step in range(1, chips):
        for piece in range(pieces):
            start = piece * depth
            direct.append((far_rows[2 * step - 1], start, same[step][piece]))
            crossed.append((far_rows[2 * step], start, other[step][piece]))
    calls = [[(far_rows[0], 0, other[0][0]), direct[0]]]
    calls += [[direct[i], crossed[i - 1]] for i in range(1, len(direct))]
    for items in calls:
        (total,) = project(items, total, whole, F32)
    total = project([crossed[-1]], total, halves, BF16)
    d_early, d_late = total
    d_above = down(d_early, "section")
    grads_late = late_backward(pos, qkv, d_late)
    late_above = down(grads_late, "section")

    near_far, cross_far = [], []
    for number in range(per_replica):
        straight, swapped = [], []
        for step in range(1, replicas):
            chosen = choose(replicas, number, step, same)
            straight.append(rotate(chosen, "dp", step))
            swapped.append(swap(straight[-1], "st"))
        near_far.append(straight)
        cross_far.append(swapped)

    begun = early_backward(packed_above, d_above, heads)
    grad_weight = weight_gradient(0, acts, same, near_far, None)
    grad_weight = weight_gradient(1, acts, other, cross_far, grad_weight)
    upstream = fill(late_above, begun)
    return (grad_weight[None], upstream.transpose(0, 2, 1, 3)[None, None])


def solution(mesh):
    in_specs = (
        P("section", "dp", None, None, "st", None),
        P("section", "dp", None),
        P("section", None, "st"),
        P("section", "dp", None, "st"),
    )
    out_specs = (P("section", "dp", "st"), P("section", "dp", None, None, "st", None))

    return jax.shard_map(local, mesh=mesh, in_specs=in_specs, out_specs=out_specs, check_vma=False)
```

```python
import functools
import math

import jax
import jax.numpy as jnp
from jax import lax
from jax.experimental import pallas as pl
from jax.experimental.pallas import tpu as pltpu
from jax.sharding import PartitionSpec as P


F32 = jnp.float32
BF16 = jnp.bfloat16
VMEM = pl.BlockSpec(memory_space=pltpu.VMEM)
SMEM = pl.BlockSpec(memory_space=pltpu.SMEM)
ANY = pl.BlockSpec(memory_space=pl.ANY)
PARAMS = pltpu.CompilerParams(vmem_limit_bytes=24 * 2**20)


def in_hbm(value):
    return pltpu.with_memory_space_constraint(value, pltpu.HBM)


def dot(a, b, dims):
    return lax.dot_general(a, b, ((dims[0], dims[1]), ((), ())), preferred_element_type=F32)


def rotate(value, axis, steps):
    count = lax.axis_size(axis)
    return lax.ppermute(value, axis, [(i, (i + steps) % count) for i in range(count)])


def swap(value, axis):
    count = lax.axis_size(axis)
    return lax.ppermute(value, axis, [(i, i ^ 1) for i in range(count)])


def down(value, axis):
    count = lax.axis_size(axis)
    return lax.ppermute(value, axis, [(i, i - 1) for i in range(1, count)])


def visibility(positions):
    seq = positions.shape[-1]
    queries = jnp.broadcast_to(positions.astype(F32), (seq, seq))
    return queries.T <= queries


def softmax(visible, query, key):
    scores = dot(key, query, ((1,), (1,))) * (1.0 / math.sqrt(query.shape[-1]))
    scores = jnp.where(visible, scores, -1e30)
    exponent = jnp.exp(scores - jnp.max(scores, axis=0, keepdims=True))
    return exponent * (1.0 / jnp.sum(exponent, axis=0, keepdims=True))


def pack_kernel(rows, pos_ref, qkv_ref, own_ref, out_ref, *refs):
    parts, (held, sems) = refs[:-2], refs[-2:]
    gets = [pltpu.make_async_copy(pos_ref, held, sems.at[3])]
    gets += [
        pltpu.make_async_copy(
            qkv_ref.at[i, pl.ds(0, rows)], out_ref.at[pl.ds(i * rows, rows)], sems.at[i]
        )
        for i in range(3)
    ]
    for number, part in enumerate(parts):
        size = part.shape[1]
        gets.append(
            pltpu.make_async_copy(
                own_ref.at[:, pl.ds(number * size, size)], part, sems.at[4 + number]
            )
        )
    for get in gets:
        get.start()
    gets[0].wait()
    spare = (out_ref.shape[0] - 3 * rows, out_ref.shape[1])
    out_ref[3 * rows :] = jnp.broadcast_to(held[...].astype(F32), spare).astype(BF16)
    for get in gets[1:]:
        get.wait()


def pack(pos, qkv, own, early, pieces):
    _, _, seq, width = qkv.shape
    rows = early * seq
    part = pltpu.VMEM((seq, own.shape[1] // pieces), BF16)
    return pl.pallas_call(
        functools.partial(pack_kernel, rows),
        name="pack",
        in_specs=[ANY] * 3,
        out_specs=[VMEM] * (1 + pieces),
        out_shape=[pltpu.VMEM((3 * rows + 16, width), BF16)] + [part] * pieces,
        scratch_shapes=[
            pltpu.VMEM(pos.shape, pos.dtype),
            pltpu.SemaphoreType.DMA((4 + pieces,)),
        ],
        compiler_params=PARAMS,
    )(in_hbm(pos), in_hbm(qkv.reshape(3, -1, width)), in_hbm(own))


def place():
    me = lax.axis_index("st")
    return lax.div(me, 2), lax.rem(me, 2)


def rows_of(weight_ref, depth, chips, step, crossed):
    chip, core = place()
    owner = 2 * lax.rem(chip - step + chips, chips) + (1 - core if crossed else core)
    return weight_ref.at[pl.ds(pl.multiple_of(owner * depth, depth), depth)]


def forward_kernel(chips, groups, pos_ref, qkv_ref, weight_ref, own_ref, out_ref, total_ref, *refs):
    kept, (held, shard, buffer, rows, head_sems, sems) = refs[:-6], refs[-6:]
    heads, _, width = buffer.shape[1:]
    size = heads // groups
    gets = [pltpu.make_async_copy(pos_ref, held, head_sems.at[groups])]
    for group in range(groups):
        part = pl.ds(group * size, size)
        gets.append(
            pltpu.make_async_copy(qkv_ref.at[:, part], buffer.at[:, part], head_sems.at[group])
        )
    fetches = [
        pltpu.make_async_copy(
            rows_of(weight_ref, rows.shape[0], chips, max(0, number - 1), number == 1),
            target,
            sems.at[number],
        )
        for number, target in enumerate((rows, *kept))
    ]
    gets.append(pltpu.make_async_copy(own_ref, shard, head_sems.at[groups + 1]))
    for get in gets + fetches:
        get.start()
    gets[0].wait()
    visible = visibility(held[...])
    for head in range(heads):
        if head % size == 0:
            gets[1 + head // size].wait()
        probs = softmax(visible, buffer[0, head], buffer[1, head])
        attended = dot(probs.astype(BF16), buffer[2, head], ((0,), (0,)))
        out_ref[:, head * width : (head + 1) * width] = attended.astype(BF16)
    gets[-1].wait()
    fetches[0].wait()
    total_ref[...] = jnp.dot(shard[...], rows[...], preferred_element_type=F32)
    for fetch in fetches[1:]:
        fetch.wait()


def forward(chips, pos, qkv, weight, own):
    _, heads, seq, width = qkv.shape
    depth, columns = own.shape[1], weight.shape[1]
    count = chips
    groups = max(size for size in (1, 2, 3) if heads % size == 0)
    return pl.pallas_call(
        functools.partial(forward_kernel, chips, groups),
        name="forward",
        in_specs=[ANY] * 4,
        out_specs=[VMEM] * (2 + count),
        out_shape=[
            jax.ShapeDtypeStruct((seq, heads * width), BF16),
            jax.ShapeDtypeStruct((seq, columns), F32),
        ]
        + [pltpu.VMEM((depth, columns), BF16)] * count,
        scratch_shapes=[
            pltpu.VMEM(pos.shape, pos.dtype),
            pltpu.VMEM(own.shape, BF16),
            pltpu.VMEM(qkv.shape, BF16),
            pltpu.VMEM((depth, columns), BF16),
            pltpu.SemaphoreType.DMA((groups + 2,)),
            pltpu.SemaphoreType.DMA((count + 1,)),
        ],
        compiler_params=PARAMS,
    )(in_hbm(pos), in_hbm(qkv), weight, in_hbm(own))


def head_gradients(visible, query, key, value, grad):
    scale = 1.0 / math.sqrt(query.shape[-1])
    probs = softmax(visible, query, key)
    d_value = dot(probs.astype(BF16), grad, ((1,), (0,)))
    d_probs = dot(value, grad, ((1,), (1,)))
    row_dot = jnp.sum(probs * d_probs, axis=0, keepdims=True)
    d_scores = (probs * (d_probs - row_dot)).astype(BF16)
    d_key = dot(d_scores, query, ((1,), (0,))) * scale
    d_query = dot(d_scores, key, ((0,), (0,))) * scale
    return d_query.astype(BF16), d_key.astype(BF16), d_value.astype(BF16)


def late_kernel(pos_ref, qkv_ref, grad_ref, out_ref):
    heads, _, width = out_ref.shape[1:]
    first = qkv_ref.shape[1] - heads
    visible = visibility(pos_ref[...])
    for head in range(heads):
        query, key, value = (qkv_ref[i, first + head] for i in range(3))
        grad = grad_ref[:, head * width : (head + 1) * width]
        for i, result in enumerate(head_gradients(visible, query, key, value, grad)):
            out_ref[i, head] = result


def late_backward(pos, qkv, grad):
    _, _, seq, width = qkv.shape
    heads = grad.shape[1] // width
    return pl.pallas_call(
        late_kernel,
        name="late_backward",
        in_specs=[VMEM] * 3,
        out_specs=VMEM,
        out_shape=pltpu.VMEM((3, heads, seq, width), BF16),
        compiler_params=PARAMS,
    )(pos, qkv, grad)


def early_kernel(packed_ref, grad_ref, out_ref, buffer, sems):
    heads, seq, width = buffer.shape[1:]
    visible = visibility(packed_ref[3 * heads * seq :][:1])
    copies = []
    for head in range(heads):
        query, key, value = (
            packed_ref[(i * heads + head) * seq : (i * heads + head + 1) * seq] for i in range(3)
        )
        grad = grad_ref[:, head * width : (head + 1) * width]
        for i, result in enumerate(head_gradients(visible, query, key, value, grad)):
            buffer[i, head] = result
        copy = pltpu.make_async_copy(buffer.at[:, head], out_ref.at[:, head], sems.at[head])
        copy.start()
        copies.append(copy)
    for copy in copies:
        copy.wait()


def early_backward(packed, grad, total):
    seq, width = grad.shape[0], packed.shape[1]
    heads = grad.shape[1] // width
    return pl.pallas_call(
        early_kernel,
        name="early_backward",
        in_specs=[VMEM] * 2,
        out_specs=ANY,
        out_shape=jax.ShapeDtypeStruct((3, total, seq, width), BF16),
        scratch_shapes=[
            pltpu.VMEM((3, heads, seq, width), BF16),
            pltpu.SemaphoreType.DMA((heads,)),
        ],
        compiler_params=PARAMS,
    )(packed, grad)


def fill_kernel(late_ref, whole_ref, out_ref, sems):
    late = late_ref.shape[1]
    first = out_ref.shape[1] - late
    puts = [
        pltpu.make_async_copy(late_ref.at[i], out_ref.at[i, pl.ds(first, late)], sems.at[i])
        for i in range(3)
    ]
    for put in puts:
        put.start()
    for put in puts:
        put.wait()


def fill(late, whole):
    return pl.pallas_call(
        fill_kernel,
        name="fill",
        in_specs=[VMEM, ANY],
        out_specs=ANY,
        out_shape=jax.ShapeDtypeStruct(whole.shape, whole.dtype),
        scratch_shapes=[pltpu.SemaphoreType.DMA((3,))],
        input_output_aliases={1: 0},
        compiler_params=PARAMS,
    )(late, whole)


def mate_kernel(chips, weight_ref, rows_ref, mate_ref, carried_ref, total_ref, *refs):
    kept, sems = refs[:-1], refs[-1]
    depth = mate_ref.shape[1]
    gets = [
        pltpu.make_async_copy(rows_of(weight_ref, depth, chips, step, True), ref, sems.at[step])
        for step, ref in enumerate(kept, 1)
    ]
    for get in gets:
        get.start()
    total_ref[...] = carried_ref[...] + jnp.dot(
        mate_ref[...], rows_ref[...], preferred_element_type=F32
    )
    for get in gets:
        get.wait()


def project_mate(chips, weight, rows, mate, total):
    depth, columns = rows.shape
    return pl.pallas_call(
        functools.partial(mate_kernel, chips),
        name="project_mate",
        in_specs=[ANY, VMEM, VMEM, VMEM],
        out_specs=[VMEM] * chips,
        out_shape=[jax.ShapeDtypeStruct(total.shape, F32)]
        + [pltpu.VMEM((depth, columns), BF16)] * (chips - 1),
        scratch_shapes=[pltpu.SemaphoreType.DMA((chips,))],
        compiler_params=PARAMS,
    )(weight, rows, mate, total)


def project_kernel(terms, splits, *refs):
    count = 1 + max(number for number, _ in terms)
    weights, grads = refs[:count], refs[count : count + len(terms)]
    refs = refs[count + len(terms) :]
    total = refs[0][...]
    for (number, start), grad in zip(terms, grads):
        rows = weights[number][start : start + grad.shape[1]]
        total = total + jnp.dot(grad[...], rows, preferred_element_type=F32)
    at = 0
    for out, size in zip(refs[1:], splits):
        out[...] = total[:, at : at + size].astype(out.dtype)
        at += size


def project(items, total, splits, dtype):
    weights, terms = [], []
    for weight, start, _ in items:
        found = [number for number, known in enumerate(weights) if known is weight]
        if not found:
            weights.append(weight)
        terms.append((found[0] if found else len(weights) - 1, start))
    grads = [grad for _, _, grad in items]
    seq = grads[0].shape[0]
    return pl.pallas_call(
        functools.partial(project_kernel, tuple(terms), splits),
        name="project",
        in_specs=[VMEM] * (len(weights) + len(grads) + 1),
        out_specs=[VMEM] * len(splits),
        out_shape=[jax.ShapeDtypeStruct((seq, size), dtype) for size in splits],
        compiler_params=PARAMS,
    )(*weights, *grads, total)


def counts(options):
    return tuple(len(pieces) for pieces in options)


def grouped(refs, sizes):
    refs = list(refs)
    return [[refs.pop(0) for _ in range(size)] for size in sizes]


def choose_kernel(per_replica, number, step, replicas, *refs):
    chips = len(refs) - 1
    chip, _ = place()
    target = lax.rem(lax.axis_index("dp") + step, replicas)
    index = lax.rem(chip - (target * per_replica + number) + chips, chips)
    for option, ref in enumerate(refs[:-1]):

        @pl.when(index == option)
        def _():
            refs[-1][...] = ref[...]


def choose(replicas, number, step, options):
    chips = len(options)
    return pl.pallas_call(
        functools.partial(choose_kernel, chips // replicas, number, step, replicas),
        name="choose",
        in_specs=[VMEM] * chips,
        out_specs=VMEM,
        out_shape=jax.ShapeDtypeStruct(options[0].shape, options[0].dtype),
        compiler_params=PARAMS,
    )(*options)


def weight_kernel(replicas, sizes, slots, split, blocks, *refs):
    acts = refs[:replicas]
    args = sum(sizes)
    options = grouped(refs[replicas : replicas + args], sizes)
    count = slots * (replicas - 1)
    far = grouped(refs[replicas + args :], [2 if split else 1] * count)
    out_ref, stacked = refs[-2:]
    step = pl.program_id(0)
    chips = len(sizes)
    seq = acts[0].shape[0]
    size = out_ref.shape[0]

    @pl.when(step == 0)
    def _():
        for number, act in enumerate(acts):
            stacked[number * seq : (number + 1) * seq] = act[...]

    chip, _ = place()
    for slot in range(slots):
        index = lax.rem(chip - (lax.axis_index("dp") * slots + slot) + chips, chips)
        for block in range(blocks):

            def part(pieces):
                piece, at = divmod(block * size, pieces[0].shape[1])
                return pieces[piece][:, at : at + size]

            @pl.when(step == slot * blocks + block)
            def _():
                near = None
                for number, pieces in enumerate(options):
                    own = part(pieces)
                    near = own if near is None else jnp.where(index == number, own, near)
                left = [near]
                for pieces in far[slot * (replicas - 1) : (slot + 1) * (replicas - 1)]:
                    if split:
                        left.append(jnp.where(index == 1, part(pieces), part(pieces[::-1])))
                    else:
                        left.append(part(pieces))
                rows = jnp.concatenate(left, axis=0)
                out_ref[...] = dot(rows, stacked[...], ((0,), (0,))).astype(BF16)


def weight_gradient(parity, acts, options, far, begun):
    replicas, slots = len(acts), len(far)
    split = len(far[0][0]) == 2
    seq, columns = acts[0].shape
    features = sum(piece.shape[1] for piece in far[0][0])
    blocks = max(counts(options))
    size = features // blocks

    def target(step):
        core = lax.rem(lax.axis_index("st") + parity, 2)
        return (2 * lax.div(step, blocks) + core) * blocks + lax.rem(step, blocks), 0

    args = [*acts, *[piece for pieces in options for piece in pieces]]
    args += [piece for slot in far for pieces in slot for piece in pieces]
    specs = [VMEM] * len(args)
    aliases = {}
    if begun is not None:
        aliases = {len(args): 0}
        args.append(begun)
        specs.append(ANY)
    return pl.pallas_call(
        functools.partial(weight_kernel, replicas, counts(options), slots, split, blocks),
        name="weight_gradient",
        grid=(slots * blocks,),
        in_specs=specs,
        out_specs=pl.BlockSpec((size, columns), target),
        scratch_shapes=[pltpu.VMEM((replicas * seq, columns), BF16)],
        out_shape=jax.ShapeDtypeStruct((2 * slots * features, columns), BF16),
        input_output_aliases=aliases,
        compiler_params=PARAMS,
    )(*args)


def pieces_of(features):
    return 2 if features % 256 == 0 else 1


def local(saved_qkv, positions, w_out, grad_out):
    qkv = saved_qkv[0, 0].transpose(0, 2, 1, 3)
    pos = positions[0]
    weight = in_hbm(w_out[0])
    heads, _, width = qkv.shape[1:]
    early = max(1, heads * 7 // 12)
    late = heads - early
    shards = lax.axis_size("st")
    replicas = lax.axis_size("dp")
    chips = shards // 2
    per_replica = chips // replicas

    own = grad_out[0, 0]
    pieces = pieces_of(own.shape[1])
    packed, *parts = pack(pos, qkv, own, early, pieces)
    packed_above = down(packed, "section")
    same = [[own]]
    other = []
    for step in range(1, chips):
        same.append([])
        for piece in range(pieces):
            same[-1].append(rotate(parts[piece], "st", 2 * step))
    other.append([swap(own, "st")])
    for step in range(1, chips):
        other.append([])
        for piece in range(pieces):
            other[-1].append(swap(same[step][piece], "st"))

    attended, total, *far_rows = forward(chips, pos, qkv, weight, own)
    acts = [attended]
    for step in range(1, replicas):
        acts.append(rotate(attended, "dp", step))

    whole = (heads * width,)
    halves = (early * width, late * width)
    depth = own.shape[1] // pieces
    total, *crossed_rows = project_mate(chips, weight, far_rows[0], other[0][0], total)
    direct, crossed = [], []
    for step in range(1, chips):
        for piece in range(pieces):
            start = piece * depth
            direct.append((far_rows[step], start, same[step][piece]))
            crossed.append((crossed_rows[step - 1], start, other[step][piece]))
    (total,) = project(direct + crossed[:-1], total, whole, F32)
    total = project([crossed[-1]], total, halves, BF16)
    d_early, d_late = total
    d_above = down(d_early, "section")
    grads_late = late_backward(pos, qkv, d_late)
    late_above = down(grads_late, "section")

    split = chips == pieces == 2
    near_far, cross_far = [], []
    for number in range(per_replica):
        straight, swapped = [], []
        for step in range(1, replicas):
            options = [parts[1], same[1][0]] if split else [value for (value,) in same]
            chosen = choose(replicas, number, step, options)
            got = [rotate(chosen, "dp", step)]
            mates = [swap(got[0], "st")]
            if split:
                got.append(rotate(got[0], "st", 2))
                mates.append(swap(got[1], "st"))
            straight.append(got)
            swapped.append(mates)
        near_far.append(straight)
        cross_far.append(swapped)

    begun = early_backward(packed_above, d_above, heads)
    grad_weight = weight_gradient(0, acts, same, near_far, None)
    grad_weight = weight_gradient(1, acts, other, cross_far, grad_weight)
    upstream = fill(late_above, begun)
    return (grad_weight[None], upstream.transpose(0, 2, 1, 3)[None, None])


def solution(mesh):
    in_specs = (
        P("section", "dp", None, None, "st", None),
        P("section", "dp", None),
        P("section", None, "st"),
        P("section", "dp", None, "st"),
    )
    out_specs = (P("section", "dp", "st"), P("section", "dp", None, None, "st", None))

    return jax.shard_map(local, mesh=mesh, in_specs=in_specs, out_specs=out_specs, check_vma=False)
```

```python
import functools
import math

import jax
import jax.numpy as jnp
from jax import lax
from jax.experimental import pallas as pl
from jax.experimental.pallas import tpu as pltpu
from jax.sharding import PartitionSpec as P


F32 = jnp.float32
BF16 = jnp.bfloat16
VMEM = pl.BlockSpec(memory_space=pltpu.VMEM)
SMEM = pl.BlockSpec(memory_space=pltpu.SMEM)
ANY = pl.BlockSpec(memory_space=pl.ANY)
PARAMS = pltpu.CompilerParams(vmem_limit_bytes=24 * 2**20)


def in_hbm(value):
    return pltpu.with_memory_space_constraint(value, pltpu.HBM)


def dot(a, b, dims):
    return lax.dot_general(a, b, ((dims[0], dims[1]), ((), ())), preferred_element_type=F32)


def rotate(value, axis, steps):
    count = lax.axis_size(axis)
    return lax.ppermute(value, axis, [(i, (i + steps) % count) for i in range(count)])


def swap(value, axis):
    count = lax.axis_size(axis)
    return lax.ppermute(value, axis, [(i, i ^ 1) for i in range(count)])


def down(value, axis):
    count = lax.axis_size(axis)
    return lax.ppermute(value, axis, [(i, i - 1) for i in range(1, count)])


def visibility(positions):
    seq = positions.shape[-1]
    queries = jnp.broadcast_to(positions.astype(F32), (seq, seq))
    return queries.T <= queries


def softmax(visible, query, key):
    scores = dot(key, query, ((1,), (1,))) * (1.0 / math.sqrt(query.shape[-1]))
    scores = jnp.where(visible, scores, -1e30)
    exponent = jnp.exp(scores - jnp.max(scores, axis=0, keepdims=True))
    return exponent * (1.0 / jnp.sum(exponent, axis=0, keepdims=True))


def pack_kernel(rows, pos_ref, qkv_ref, own_ref, out_ref, *refs):
    parts, (held, sems) = refs[:-2], refs[-2:]
    gets = [pltpu.make_async_copy(pos_ref, held, sems.at[3])]
    gets += [
        pltpu.make_async_copy(
            qkv_ref.at[i, pl.ds(0, rows)], out_ref.at[pl.ds(i * rows, rows)], sems.at[i]
        )
        for i in range(3)
    ]
    for number, part in enumerate(parts):
        size = part.shape[1]
        gets.append(
            pltpu.make_async_copy(
                own_ref.at[:, pl.ds(number * size, size)], part, sems.at[4 + number]
            )
        )
    for get in gets:
        get.start()
    gets[0].wait()
    spare = (out_ref.shape[0] - 3 * rows, out_ref.shape[1])
    out_ref[3 * rows :] = jnp.broadcast_to(held[...].astype(F32), spare).astype(BF16)
    for get in gets[1:]:
        get.wait()


def pack(pos, qkv, own, early, pieces):
    _, _, seq, width = qkv.shape
    rows = early * seq
    part = pltpu.VMEM((seq, own.shape[1] // pieces), BF16)
    return pl.pallas_call(
        functools.partial(pack_kernel, rows),
        name="pack",
        in_specs=[ANY] * 3,
        out_specs=[VMEM] * (1 + pieces),
        out_shape=[pltpu.VMEM((3 * rows + 16, width), BF16)] + [part] * pieces,
        scratch_shapes=[
            pltpu.VMEM(pos.shape, pos.dtype),
            pltpu.SemaphoreType.DMA((4 + pieces,)),
        ],
        compiler_params=PARAMS,
    )(in_hbm(pos), in_hbm(qkv.reshape(3, -1, width)), in_hbm(own))


def place():
    me = lax.axis_index("st")
    return lax.div(me, 2), lax.rem(me, 2)


def rows_of(weight_ref, depth, chips, step, crossed):
    chip, core = place()
    owner = 2 * lax.rem(chip - step + chips, chips) + (1 - core if crossed else core)
    return weight_ref.at[pl.ds(pl.multiple_of(owner * depth, depth), depth)]


def forward_kernel(chips, groups, pos_ref, qkv_ref, weight_ref, own_ref, out_ref, total_ref, *refs):
    kept, (held, shard, buffer, rows, head_sems, sems) = refs[:-6], refs[-6:]
    heads, _, width = buffer.shape[1:]
    size = heads // groups
    gets = [pltpu.make_async_copy(pos_ref, held, head_sems.at[groups])]
    for group in range(groups):
        part = pl.ds(group * size, size)
        gets.append(
            pltpu.make_async_copy(qkv_ref.at[:, part], buffer.at[:, part], head_sems.at[group])
        )
    fetches = [
        pltpu.make_async_copy(
            rows_of(weight_ref, rows.shape[0], chips, number // 2, number % 2),
            target,
            sems.at[number],
        )
        for number, target in enumerate((rows, *kept))
    ]
    gets.append(pltpu.make_async_copy(own_ref, shard, head_sems.at[groups + 1]))
    for get in gets + fetches:
        get.start()
    gets[0].wait()
    visible = visibility(held[...])
    for head in range(heads):
        if head % size == 0:
            gets[1 + head // size].wait()
        probs = softmax(visible, buffer[0, head], buffer[1, head])
        attended = dot(probs.astype(BF16), buffer[2, head], ((0,), (0,)))
        out_ref[:, head * width : (head + 1) * width] = attended.astype(BF16)
    gets[-1].wait()
    fetches[0].wait()
    total_ref[...] = jnp.dot(shard[...], rows[...], preferred_element_type=F32)
    for fetch in fetches[1:]:
        fetch.wait()


def forward(chips, pos, qkv, weight, own):
    _, heads, seq, width = qkv.shape
    depth, columns = own.shape[1], weight.shape[1]
    count = 2 * chips - 1
    groups = max(size for size in (1, 2, 3) if heads % size == 0)
    return pl.pallas_call(
        functools.partial(forward_kernel, chips, groups),
        name="forward",
        in_specs=[ANY] * 4,
        out_specs=[VMEM] * (2 + count),
        out_shape=[
            jax.ShapeDtypeStruct((seq, heads * width), BF16),
            jax.ShapeDtypeStruct((seq, columns), F32),
        ]
        + [pltpu.VMEM((depth, columns), BF16)] * count,
        scratch_shapes=[
            pltpu.VMEM(pos.shape, pos.dtype),
            pltpu.VMEM(own.shape, BF16),
            pltpu.VMEM(qkv.shape, BF16),
            pltpu.VMEM((depth, columns), BF16),
            pltpu.SemaphoreType.DMA((groups + 2,)),
            pltpu.SemaphoreType.DMA((count + 1,)),
        ],
        compiler_params=PARAMS,
    )(in_hbm(pos), in_hbm(qkv), weight, in_hbm(own))


def head_gradients(visible, query, key, value, grad):
    scale = 1.0 / math.sqrt(query.shape[-1])
    probs = softmax(visible, query, key)
    d_value = dot(probs.astype(BF16), grad, ((1,), (0,)))
    d_probs = dot(value, grad, ((1,), (1,)))
    row_dot = jnp.sum(probs * d_probs, axis=0, keepdims=True)
    d_scores = (probs * (d_probs - row_dot)).astype(BF16)
    d_key = dot(d_scores, query, ((1,), (0,))) * scale
    d_query = dot(d_scores, key, ((0,), (0,))) * scale
    return d_query.astype(BF16), d_key.astype(BF16), d_value.astype(BF16)


def late_kernel(pos_ref, qkv_ref, grad_ref, out_ref):
    heads, _, width = out_ref.shape[1:]
    first = qkv_ref.shape[1] - heads
    visible = visibility(pos_ref[...])
    for head in range(heads):
        query, key, value = (qkv_ref[i, first + head] for i in range(3))
        grad = grad_ref[:, head * width : (head + 1) * width]
        for i, result in enumerate(head_gradients(visible, query, key, value, grad)):
            out_ref[i, head] = result


def late_backward(pos, qkv, grad):
    _, _, seq, width = qkv.shape
    heads = grad.shape[1] // width
    return pl.pallas_call(
        late_kernel,
        name="late_backward",
        in_specs=[VMEM] * 3,
        out_specs=VMEM,
        out_shape=pltpu.VMEM((3, heads, seq, width), BF16),
        compiler_params=PARAMS,
    )(pos, qkv, grad)


def early_kernel(packed_ref, grad_ref, out_ref, buffer, sems):
    heads, seq, width = buffer.shape[1:]
    visible = visibility(packed_ref[3 * heads * seq :][:1])
    copies = []
    for head in range(heads):
        query, key, value = (
            packed_ref[(i * heads + head) * seq : (i * heads + head + 1) * seq] for i in range(3)
        )
        grad = grad_ref[:, head * width : (head + 1) * width]
        for i, result in enumerate(head_gradients(visible, query, key, value, grad)):
            buffer[i, head] = result
        copy = pltpu.make_async_copy(buffer.at[:, head], out_ref.at[:, head], sems.at[head])
        copy.start()
        copies.append(copy)
    for copy in copies:
        copy.wait()


def early_backward(packed, grad, total):
    seq, width = grad.shape[0], packed.shape[1]
    heads = grad.shape[1] // width
    return pl.pallas_call(
        early_kernel,
        name="early_backward",
        in_specs=[VMEM] * 2,
        out_specs=ANY,
        out_shape=jax.ShapeDtypeStruct((3, total, seq, width), BF16),
        scratch_shapes=[
            pltpu.VMEM((3, heads, seq, width), BF16),
            pltpu.SemaphoreType.DMA((heads,)),
        ],
        compiler_params=PARAMS,
    )(packed, grad)


def fill_kernel(late_ref, whole_ref, out_ref, sems):
    late = late_ref.shape[1]
    first = out_ref.shape[1] - late
    puts = [
        pltpu.make_async_copy(late_ref.at[i], out_ref.at[i, pl.ds(first, late)], sems.at[i])
        for i in range(3)
    ]
    for put in puts:
        put.start()
    for put in puts:
        put.wait()


def fill(late, whole):
    return pl.pallas_call(
        fill_kernel,
        name="fill",
        in_specs=[VMEM, ANY],
        out_specs=ANY,
        out_shape=jax.ShapeDtypeStruct(whole.shape, whole.dtype),
        scratch_shapes=[pltpu.SemaphoreType.DMA((3,))],
        input_output_aliases={1: 0},
        compiler_params=PARAMS,
    )(late, whole)


def project_kernel(terms, splits, *refs):
    count = 1 + max(number for number, _ in terms)
    weights, grads = refs[:count], refs[count : count + len(terms)]
    refs = refs[count + len(terms) :]
    total = refs[0][...]
    for (number, start), grad in zip(terms, grads):
        rows = weights[number][start : start + grad.shape[1]]
        total = total + jnp.dot(grad[...], rows, preferred_element_type=F32)
    at = 0
    for out, size in zip(refs[1:], splits):
        out[...] = total[:, at : at + size].astype(out.dtype)
        at += size


def project(items, total, splits, dtype):
    weights, terms = [], []
    for weight, start, _ in items:
        found = [number for number, known in enumerate(weights) if known is weight]
        if not found:
            weights.append(weight)
        terms.append((found[0] if found else len(weights) - 1, start))
    grads = [grad for _, _, grad in items]
    seq = grads[0].shape[0]
    return pl.pallas_call(
        functools.partial(project_kernel, tuple(terms), splits),
        name="project",
        in_specs=[VMEM] * (len(weights) + len(grads) + 1),
        out_specs=[VMEM] * len(splits),
        out_shape=[jax.ShapeDtypeStruct((seq, size), dtype) for size in splits],
        compiler_params=PARAMS,
    )(*weights, *grads, total)


def counts(options):
    return tuple(len(pieces) for pieces in options)


def grouped(refs, sizes):
    refs = list(refs)
    return [[refs.pop(0) for _ in range(size)] for size in sizes]


def choose_kernel(per_replica, number, step, replicas, *refs):
    chips = len(refs) - 1
    chip, _ = place()
    target = lax.rem(lax.axis_index("dp") + step, replicas)
    index = lax.rem(chip - (target * per_replica + number) + chips, chips)
    for option, ref in enumerate(refs[:-1]):

        @pl.when(index == option)
        def _():
            refs[-1][...] = ref[...]


def choose(replicas, number, step, options):
    chips = len(options)
    return pl.pallas_call(
        functools.partial(choose_kernel, chips // replicas, number, step, replicas),
        name="choose",
        in_specs=[VMEM] * chips,
        out_specs=VMEM,
        out_shape=jax.ShapeDtypeStruct(options[0].shape, options[0].dtype),
        compiler_params=PARAMS,
    )(*options)


def weight_kernel(replicas, sizes, slots, split, blocks, *refs):
    acts = refs[:replicas]
    args = sum(sizes)
    options = grouped(refs[replicas : replicas + args], sizes)
    count = slots * (replicas - 1)
    far = grouped(refs[replicas + args :], [2 if split else 1] * count)
    out_ref, stacked = refs[-2:]
    step = pl.program_id(0)
    chips = len(sizes)
    seq = acts[0].shape[0]
    size = out_ref.shape[0]

    @pl.when(step == 0)
    def _():
        for number, act in enumerate(acts):
            stacked[number * seq : (number + 1) * seq] = act[...]

    chip, _ = place()
    for slot in range(slots):
        index = lax.rem(chip - (lax.axis_index("dp") * slots + slot) + chips, chips)
        for block in range(blocks):

            def part(pieces):
                piece, at = divmod(block * size, pieces[0].shape[1])
                return pieces[piece][:, at : at + size]

            @pl.when(step == slot * blocks + block)
            def _():
                near = None
                for number, pieces in enumerate(options):
                    own = part(pieces)
                    near = own if near is None else jnp.where(index == number, own, near)
                left = [near]
                for pieces in far[slot * (replicas - 1) : (slot + 1) * (replicas - 1)]:
                    if split:
                        left.append(jnp.where(index == 1, part(pieces), part(pieces[::-1])))
                    else:
                        left.append(part(pieces))
                rows = jnp.concatenate(left, axis=0)
                out_ref[...] = dot(rows, stacked[...], ((0,), (0,))).astype(BF16)


def weight_gradient(parity, acts, options, far, begun):
    replicas, slots = len(acts), len(far)
    split = len(far[0][0]) == 2
    seq, columns = acts[0].shape
    features = sum(piece.shape[1] for piece in far[0][0])
    blocks = max(counts(options))
    size = features // blocks

    def target(step):
        core = lax.rem(lax.axis_index("st") + parity, 2)
        return (2 * lax.div(step, blocks) + core) * blocks + lax.rem(step, blocks), 0

    args = [*acts, *[piece for pieces in options for piece in pieces]]
    args += [piece for slot in far for pieces in slot for piece in pieces]
    specs = [VMEM] * len(args)
    aliases = {}
    if begun is not None:
        aliases = {len(args): 0}
        args.append(begun)
        specs.append(ANY)
    return pl.pallas_call(
        functools.partial(weight_kernel, replicas, counts(options), slots, split, blocks),
        name="weight_gradient",
        grid=(slots * blocks,),
        in_specs=specs,
        out_specs=pl.BlockSpec((size, columns), target),
        scratch_shapes=[pltpu.VMEM((replicas * seq, columns), BF16)],
        out_shape=jax.ShapeDtypeStruct((2 * slots * features, columns), BF16),
        input_output_aliases=aliases,
        compiler_params=PARAMS,
    )(*args)


def pieces_of(features):
    return 2 if features % 256 == 0 else 1


def local(saved_qkv, positions, w_out, grad_out):
    qkv = saved_qkv[0, 0].transpose(0, 2, 1, 3)
    pos = positions[0]
    weight = in_hbm(w_out[0])
    heads, _, width = qkv.shape[1:]
    early = max(1, heads * 7 // 12)
    late = heads - early
    shards = lax.axis_size("st")
    replicas = lax.axis_size("dp")
    chips = shards // 2
    per_replica = chips // replicas

    own = grad_out[0, 0]
    pieces = pieces_of(own.shape[1])
    packed, *parts = pack(pos, qkv, own, early, pieces)
    packed_above = down(packed, "section")
    same = [[own]]
    other = []
    for step in range(1, chips):
        same.append([])
        for piece in range(pieces):
            same[-1].append(rotate(parts[piece], "st", 2 * step))
    other.append([swap(own, "st")])
    for step in range(1, chips):
        other.append([])
        for piece in range(pieces):
            other[-1].append(swap(same[step][piece], "st"))

    attended, total, *far_rows = forward(chips, pos, qkv, weight, own)
    acts = [attended]
    for step in range(1, replicas):
        acts.append(rotate(attended, "dp", step))

    whole = (heads * width,)
    halves = (early * width, late * width)
    depth = own.shape[1] // pieces
    direct, crossed = [], []
    for step in range(1, chips):
        for piece in range(pieces):
            start = piece * depth
            direct.append((far_rows[2 * step - 1], start, same[step][piece]))
            crossed.append((far_rows[2 * step], start, other[step][piece]))
    mate = (far_rows[0], 0, other[0][0])
    (total,) = project([mate] + direct + crossed[:-1], total, whole, F32)
    total = project([crossed[-1]], total, halves, BF16)
    d_early, d_late = total
    d_above = down(d_early, "section")
    grads_late = late_backward(pos, qkv, d_late)
    late_above = down(grads_late, "section")

    split = chips == pieces == 2
    near_far, cross_far = [], []
    for number in range(per_replica):
        straight, swapped = [], []
        for step in range(1, replicas):
            options = [parts[1], same[1][0]] if split else [value for (value,) in same]
            chosen = choose(replicas, number, step, options)
            got = [rotate(chosen, "dp", step)]
            mates = [swap(got[0], "st")]
            if split:
                got.append(rotate(got[0], "st", 2))
                mates.append(swap(got[1], "st"))
            straight.append(got)
            swapped.append(mates)
        near_far.append(straight)
        cross_far.append(swapped)

    begun = early_backward(packed_above, d_above, heads)
    grad_weight = weight_gradient(0, acts, same, near_far, None)
    grad_weight = weight_gradient(1, acts, other, cross_far, grad_weight)
    upstream = fill(late_above, begun)
    return (grad_weight[None], upstream.transpose(0, 2, 1, 3)[None, None])


def solution(mesh):
    in_specs = (
        P("section", "dp", None, None, "st", None),
        P("section", "dp", None),
        P("section", None, "st"),
        P("section", "dp", None, "st"),
    )
    out_specs = (P("section", "dp", "st"), P("section", "dp", None, None, "st", None))

    return jax.shard_map(local, mesh=mesh, in_specs=in_specs, out_specs=out_specs, check_vma=False)
```

```python
import functools
import math

import jax
import jax.numpy as jnp
from jax import lax
from jax.experimental import pallas as pl
from jax.experimental.pallas import tpu as pltpu
from jax.sharding import PartitionSpec as P


F32 = jnp.float32
BF16 = jnp.bfloat16
VMEM = pl.BlockSpec(memory_space=pltpu.VMEM)
SMEM = pl.BlockSpec(memory_space=pltpu.SMEM)
ANY = pl.BlockSpec(memory_space=pl.ANY)
PARAMS = pltpu.CompilerParams(vmem_limit_bytes=24 * 2**20)


def in_hbm(value):
    return pltpu.with_memory_space_constraint(value, pltpu.HBM)


def dot(a, b, dims):
    return lax.dot_general(a, b, ((dims[0], dims[1]), ((), ())), preferred_element_type=F32)


def rotate(value, axis, steps):
    count = lax.axis_size(axis)
    return lax.ppermute(value, axis, [(i, (i + steps) % count) for i in range(count)])


def swap(value, axis):
    count = lax.axis_size(axis)
    return lax.ppermute(value, axis, [(i, i ^ 1) for i in range(count)])


def down(value, axis):
    count = lax.axis_size(axis)
    return lax.ppermute(value, axis, [(i, i - 1) for i in range(1, count)])


def visibility(positions):
    seq = positions.shape[-1]
    queries = jnp.broadcast_to(positions.astype(F32), (seq, seq))
    return queries.T <= queries


def softmax(visible, query, key):
    scores = dot(key, query, ((1,), (1,))) * (1.0 / math.sqrt(query.shape[-1]))
    scores = jnp.where(visible, scores, -1e30)
    exponent = jnp.exp(scores - jnp.max(scores, axis=0, keepdims=True))
    return exponent * (1.0 / jnp.sum(exponent, axis=0, keepdims=True))


def pack_kernel(rows, pos_ref, qkv_ref, own_ref, out_ref, *refs):
    parts, (held, sems) = refs[:-2], refs[-2:]
    gets = [pltpu.make_async_copy(pos_ref, held, sems.at[3])]
    gets += [
        pltpu.make_async_copy(
            qkv_ref.at[i, pl.ds(0, rows)], out_ref.at[pl.ds(i * rows, rows)], sems.at[i]
        )
        for i in range(3)
    ]
    for number, part in enumerate(parts):
        size = part.shape[1]
        gets.append(
            pltpu.make_async_copy(
                own_ref.at[:, pl.ds(number * size, size)], part, sems.at[4 + number]
            )
        )
    for get in gets:
        get.start()
    gets[0].wait()
    spare = (out_ref.shape[0] - 3 * rows, out_ref.shape[1])
    out_ref[3 * rows :] = jnp.broadcast_to(held[...].astype(F32), spare).astype(BF16)
    for get in gets[1:]:
        get.wait()


def pack(pos, qkv, own, early, pieces):
    _, _, seq, width = qkv.shape
    rows = early * seq
    part = pltpu.VMEM((seq, own.shape[1] // pieces), BF16)
    return pl.pallas_call(
        functools.partial(pack_kernel, rows),
        name="pack",
        in_specs=[ANY] * 3,
        out_specs=[VMEM] * (1 + pieces),
        out_shape=[pltpu.VMEM((3 * rows + 16, width), BF16)] + [part] * pieces,
        scratch_shapes=[
            pltpu.VMEM(pos.shape, pos.dtype),
            pltpu.SemaphoreType.DMA((4 + pieces,)),
        ],
        compiler_params=PARAMS,
    )(in_hbm(pos), in_hbm(qkv.reshape(3, -1, width)), in_hbm(own))


def place():
    me = lax.axis_index("st")
    return lax.div(me, 2), lax.rem(me, 2)


def rows_of(weight_ref, depth, chips, step, crossed):
    chip, core = place()
    owner = 2 * lax.rem(chip - step + chips, chips) + (1 - core if crossed else core)
    return weight_ref.at[pl.ds(pl.multiple_of(owner * depth, depth), depth)]


def forward_kernel(chips, groups, pos_ref, qkv_ref, weight_ref, own_ref, out_ref, total_ref, *refs):
    kept, (held, shard, buffer, rows, head_sems, sems) = refs[:-6], refs[-6:]
    heads, _, width = buffer.shape[1:]
    size = heads // groups
    gets = [pltpu.make_async_copy(pos_ref, held, head_sems.at[groups])]
    for group in range(groups):
        part = pl.ds(group * size, size)
        gets.append(
            pltpu.make_async_copy(qkv_ref.at[:, part], buffer.at[:, part], head_sems.at[group])
        )
    fetches = [
        pltpu.make_async_copy(
            rows_of(weight_ref, rows.shape[0], chips, max(0, number - 1), number == 1),
            target,
            sems.at[number],
        )
        for number, target in enumerate((rows, *kept))
    ]
    gets.append(pltpu.make_async_copy(own_ref, shard, head_sems.at[groups + 1]))
    for get in gets + fetches:
        get.start()
    gets[0].wait()
    visible = visibility(held[...])
    for head in range(heads):
        if head % size == 0:
            gets[1 + head // size].wait()
        probs = softmax(visible, buffer[0, head], buffer[1, head])
        attended = dot(probs.astype(BF16), buffer[2, head], ((0,), (0,)))
        out_ref[:, head * width : (head + 1) * width] = attended.astype(BF16)
    gets[-1].wait()
    fetches[0].wait()
    total_ref[...] = jnp.dot(shard[...], rows[...], preferred_element_type=F32)
    for fetch in fetches[1:]:
        fetch.wait()


def forward(chips, pos, qkv, weight, own):
    _, heads, seq, width = qkv.shape
    depth, columns = own.shape[1], weight.shape[1]
    count = chips
    groups = max(size for size in (1, 2, 3) if heads % size == 0)
    return pl.pallas_call(
        functools.partial(forward_kernel, chips, groups),
        name="forward",
        in_specs=[ANY] * 4,
        out_specs=[VMEM] * (2 + count),
        out_shape=[
            jax.ShapeDtypeStruct((seq, heads * width), BF16),
            jax.ShapeDtypeStruct((seq, columns), F32),
        ]
        + [pltpu.VMEM((depth, columns), BF16)] * count,
        scratch_shapes=[
            pltpu.VMEM(pos.shape, pos.dtype),
            pltpu.VMEM(own.shape, BF16),
            pltpu.VMEM(qkv.shape, BF16),
            pltpu.VMEM((depth, columns), BF16),
            pltpu.SemaphoreType.DMA((groups + 2,)),
            pltpu.SemaphoreType.DMA((count + 1,)),
        ],
        compiler_params=PARAMS,
    )(in_hbm(pos), in_hbm(qkv), weight, in_hbm(own))


def head_gradients(visible, query, key, value, grad):
    scale = 1.0 / math.sqrt(query.shape[-1])
    probs = softmax(visible, query, key)
    d_value = dot(probs.astype(BF16), grad, ((1,), (0,)))
    d_probs = dot(value, grad, ((1,), (1,)))
    row_dot = jnp.sum(probs * d_probs, axis=0, keepdims=True)
    d_scores = (probs * (d_probs - row_dot)).astype(BF16)
    d_key = dot(d_scores, query, ((1,), (0,))) * scale
    d_query = dot(d_scores, key, ((0,), (0,))) * scale
    return d_query.astype(BF16), d_key.astype(BF16), d_value.astype(BF16)


def late_kernel(pos_ref, qkv_ref, grad_ref, out_ref):
    heads, _, width = out_ref.shape[1:]
    first = qkv_ref.shape[1] - heads
    visible = visibility(pos_ref[...])
    for head in range(heads):
        query, key, value = (qkv_ref[i, first + head] for i in range(3))
        grad = grad_ref[:, head * width : (head + 1) * width]
        for i, result in enumerate(head_gradients(visible, query, key, value, grad)):
            out_ref[i, head] = result


def late_backward(pos, qkv, grad):
    _, _, seq, width = qkv.shape
    heads = grad.shape[1] // width
    return pl.pallas_call(
        late_kernel,
        name="late_backward",
        in_specs=[VMEM] * 3,
        out_specs=VMEM,
        out_shape=pltpu.VMEM((3, heads, seq, width), BF16),
        compiler_params=PARAMS,
    )(pos, qkv, grad)


def early_kernel(packed_ref, grad_ref, out_ref, buffer, sems):
    heads, seq, width = buffer.shape[1:]
    visible = visibility(packed_ref[3 * heads * seq :][:1])
    copies = []
    for head in range(heads):
        query, key, value = (
            packed_ref[(i * heads + head) * seq : (i * heads + head + 1) * seq] for i in range(3)
        )
        grad = grad_ref[:, head * width : (head + 1) * width]
        for i, result in enumerate(head_gradients(visible, query, key, value, grad)):
            buffer[i, head] = result
        copy = pltpu.make_async_copy(buffer.at[:, head], out_ref.at[:, head], sems.at[head])
        copy.start()
        copies.append(copy)
    for copy in copies:
        copy.wait()


def early_backward(packed, grad, total):
    seq, width = grad.shape[0], packed.shape[1]
    heads = grad.shape[1] // width
    return pl.pallas_call(
        early_kernel,
        name="early_backward",
        in_specs=[VMEM] * 2,
        out_specs=ANY,
        out_shape=jax.ShapeDtypeStruct((3, total, seq, width), BF16),
        scratch_shapes=[
            pltpu.VMEM((3, heads, seq, width), BF16),
            pltpu.SemaphoreType.DMA((heads,)),
        ],
        compiler_params=PARAMS,
    )(packed, grad)


def fill_kernel(late_ref, whole_ref, out_ref, sems):
    late = late_ref.shape[1]
    first = out_ref.shape[1] - late
    puts = [
        pltpu.make_async_copy(late_ref.at[i], out_ref.at[i, pl.ds(first, late)], sems.at[i])
        for i in range(3)
    ]
    for put in puts:
        put.start()
    for put in puts:
        put.wait()


def fill(late, whole):
    return pl.pallas_call(
        fill_kernel,
        name="fill",
        in_specs=[VMEM, ANY],
        out_specs=ANY,
        out_shape=jax.ShapeDtypeStruct(whole.shape, whole.dtype),
        scratch_shapes=[pltpu.SemaphoreType.DMA((3,))],
        input_output_aliases={1: 0},
        compiler_params=PARAMS,
    )(late, whole)


def middle_kernel(chips, pieces, weight_ref, *refs):
    steps = chips - 1
    count = 1 + steps * pieces
    rows, refs = refs[: 1 + steps], refs[1 + steps :]
    direct, crossed = refs[:count], refs[count : 2 * count - 2]
    carried_ref, total_ref = refs[2 * count - 2 : 2 * count]
    kept, sems = refs[2 * count : -1], refs[-1]
    depth = kept[0].shape[0]
    size = depth // pieces
    gets = []
    for step in range(1, chips):
        source = rows_of(weight_ref, depth, chips, step, True)
        for piece in range(pieces):
            part = pl.ds(piece * size, size)
            gets.append(
                pltpu.make_async_copy(
                    source.at[part], kept[step - 1].at[part], sems.at[len(gets)]
                )
            )
    for get in gets:
        get.start()
    total = carried_ref[...]
    total = total + jnp.dot(direct[0][...], rows[0][...], preferred_element_type=F32)
    for number, grad in enumerate(direct[1:]):
        step, piece = divmod(number, pieces)
        part = rows[1 + step][piece * size : (piece + 1) * size]
        total = total + jnp.dot(grad[...], part, preferred_element_type=F32)
    for number, grad in enumerate(crossed):
        step, piece = divmod(number, pieces)
        gets[number].wait()
        part = kept[step][piece * size : (piece + 1) * size]
        total = total + jnp.dot(grad[...], part, preferred_element_type=F32)
    total_ref[...] = total
    for get in gets[len(crossed) :]:
        get.wait()


def project_middle(chips, pieces, weight, rows, direct, crossed, total):
    depth, columns = rows[0].shape
    return pl.pallas_call(
        functools.partial(middle_kernel, chips, pieces),
        name="project_middle",
        in_specs=[ANY] + [VMEM] * (len(rows) + len(direct) + len(crossed) + 1),
        out_specs=[VMEM] * chips,
        out_shape=[jax.ShapeDtypeStruct(total.shape, F32)]
        + [pltpu.VMEM((depth, columns), BF16)] * (chips - 1),
        scratch_shapes=[pltpu.SemaphoreType.DMA(((chips - 1) * pieces,))],
        compiler_params=PARAMS,
    )(weight, *rows, *direct, *crossed, total)


def project_kernel(first, splits, rows_ref, grad_ref, carried_ref, *outs):
    rows = rows_ref[first : first + grad_ref.shape[1]]
    total = carried_ref[...] + jnp.dot(grad_ref[...], rows, preferred_element_type=F32)
    at = 0
    for out, size in zip(outs, splits):
        out[...] = total[:, at : at + size].astype(BF16)
        at += size


def project_last(rows, first, grad, total, splits):
    seq = grad.shape[0]
    return pl.pallas_call(
        functools.partial(project_kernel, first, splits),
        name="project_last",
        in_specs=[VMEM] * 3,
        out_specs=[VMEM] * len(splits),
        out_shape=[jax.ShapeDtypeStruct((seq, size), BF16) for size in splits],
        compiler_params=PARAMS,
    )(rows, grad, total)


def counts(options):
    return tuple(len(pieces) for pieces in options)


def grouped(refs, sizes):
    refs = list(refs)
    return [[refs.pop(0) for _ in range(size)] for size in sizes]


def choose_kernel(per_replica, number, step, replicas, *refs):
    chips = len(refs) - 1
    chip, _ = place()
    target = lax.rem(lax.axis_index("dp") + step, replicas)
    index = lax.rem(chip - (target * per_replica + number) + chips, chips)
    for option, ref in enumerate(refs[:-1]):

        @pl.when(index == option)
        def _():
            refs[-1][...] = ref[...]


def choose(replicas, number, step, options):
    chips = len(options)
    return pl.pallas_call(
        functools.partial(choose_kernel, chips // replicas, number, step, replicas),
        name="choose",
        in_specs=[VMEM] * chips,
        out_specs=VMEM,
        out_shape=jax.ShapeDtypeStruct(options[0].shape, options[0].dtype),
        compiler_params=PARAMS,
    )(*options)


def weight_kernel(replicas, sizes, slots, split, blocks, *refs):
    acts = refs[:replicas]
    args = sum(sizes)
    options = grouped(refs[replicas : replicas + args], sizes)
    count = slots * (replicas - 1)
    far = grouped(refs[replicas + args :], [2 if split else 1] * count)
    out_ref, stacked = refs[-2:]
    step = pl.program_id(0)
    chips = len(sizes)
    seq = acts[0].shape[0]
    size = out_ref.shape[0]

    @pl.when(step == 0)
    def _():
        for number, act in enumerate(acts):
            stacked[number * seq : (number + 1) * seq] = act[...]

    chip, _ = place()
    for slot in range(slots):
        index = lax.rem(chip - (lax.axis_index("dp") * slots + slot) + chips, chips)
        for block in range(blocks):

            def part(pieces):
                piece, at = divmod(block * size, pieces[0].shape[1])
                return pieces[piece][:, at : at + size]

            @pl.when(step == slot * blocks + block)
            def _():
                near = None
                for number, pieces in enumerate(options):
                    own = part(pieces)
                    near = own if near is None else jnp.where(index == number, own, near)
                left = [near]
                for pieces in far[slot * (replicas - 1) : (slot + 1) * (replicas - 1)]:
                    if split:
                        left.append(jnp.where(index == 1, part(pieces), part(pieces[::-1])))
                    else:
                        left.append(part(pieces))
                rows = jnp.concatenate(left, axis=0)
                out_ref[...] = dot(rows, stacked[...], ((0,), (0,))).astype(BF16)


def weight_gradient(parity, acts, options, far, begun):
    replicas, slots = len(acts), len(far)
    split = len(far[0][0]) == 2
    seq, columns = acts[0].shape
    features = sum(piece.shape[1] for piece in far[0][0])
    blocks = max(counts(options))
    size = features // blocks

    def target(step):
        core = lax.rem(lax.axis_index("st") + parity, 2)
        return (2 * lax.div(step, blocks) + core) * blocks + lax.rem(step, blocks), 0

    args = [*acts, *[piece for pieces in options for piece in pieces]]
    args += [piece for slot in far for pieces in slot for piece in pieces]
    specs = [VMEM] * len(args)
    aliases = {}
    if begun is not None:
        aliases = {len(args): 0}
        args.append(begun)
        specs.append(ANY)
    return pl.pallas_call(
        functools.partial(weight_kernel, replicas, counts(options), slots, split, blocks),
        name="weight_gradient",
        grid=(slots * blocks,),
        in_specs=specs,
        out_specs=pl.BlockSpec((size, columns), target),
        scratch_shapes=[pltpu.VMEM((replicas * seq, columns), BF16)],
        out_shape=jax.ShapeDtypeStruct((2 * slots * features, columns), BF16),
        input_output_aliases=aliases,
        compiler_params=PARAMS,
    )(*args)


def pieces_of(features):
    return 2 if features % 256 == 0 else 1


def local(saved_qkv, positions, w_out, grad_out):
    qkv = saved_qkv[0, 0].transpose(0, 2, 1, 3)
    pos = positions[0]
    weight = in_hbm(w_out[0])
    heads, _, width = qkv.shape[1:]
    early = max(1, heads * 7 // 12)
    late = heads - early
    shards = lax.axis_size("st")
    replicas = lax.axis_size("dp")
    chips = shards // 2
    per_replica = chips // replicas

    own = grad_out[0, 0]
    pieces = pieces_of(own.shape[1])
    packed, *parts = pack(pos, qkv, own, early, pieces)
    packed_above = down(packed, "section")
    same = [[own]]
    other = []
    for step in range(1, chips):
        same.append([])
        for piece in range(pieces):
            same[-1].append(rotate(parts[piece], "st", 2 * step))
    other.append([swap(own, "st")])
    for step in range(1, chips):
        other.append([])
        for piece in range(pieces):
            other[-1].append(swap(same[step][piece], "st"))

    attended, total, *far_rows = forward(chips, pos, qkv, weight, own)
    acts = [attended]
    for step in range(1, replicas):
        acts.append(rotate(attended, "dp", step))

    halves = (early * width, late * width)
    depth = own.shape[1] // pieces
    direct = [other[0][0]] + [value for values in same[1:] for value in values]
    crossed = [value for values in other[1:] for value in values]
    total, *crossed_rows = project_middle(
        chips, pieces, weight, far_rows, direct, crossed[:-1], total
    )
    total = project_last(crossed_rows[-1], (pieces - 1) * depth, crossed[-1], total, halves)
    d_early, d_late = total
    d_above = down(d_early, "section")
    grads_late = late_backward(pos, qkv, d_late)
    late_above = down(grads_late, "section")

    split = chips == pieces == 2
    near_far, cross_far = [], []
    for number in range(per_replica):
        straight, swapped = [], []
        for step in range(1, replicas):
            options = [parts[1], same[1][0]] if split else [value for (value,) in same]
            chosen = choose(replicas, number, step, options)
            got = [rotate(chosen, "dp", step)]
            mates = [swap(got[0], "st")]
            if split:
                got.append(rotate(got[0], "st", 2))
                mates.append(swap(got[1], "st"))
            straight.append(got)
            swapped.append(mates)
        near_far.append(straight)
        cross_far.append(swapped)

    begun = early_backward(packed_above, d_above, heads)
    grad_weight = weight_gradient(0, acts, same, near_far, None)
    grad_weight = weight_gradient(1, acts, other, cross_far, grad_weight)
    upstream = fill(late_above, begun)
    return (grad_weight[None], upstream.transpose(0, 2, 1, 3)[None, None])


def solution(mesh):
    in_specs = (
        P("section", "dp", None, None, "st", None),
        P("section", "dp", None),
        P("section", None, "st"),
        P("section", "dp", None, "st"),
    )
    out_specs = (P("section", "dp", "st"), P("section", "dp", None, None, "st", None))

    return jax.shard_map(local, mesh=mesh, in_specs=in_specs, out_specs=out_specs, check_vma=False)
```

```python
import functools
import math

import jax
import jax.numpy as jnp
from jax import lax
from jax.experimental import pallas as pl
from jax.experimental.pallas import tpu as pltpu
from jax.sharding import PartitionSpec as P


F32 = jnp.float32
BF16 = jnp.bfloat16
VMEM = pl.BlockSpec(memory_space=pltpu.VMEM)
SMEM = pl.BlockSpec(memory_space=pltpu.SMEM)
ANY = pl.BlockSpec(memory_space=pl.ANY)
PARAMS = pltpu.CompilerParams(vmem_limit_bytes=24 * 2**20)


def in_hbm(value):
    return pltpu.with_memory_space_constraint(value, pltpu.HBM)


def dot(a, b, dims):
    return lax.dot_general(a, b, ((dims[0], dims[1]), ((), ())), preferred_element_type=F32)


def rotate(value, axis, steps):
    count = lax.axis_size(axis)
    return lax.ppermute(value, axis, [(i, (i + steps) % count) for i in range(count)])


def swap(value, axis):
    count = lax.axis_size(axis)
    return lax.ppermute(value, axis, [(i, i ^ 1) for i in range(count)])


def down(value, axis):
    count = lax.axis_size(axis)
    return lax.ppermute(value, axis, [(i, i - 1) for i in range(1, count)])


def visibility(positions):
    seq = positions.shape[-1]
    queries = jnp.broadcast_to(positions.astype(F32), (seq, seq))
    return queries.T <= queries


def softmax(visible, query, key):
    scores = dot(key, query, ((1,), (1,))) * (1.0 / math.sqrt(query.shape[-1]))
    scores = jnp.where(visible, scores, -1e30)
    exponent = jnp.exp(scores - jnp.max(scores, axis=0, keepdims=True))
    return exponent * (1.0 / jnp.sum(exponent, axis=0, keepdims=True))


def pack_kernel(rows, pos_ref, qkv_ref, own_ref, out_ref, *refs):
    parts, (held, sems) = refs[:-2], refs[-2:]
    gets = [pltpu.make_async_copy(pos_ref, held, sems.at[3])]
    gets += [
        pltpu.make_async_copy(
            qkv_ref.at[i, pl.ds(0, rows)], out_ref.at[pl.ds(i * rows, rows)], sems.at[i]
        )
        for i in range(3)
    ]
    for number, part in enumerate(parts):
        size = part.shape[1]
        gets.append(
            pltpu.make_async_copy(
                own_ref.at[:, pl.ds(number * size, size)], part, sems.at[4 + number]
            )
        )
    for get in gets:
        get.start()
    gets[0].wait()
    spare = (out_ref.shape[0] - 3 * rows, out_ref.shape[1])
    out_ref[3 * rows :] = jnp.broadcast_to(held[...].astype(F32), spare).astype(BF16)
    for get in gets[1:]:
        get.wait()


def pack(pos, qkv, own, early, pieces):
    _, _, seq, width = qkv.shape
    rows = early * seq
    part = pltpu.VMEM((seq, own.shape[1] // pieces), BF16)
    return pl.pallas_call(
        functools.partial(pack_kernel, rows),
        name="pack",
        in_specs=[ANY] * 3,
        out_specs=[VMEM] * (1 + pieces),
        out_shape=[pltpu.VMEM((3 * rows + 16, width), BF16)] + [part] * pieces,
        scratch_shapes=[
            pltpu.VMEM(pos.shape, pos.dtype),
            pltpu.SemaphoreType.DMA((4 + pieces,)),
        ],
        compiler_params=PARAMS,
    )(in_hbm(pos), in_hbm(qkv.reshape(3, -1, width)), in_hbm(own))


def place():
    me = lax.axis_index("st")
    return lax.div(me, 2), lax.rem(me, 2)


def rows_of(weight_ref, depth, chips, step, crossed):
    chip, core = place()
    owner = 2 * lax.rem(chip - step + chips, chips) + (1 - core if crossed else core)
    return weight_ref.at[pl.ds(pl.multiple_of(owner * depth, depth), depth)]


def forward_kernel(chips, groups, pos_ref, qkv_ref, weight_ref, own_ref, out_ref, total_ref, *refs):
    kept, (held, shard, buffer, rows, head_sems, sems) = refs[:-6], refs[-6:]
    heads, _, width = buffer.shape[1:]
    size = heads // groups
    gets = [pltpu.make_async_copy(pos_ref, held, head_sems.at[groups])]
    for group in range(groups):
        part = pl.ds(group * size, size)
        gets.append(
            pltpu.make_async_copy(qkv_ref.at[:, part], buffer.at[:, part], head_sems.at[group])
        )
    fetches = [
        pltpu.make_async_copy(
            rows_of(weight_ref, rows.shape[0], chips, number // 2, number % 2),
            target,
            sems.at[number],
        )
        for number, target in enumerate((rows, *kept))
    ]
    gets.append(pltpu.make_async_copy(own_ref, shard, head_sems.at[groups + 1]))
    for get in gets + fetches:
        get.start()
    gets[0].wait()
    visible = visibility(held[...])
    for head in range(heads):
        if head % size == 0:
            gets[1 + head // size].wait()
        probs = softmax(visible, buffer[0, head], buffer[1, head])
        attended = dot(probs.astype(BF16), buffer[2, head], ((0,), (0,)))
        out_ref[:, head * width : (head + 1) * width] = attended.astype(BF16)
    gets[-1].wait()
    fetches[0].wait()
    total_ref[...] = jnp.dot(shard[...], rows[...], preferred_element_type=F32)
    for fetch in fetches[1:]:
        fetch.wait()


def forward(chips, pos, qkv, weight, own):
    _, heads, seq, width = qkv.shape
    depth, columns = own.shape[1], weight.shape[1]
    count = 2 * chips - 1
    groups = max(size for size in (1, 2, 3) if heads % size == 0)
    return pl.pallas_call(
        functools.partial(forward_kernel, chips, groups),
        name="forward",
        in_specs=[ANY] * 4,
        out_specs=[VMEM] * (2 + count),
        out_shape=[
            jax.ShapeDtypeStruct((seq, heads * width), BF16),
            jax.ShapeDtypeStruct((seq, columns), F32),
        ]
        + [pltpu.VMEM((depth, columns), BF16)] * count,
        scratch_shapes=[
            pltpu.VMEM(pos.shape, pos.dtype),
            pltpu.VMEM(own.shape, BF16),
            pltpu.VMEM(qkv.shape, BF16),
            pltpu.VMEM((depth, columns), BF16),
            pltpu.SemaphoreType.DMA((groups + 2,)),
            pltpu.SemaphoreType.DMA((count + 1,)),
        ],
        compiler_params=PARAMS,
    )(in_hbm(pos), in_hbm(qkv), weight, in_hbm(own))


def head_gradients(visible, query, key, value, grad):
    scale = 1.0 / math.sqrt(query.shape[-1])
    probs = softmax(visible, query, key)
    d_value = dot(probs.astype(BF16), grad, ((1,), (0,)))
    d_probs = dot(value, grad, ((1,), (1,)))
    row_dot = jnp.sum(probs * d_probs, axis=0, keepdims=True)
    d_scores = (probs * (d_probs - row_dot)).astype(BF16)
    d_key = dot(d_scores, query, ((1,), (0,))) * scale
    d_query = dot(d_scores, key, ((0,), (0,))) * scale
    return d_query.astype(BF16), d_key.astype(BF16), d_value.astype(BF16)


def late_kernel(pos_ref, qkv_ref, grad_ref, out_ref):
    heads, _, width = out_ref.shape[1:]
    first = qkv_ref.shape[1] - heads
    visible = visibility(pos_ref[...])
    for head in range(heads):
        query, key, value = (qkv_ref[i, first + head] for i in range(3))
        grad = grad_ref[:, head * width : (head + 1) * width]
        for i, result in enumerate(head_gradients(visible, query, key, value, grad)):
            out_ref[i, head] = result


def late_backward(pos, qkv, grad):
    _, _, seq, width = qkv.shape
    heads = grad.shape[1] // width
    return pl.pallas_call(
        late_kernel,
        name="late_backward",
        in_specs=[VMEM] * 3,
        out_specs=VMEM,
        out_shape=pltpu.VMEM((3, heads, seq, width), BF16),
        compiler_params=PARAMS,
    )(pos, qkv, grad)


def early_kernel(packed_ref, grad_ref, out_ref, buffer, sems):
    heads, seq, width = buffer.shape[1:]
    visible = visibility(packed_ref[3 * heads * seq :][:1])
    copies = []
    for head in range(heads):
        query, key, value = (
            packed_ref[(i * heads + head) * seq : (i * heads + head + 1) * seq] for i in range(3)
        )
        grad = grad_ref[:, head * width : (head + 1) * width]
        for i, result in enumerate(head_gradients(visible, query, key, value, grad)):
            buffer[i, head] = result
        copy = pltpu.make_async_copy(buffer.at[:, head], out_ref.at[:, head], sems.at[head])
        copy.start()
        copies.append(copy)
    for copy in copies:
        copy.wait()


def early_backward(packed, grad, total):
    seq, width = grad.shape[0], packed.shape[1]
    heads = grad.shape[1] // width
    return pl.pallas_call(
        early_kernel,
        name="early_backward",
        in_specs=[VMEM] * 2,
        out_specs=ANY,
        out_shape=jax.ShapeDtypeStruct((3, total, seq, width), BF16),
        scratch_shapes=[
            pltpu.VMEM((3, heads, seq, width), BF16),
            pltpu.SemaphoreType.DMA((heads,)),
        ],
        compiler_params=PARAMS,
    )(packed, grad)


def fill_kernel(late_ref, whole_ref, out_ref, sems):
    late = late_ref.shape[1]
    first = out_ref.shape[1] - late
    puts = [
        pltpu.make_async_copy(late_ref.at[i], out_ref.at[i, pl.ds(first, late)], sems.at[i])
        for i in range(3)
    ]
    for put in puts:
        put.start()
    for put in puts:
        put.wait()


def fill(late, whole):
    return pl.pallas_call(
        fill_kernel,
        name="fill",
        in_specs=[VMEM, ANY],
        out_specs=ANY,
        out_shape=jax.ShapeDtypeStruct(whole.shape, whole.dtype),
        scratch_shapes=[pltpu.SemaphoreType.DMA((3,))],
        input_output_aliases={1: 0},
        compiler_params=PARAMS,
    )(late, whole)


def project_kernel(terms, splits, *refs):
    count = 1 + max(number for number, _ in terms)
    weights, grads = refs[:count], refs[count : count + len(terms)]
    refs = refs[count + len(terms) :]
    total = refs[0][...]
    for (number, start), grad in zip(terms, grads):
        rows = weights[number][start : start + grad.shape[1]]
        total = total + jnp.dot(grad[...], rows, preferred_element_type=F32)
    at = 0
    for out, size in zip(refs[1:], splits):
        out[...] = total[:, at : at + size].astype(out.dtype)
        at += size


def project(items, total, splits, dtype):
    weights, terms = [], []
    for weight, start, _ in items:
        found = [number for number, known in enumerate(weights) if known is weight]
        if not found:
            weights.append(weight)
        terms.append((found[0] if found else len(weights) - 1, start))
    grads = [grad for _, _, grad in items]
    seq = grads[0].shape[0]
    return pl.pallas_call(
        functools.partial(project_kernel, tuple(terms), splits),
        name="project",
        in_specs=[VMEM] * (len(weights) + len(grads) + 1),
        out_specs=[VMEM] * len(splits),
        out_shape=[jax.ShapeDtypeStruct((seq, size), dtype) for size in splits],
        compiler_params=PARAMS,
    )(*weights, *grads, total)


def counts(options):
    return tuple(len(pieces) for pieces in options)


def grouped(refs, sizes):
    refs = list(refs)
    return [[refs.pop(0) for _ in range(size)] for size in sizes]


def choose_kernel(per_replica, number, step, replicas, *refs):
    chips = len(refs) - 1
    chip, _ = place()
    target = lax.rem(lax.axis_index("dp") + step, replicas)
    index = lax.rem(chip - (target * per_replica + number) + chips, chips)
    for option, ref in enumerate(refs[:-1]):

        @pl.when(index == option)
        def _():
            refs[-1][...] = ref[...]


def choose(replicas, number, step, options):
    chips = len(options)
    return pl.pallas_call(
        functools.partial(choose_kernel, chips // replicas, number, step, replicas),
        name="choose",
        in_specs=[VMEM] * chips,
        out_specs=VMEM,
        out_shape=jax.ShapeDtypeStruct(options[0].shape, options[0].dtype),
        compiler_params=PARAMS,
    )(*options)


def weight_kernel(replicas, sizes, far_sizes, slots, blocks, *refs):
    refs = list(refs)
    acts = [refs.pop(0) for _ in range(replicas)]
    options = grouped(refs, sizes)
    far = grouped(refs[sum(sizes) :], far_sizes)
    out_ref, stacked = refs[-2:]
    step = pl.program_id(0)
    chips = len(sizes) // 2
    seq = acts[0].shape[0]
    size = out_ref.shape[0]

    @pl.when(step == 0)
    def _():
        for number, act in enumerate(acts):
            stacked[number * seq : (number + 1) * seq] = act[...]

    chip, _ = place()
    for turn in range(2 * slots):
        parity, slot = divmod(turn, slots)
        index = lax.rem(chip - (lax.axis_index("dp") * slots + slot) + chips, chips)
        for block in range(blocks):

            def part(pieces):
                piece, at = divmod(block * size, pieces[0].shape[1])
                return pieces[piece][:, at : at + size]

            @pl.when(step == turn * blocks + block)
            def _():
                near = None
                for number, pieces in enumerate(options[parity * chips : (parity + 1) * chips]):
                    own = part(pieces)
                    near = own if near is None else jnp.where(index == number, own, near)
                left = [near]
                for pieces in far[turn * (replicas - 1) : (turn + 1) * (replicas - 1)]:
                    if len(pieces) == 2:
                        left.append(jnp.where(index == 1, part(pieces), part(pieces[::-1])))
                    else:
                        left.append(part(pieces))
                rows = jnp.concatenate(left, axis=0)
                out_ref[...] = dot(rows, stacked[...], ((0,), (0,))).astype(BF16)


def weight_gradient(acts, options, far):
    replicas, slots = len(acts), len(far) // 2
    far = [pieces for slot in far for pieces in slot]
    seq, columns = acts[0].shape
    features = sum(piece.shape[1] for piece in far[0])
    blocks = max(counts(options))
    size = features // blocks

    def target(step):
        turn = lax.div(step, blocks)
        core = lax.rem(lax.axis_index("st") + lax.div(turn, slots), 2)
        return (2 * lax.rem(turn, slots) + core) * blocks + lax.rem(step, blocks), 0

    args = [*acts, *[piece for pieces in options for piece in pieces]]
    args += [piece for pieces in far for piece in pieces]
    return pl.pallas_call(
        functools.partial(weight_kernel, replicas, counts(options), counts(far), slots, blocks),
        name="weight_gradient",
        grid=(2 * slots * blocks,),
        in_specs=[VMEM] * len(args),
        out_specs=pl.BlockSpec((size, columns), target),
        scratch_shapes=[pltpu.VMEM((replicas * seq, columns), BF16)],
        out_shape=jax.ShapeDtypeStruct((2 * slots * features, columns), BF16),
        compiler_params=PARAMS,
    )(*args)


def pieces_of(features):
    return 2 if features % 256 == 0 else 1


def local(saved_qkv, positions, w_out, grad_out):
    qkv = saved_qkv[0, 0].transpose(0, 2, 1, 3)
    pos = positions[0]
    weight = in_hbm(w_out[0])
    heads, _, width = qkv.shape[1:]
    early = max(1, heads * 8 // 12)
    late = heads - early
    shards = lax.axis_size("st")
    replicas = lax.axis_size("dp")
    chips = shards // 2
    per_replica = chips // replicas

    own = grad_out[0, 0]
    pieces = pieces_of(own.shape[1])
    packed, *parts = pack(pos, qkv, own, early, pieces)
    packed_above = down(packed, "section")
    same = [[own]]
    other = []
    for step in range(1, chips):
        same.append([])
        for piece in range(pieces):
            same[-1].append(rotate(parts[piece], "st", 2 * step))
    other.append([swap(own, "st")])
    for step in range(1, chips):
        other.append([])
        for piece in range(pieces):
            other[-1].append(swap(same[step][piece], "st"))

    attended, total, *far_rows = forward(chips, pos, qkv, weight, own)
    acts = [attended]
    for step in range(1, replicas):
        acts.append(rotate(attended, "dp", step))

    whole = (heads * width,)
    halves = (early * width, late * width)
    depth = own.shape[1] // pieces
    direct, crossed = [], []
    for step in range(1, chips):
        for piece in range(pieces):
            start = piece * depth
            direct.append((far_rows[2 * step - 1], start, same[step][piece]))
            crossed.append((far_rows[2 * step], start, other[step][piece]))
    mate = (far_rows[0], 0, other[0][0])
    (total,) = project([mate] + direct + crossed[:-1], total, whole, F32)
    total = project([crossed[-1]], total, halves, BF16)
    d_early, d_late = total
    d_above = down(d_early, "section")
    grads_late = late_backward(pos, qkv, d_late)
    late_above = down(grads_late, "section")

    split = chips == pieces == 2
    near_far, cross_far = [], []
    for number in range(per_replica):
        straight, swapped = [], []
        for step in range(1, replicas):
            options = [parts[1], same[1][0]] if split else [value for (value,) in same]
            chosen = choose(replicas, number, step, options)
            got = [rotate(chosen, "dp", step)]
            mates = [swap(got[0], "st")]
            if split:
                got.append(rotate(got[0], "st", 2))
                mates.append(swap(got[1], "st"))
            straight.append(got)
            swapped.append(mates)
        near_far.append(straight)
        cross_far.append(swapped)

    begun = early_backward(packed_above, d_above, heads)
    grad_weight = weight_gradient(acts, same + other, near_far + cross_far)
    upstream = fill(late_above, begun)
    return (grad_weight[None], upstream.transpose(0, 2, 1, 3)[None, None])


def solution(mesh):
    in_specs = (
        P("section", "dp", None, None, "st", None),
        P("section", "dp", None),
        P("section", None, "st"),
        P("section", "dp", None, "st"),
    )
    out_specs = (P("section", "dp", "st"), P("section", "dp", None, None, "st", None))

    return jax.shard_map(local, mesh=mesh, in_specs=in_specs, out_specs=out_specs, check_vma=False)
```

```python
import functools
import math

import jax
import jax.numpy as jnp
from jax import lax
from jax.experimental import pallas as pl
from jax.experimental.pallas import tpu as pltpu
from jax.sharding import PartitionSpec as P


F32 = jnp.float32
BF16 = jnp.bfloat16
VMEM = pl.BlockSpec(memory_space=pltpu.VMEM)
SMEM = pl.BlockSpec(memory_space=pltpu.SMEM)
ANY = pl.BlockSpec(memory_space=pl.ANY)
PARAMS = pltpu.CompilerParams(vmem_limit_bytes=24 * 2**20)


def in_hbm(value):
    return pltpu.with_memory_space_constraint(value, pltpu.HBM)


def dot(a, b, dims):
    return lax.dot_general(a, b, ((dims[0], dims[1]), ((), ())), preferred_element_type=F32)


def rotate(value, axis, steps):
    count = lax.axis_size(axis)
    return lax.ppermute(value, axis, [(i, (i + steps) % count) for i in range(count)])


def swap(value, axis):
    count = lax.axis_size(axis)
    return lax.ppermute(value, axis, [(i, i ^ 1) for i in range(count)])


def down(value, axis):
    count = lax.axis_size(axis)
    return lax.ppermute(value, axis, [(i, i - 1) for i in range(1, count)])


def visibility(positions):
    seq = positions.shape[-1]
    queries = jnp.broadcast_to(positions.astype(F32), (seq, seq))
    return queries.T <= queries


def softmax(visible, query, key):
    scores = dot(key, query, ((1,), (1,))) * (1.0 / math.sqrt(query.shape[-1]))
    scores = jnp.where(visible, scores, -1e30)
    exponent = jnp.exp(scores - jnp.max(scores, axis=0, keepdims=True))
    return exponent * (1.0 / jnp.sum(exponent, axis=0, keepdims=True))


def pack_kernel(rows, pos_ref, qkv_ref, own_ref, out_ref, *refs):
    parts, (held, sems) = refs[:-2], refs[-2:]
    gets = [pltpu.make_async_copy(pos_ref, held, sems.at[3])]
    gets += [
        pltpu.make_async_copy(
            qkv_ref.at[i, pl.ds(0, rows)], out_ref.at[pl.ds(i * rows, rows)], sems.at[i]
        )
        for i in range(3)
    ]
    for number, part in enumerate(parts):
        size = part.shape[1]
        gets.append(
            pltpu.make_async_copy(
                own_ref.at[:, pl.ds(number * size, size)], part, sems.at[4 + number]
            )
        )
    for get in gets:
        get.start()
    gets[0].wait()
    spare = (out_ref.shape[0] - 3 * rows, out_ref.shape[1])
    out_ref[3 * rows :] = jnp.broadcast_to(held[...].astype(F32), spare).astype(BF16)
    for get in gets[1:]:
        get.wait()


def pack(pos, qkv, own, early, pieces):
    _, _, seq, width = qkv.shape
    rows = early * seq
    part = pltpu.VMEM((seq, own.shape[1] // pieces), BF16)
    return pl.pallas_call(
        functools.partial(pack_kernel, rows),
        name="pack",
        in_specs=[ANY] * 3,
        out_specs=[VMEM] * (1 + pieces),
        out_shape=[pltpu.VMEM((3 * rows + 16, width), BF16)] + [part] * pieces,
        scratch_shapes=[
            pltpu.VMEM(pos.shape, pos.dtype),
            pltpu.SemaphoreType.DMA((4 + pieces,)),
        ],
        compiler_params=PARAMS,
    )(in_hbm(pos), in_hbm(qkv.reshape(3, -1, width)), in_hbm(own))


def place():
    me = lax.axis_index("st")
    return lax.div(me, 2), lax.rem(me, 2)


def rows_of(weight_ref, depth, chips, step, crossed):
    chip, core = place()
    owner = 2 * lax.rem(chip - step + chips, chips) + (1 - core if crossed else core)
    return weight_ref.at[pl.ds(pl.multiple_of(owner * depth, depth), depth)]


def forward_kernel(chips, groups, pos_ref, qkv_ref, weight_ref, own_ref, out_ref, total_ref, *refs):
    kept, (held, shard, buffer, rows, head_sems, sems) = refs[:-6], refs[-6:]
    heads, _, width = buffer.shape[1:]
    size = heads // groups
    gets = [pltpu.make_async_copy(pos_ref, held, head_sems.at[groups])]
    for group in range(groups):
        part = pl.ds(group * size, size)
        gets.append(
            pltpu.make_async_copy(qkv_ref.at[:, part], buffer.at[:, part], head_sems.at[group])
        )
    fetches = [
        pltpu.make_async_copy(
            rows_of(weight_ref, rows.shape[0], chips, number // 2, number % 2),
            target,
            sems.at[number],
        )
        for number, target in enumerate((rows, *kept))
    ]
    gets.append(pltpu.make_async_copy(own_ref, shard, head_sems.at[groups + 1]))
    for get in gets + fetches:
        get.start()
    gets[0].wait()
    visible = visibility(held[...])
    for head in range(heads):
        if head % size == 0:
            gets[1 + head // size].wait()
        probs = softmax(visible, buffer[0, head], buffer[1, head])
        attended = dot(probs.astype(BF16), buffer[2, head], ((0,), (0,)))
        out_ref[:, head * width : (head + 1) * width] = attended.astype(BF16)
    gets[-1].wait()
    fetches[0].wait()
    total_ref[...] = jnp.dot(shard[...], rows[...], preferred_element_type=F32)
    for fetch in fetches[1:]:
        fetch.wait()


def forward(chips, pos, qkv, weight, own):
    _, heads, seq, width = qkv.shape
    depth, columns = own.shape[1], weight.shape[1]
    count = 2 * chips - 1
    groups = max(size for size in (1, 2, 3) if heads % size == 0)
    return pl.pallas_call(
        functools.partial(forward_kernel, chips, groups),
        name="forward",
        in_specs=[ANY] * 4,
        out_specs=[VMEM] * (2 + count),
        out_shape=[
            jax.ShapeDtypeStruct((seq, heads * width), BF16),
            jax.ShapeDtypeStruct((seq, columns), F32),
        ]
        + [pltpu.VMEM((depth, columns), BF16)] * count,
        scratch_shapes=[
            pltpu.VMEM(pos.shape, pos.dtype),
            pltpu.VMEM(own.shape, BF16),
            pltpu.VMEM(qkv.shape, BF16),
            pltpu.VMEM((depth, columns), BF16),
            pltpu.SemaphoreType.DMA((groups + 2,)),
            pltpu.SemaphoreType.DMA((count + 1,)),
        ],
        compiler_params=PARAMS,
    )(in_hbm(pos), in_hbm(qkv), weight, in_hbm(own))


def head_gradients(visible, query, key, value, grad):
    scale = 1.0 / math.sqrt(query.shape[-1])
    probs = softmax(visible, query, key)
    d_value = dot(probs.astype(BF16), grad, ((1,), (0,)))
    d_probs = dot(value, grad, ((1,), (1,)))
    row_dot = jnp.sum(probs * d_probs, axis=0, keepdims=True)
    d_scores = (probs * (d_probs - row_dot)).astype(BF16)
    d_key = dot(d_scores, query, ((1,), (0,))) * scale
    d_query = dot(d_scores, key, ((0,), (0,))) * scale
    return d_query.astype(BF16), d_key.astype(BF16), d_value.astype(BF16)


def late_kernel(pos_ref, qkv_ref, grad_ref, out_ref):
    heads, _, width = out_ref.shape[1:]
    first = qkv_ref.shape[1] - heads
    visible = visibility(pos_ref[...])
    for head in range(heads):
        query, key, value = (qkv_ref[i, first + head] for i in range(3))
        grad = grad_ref[:, head * width : (head + 1) * width]
        for i, result in enumerate(head_gradients(visible, query, key, value, grad)):
            out_ref[i, head] = result


def late_backward(pos, qkv, grad):
    _, _, seq, width = qkv.shape
    heads = grad.shape[1] // width
    return pl.pallas_call(
        late_kernel,
        name="late_backward",
        in_specs=[VMEM] * 3,
        out_specs=VMEM,
        out_shape=pltpu.VMEM((3, heads, seq, width), BF16),
        compiler_params=PARAMS,
    )(pos, qkv, grad)


def fill_kernel(late_ref, whole_ref, out_ref, sems):
    late = late_ref.shape[1]
    first = out_ref.shape[1] - late
    puts = [
        pltpu.make_async_copy(late_ref.at[i], out_ref.at[i, pl.ds(first, late)], sems.at[i])
        for i in range(3)
    ]
    for put in puts:
        put.start()
    for put in puts:
        put.wait()


def fill(late, whole):
    return pl.pallas_call(
        fill_kernel,
        name="fill",
        in_specs=[VMEM, ANY],
        out_specs=ANY,
        out_shape=jax.ShapeDtypeStruct(whole.shape, whole.dtype),
        scratch_shapes=[pltpu.SemaphoreType.DMA((3,))],
        input_output_aliases={1: 0},
        compiler_params=PARAMS,
    )(late, whole)


def project_kernel(terms, splits, *refs):
    count = 1 + max(number for number, _ in terms)
    weights, grads = refs[:count], refs[count : count + len(terms)]
    refs = refs[count + len(terms) :]
    total = refs[0][...]
    for (number, start), grad in zip(terms, grads):
        rows = weights[number][start : start + grad.shape[1]]
        total = total + jnp.dot(grad[...], rows, preferred_element_type=F32)
    at = 0
    for out, size in zip(refs[1:], splits):
        out[...] = total[:, at : at + size].astype(out.dtype)
        at += size


def project(items, total, splits, dtype):
    weights, terms = [], []
    for weight, start, _ in items:
        found = [number for number, known in enumerate(weights) if known is weight]
        if not found:
            weights.append(weight)
        terms.append((found[0] if found else len(weights) - 1, start))
    grads = [grad for _, _, grad in items]
    seq = grads[0].shape[0]
    return pl.pallas_call(
        functools.partial(project_kernel, tuple(terms), splits),
        name="project",
        in_specs=[VMEM] * (len(weights) + len(grads) + 1),
        out_specs=[VMEM] * len(splits),
        out_shape=[jax.ShapeDtypeStruct((seq, size), dtype) for size in splits],
        compiler_params=PARAMS,
    )(*weights, *grads, total)


def counts(options):
    return tuple(len(pieces) for pieces in options)


def grouped(refs, sizes):
    refs = list(refs)
    return [[refs.pop(0) for _ in range(size)] for size in sizes]


def choose_kernel(per_replica, number, step, replicas, *refs):
    chips = len(refs) - 1
    chip, _ = place()
    target = lax.rem(lax.axis_index("dp") + step, replicas)
    index = lax.rem(chip - (target * per_replica + number) + chips, chips)
    for option, ref in enumerate(refs[:-1]):

        @pl.when(index == option)
        def _():
            refs[-1][...] = ref[...]


def choose(replicas, number, step, options):
    chips = len(options)
    return pl.pallas_call(
        functools.partial(choose_kernel, chips // replicas, number, step, replicas),
        name="choose",
        in_specs=[VMEM] * chips,
        out_specs=VMEM,
        out_shape=jax.ShapeDtypeStruct(options[0].shape, options[0].dtype),
        compiler_params=PARAMS,
    )(*options)


def finish_kernel(replicas, sizes, far_sizes, slots, blocks, packed_ref, grad_ref, *refs):
    refs = list(refs)
    acts = [refs.pop(0) for _ in range(replicas)]
    options = grouped(refs, sizes)
    far = grouped(refs[sum(sizes) :], far_sizes)
    out_ref, weight_ref, held, stacked, ready, head_sems, sems = refs[-7:]
    heads, seq, width = held.shape[1:]
    copies = []
    visible = visibility(packed_ref[3 * heads * seq :][:1])
    for head in range(heads):
        query, key, value = (
            packed_ref[(i * heads + head) * seq : (i * heads + head + 1) * seq] for i in range(3)
        )
        grad = grad_ref[:, head * width : (head + 1) * width]
        for i, result in enumerate(head_gradients(visible, query, key, value, grad)):
            held[i, head] = result
        copies.append(
            pltpu.make_async_copy(held.at[:, head], out_ref.at[:, head], head_sems.at[head])
        )
        copies[-1].start()

    for number, act in enumerate(acts):
        stacked[number * seq : (number + 1) * seq] = act[...]
    chip, core = place()
    chips = len(sizes) // 2
    size = ready.shape[1]
    spans = [(turn, block * size, size) for turn in range(2 * slots) for block in range(blocks)]
    if size % 256 == 0:
        turn, first, _ = spans.pop()
        spans += [(turn, first, size // 2), (turn, first + size // 2, size // 2)]
    puts = []
    for number, (turn, first, count) in enumerate(spans):
        parity, slot = divmod(turn, slots)
        index = lax.rem(chip - (lax.axis_index("dp") * slots + slot) + chips, chips)

        def part(pieces):
            piece, at = divmod(first, pieces[0].shape[1])
            return pieces[piece][:, at : at + count]

        near = None
        for option, pieces in enumerate(options[parity * chips : (parity + 1) * chips]):
            own = part(pieces)
            near = own if near is None else jnp.where(index == option, own, near)
        left = [near]
        for pieces in far[turn * (replicas - 1) : (turn + 1) * (replicas - 1)]:
            if len(pieces) == 2:
                left.append(jnp.where(index == 1, part(pieces), part(pieces[::-1])))
            else:
                left.append(part(pieces))
        block = dot(jnp.concatenate(left, axis=0), stacked[...], ((0,), (0,))).astype(BF16)
        if number >= 2:
            puts[number - 2].wait()
        place_in = ready.at[number % 2, pl.ds(0, count)]
        place_in[...] = block
        row = (2 * slot + lax.rem(core + parity, 2)) * (size * blocks) + first
        target = weight_ref.at[pl.ds(pl.multiple_of(row, 128), count)]
        puts.append(pltpu.make_async_copy(place_in, target, sems.at[number % 2]))
        puts[-1].start()
    for copy in copies + puts[-2:]:
        copy.wait()


def finish(packed, grad, total, acts, options, far):
    seq, width = grad.shape[0], packed.shape[1]
    heads = grad.shape[1] // width
    replicas, slots = len(acts), len(far) // 2
    far = [pieces for slot in far for pieces in slot]
    columns = acts[0].shape[1]
    features = sum(piece.shape[1] for piece in far[0])
    blocks = max(counts(options))
    size = features // blocks
    args = [*acts, *[piece for pieces in options for piece in pieces]]
    args += [piece for pieces in far for piece in pieces]
    return pl.pallas_call(
        functools.partial(finish_kernel, replicas, counts(options), counts(far), slots, blocks),
        name="finish",
        in_specs=[VMEM] * (2 + len(args)),
        out_specs=[ANY, ANY],
        out_shape=[
            jax.ShapeDtypeStruct((3, total, seq, width), BF16),
            jax.ShapeDtypeStruct((2 * slots * features, columns), BF16),
        ],
        scratch_shapes=[
            pltpu.VMEM((3, heads, seq, width), BF16),
            pltpu.VMEM((replicas * seq, columns), BF16),
            pltpu.VMEM((2, size, columns), BF16),
            pltpu.SemaphoreType.DMA((heads,)),
            pltpu.SemaphoreType.DMA((2,)),
        ],
        compiler_params=PARAMS,
    )(packed, grad, *args)


def pieces_of(features):
    return 2 if features % 256 == 0 else 1


def local(saved_qkv, positions, w_out, grad_out):
    qkv = saved_qkv[0, 0].transpose(0, 2, 1, 3)
    pos = positions[0]
    weight = in_hbm(w_out[0])
    heads, _, width = qkv.shape[1:]
    early = max(1, heads * 8 // 12)
    late = heads - early
    shards = lax.axis_size("st")
    replicas = lax.axis_size("dp")
    chips = shards // 2
    per_replica = chips // replicas

    own = grad_out[0, 0]
    pieces = pieces_of(own.shape[1])
    packed, *parts = pack(pos, qkv, own, early, pieces)
    packed_above = down(packed, "section")
    same = [[own]]
    other = []
    for step in range(1, chips):
        same.append([])
        for piece in range(pieces):
            same[-1].append(rotate(parts[piece], "st", 2 * step))
    other.append([swap(own, "st")])
    for step in range(1, chips):
        other.append([])
        for piece in range(pieces):
            other[-1].append(swap(same[step][piece], "st"))

    attended, total, *far_rows = forward(chips, pos, qkv, weight, own)
    acts = [attended]
    for step in range(1, replicas):
        acts.append(rotate(attended, "dp", step))

    whole = (heads * width,)
    halves = (early * width, late * width)
    depth = own.shape[1] // pieces
    direct, crossed = [], []
    for step in range(1, chips):
        for piece in range(pieces):
            start = piece * depth
            direct.append((far_rows[2 * step - 1], start, same[step][piece]))
            crossed.append((far_rows[2 * step], start, other[step][piece]))
    mate = (far_rows[0], 0, other[0][0])
    (total,) = project([mate] + direct + crossed[:-1], total, whole, F32)
    total = project([crossed[-1]], total, halves, BF16)
    d_early, d_late = total
    d_above = down(d_early, "section")
    grads_late = late_backward(pos, qkv, d_late)
    late_above = down(grads_late, "section")

    split = chips == pieces == 2
    near_far, cross_far = [], []
    for number in range(per_replica):
        straight, swapped = [], []
        for step in range(1, replicas):
            options = [parts[1], same[1][0]] if split else [value for (value,) in same]
            chosen = choose(replicas, number, step, options)
            got = [rotate(chosen, "dp", step)]
            mates = [swap(got[0], "st")]
            if split:
                got.append(rotate(got[0], "st", 2))
                mates.append(swap(got[1], "st"))
            straight.append(got)
            swapped.append(mates)
        near_far.append(straight)
        cross_far.append(swapped)

    begun, grad_weight = finish(
        packed_above, d_above, heads, acts, same + other, near_far + cross_far
    )
    upstream = fill(late_above, begun)
    return (grad_weight[None], upstream.transpose(0, 2, 1, 3)[None, None])


def solution(mesh):
    in_specs = (
        P("section", "dp", None, None, "st", None),
        P("section", "dp", None),
        P("section", None, "st"),
        P("section", "dp", None, "st"),
    )
    out_specs = (P("section", "dp", "st"), P("section", "dp", None, None, "st", None))

    return jax.shard_map(local, mesh=mesh, in_specs=in_specs, out_specs=out_specs, check_vma=False)
```

```python
import functools
import math

import jax
import jax.numpy as jnp
from jax import lax
from jax.experimental import pallas as pl
from jax.experimental.pallas import tpu as pltpu
from jax.sharding import PartitionSpec as P


F32 = jnp.float32
BF16 = jnp.bfloat16
VMEM = pl.BlockSpec(memory_space=pltpu.VMEM)
SMEM = pl.BlockSpec(memory_space=pltpu.SMEM)
ANY = pl.BlockSpec(memory_space=pl.ANY)
PARAMS = pltpu.CompilerParams(vmem_limit_bytes=24 * 2**20)


def in_hbm(value):
    return pltpu.with_memory_space_constraint(value, pltpu.HBM)


def dot(a, b, dims):
    return lax.dot_general(a, b, ((dims[0], dims[1]), ((), ())), preferred_element_type=F32)


def rotate(value, axis, steps):
    count = lax.axis_size(axis)
    return lax.ppermute(value, axis, [(i, (i + steps) % count) for i in range(count)])


def swap(value, axis):
    count = lax.axis_size(axis)
    return lax.ppermute(value, axis, [(i, i ^ 1) for i in range(count)])


def down(value, axis):
    count = lax.axis_size(axis)
    return lax.ppermute(value, axis, [(i, i - 1) for i in range(1, count)])


def visibility(positions):
    seq = positions.shape[-1]
    queries = jnp.broadcast_to(positions.astype(F32), (seq, seq))
    return queries.T <= queries


def softmax(visible, query, key):
    scores = dot(key, query, ((1,), (1,))) * (1.0 / math.sqrt(query.shape[-1]))
    scores = jnp.where(visible, scores, -1e30)
    exponent = jnp.exp(scores - jnp.max(scores, axis=0, keepdims=True))
    return exponent * (1.0 / jnp.sum(exponent, axis=0, keepdims=True))


def pack_kernel(rows, pos_ref, qkv_ref, own_ref, out_ref, *refs):
    parts, (held, sems) = refs[:-2], refs[-2:]
    gets = [pltpu.make_async_copy(pos_ref, held, sems.at[3])]
    gets += [
        pltpu.make_async_copy(
            qkv_ref.at[i, pl.ds(0, rows)], out_ref.at[pl.ds(i * rows, rows)], sems.at[i]
        )
        for i in range(3)
    ]
    for number, part in enumerate(parts):
        size = part.shape[1]
        gets.append(
            pltpu.make_async_copy(
                own_ref.at[:, pl.ds(number * size, size)], part, sems.at[4 + number]
            )
        )
    for get in gets:
        get.start()
    gets[0].wait()
    spare = (out_ref.shape[0] - 3 * rows, out_ref.shape[1])
    out_ref[3 * rows :] = jnp.broadcast_to(held[...].astype(F32), spare).astype(BF16)
    for get in gets[1:]:
        get.wait()


def pack(pos, qkv, own, early, pieces):
    _, _, seq, width = qkv.shape
    rows = early * seq
    part = pltpu.VMEM((seq, own.shape[1] // pieces), BF16)
    return pl.pallas_call(
        functools.partial(pack_kernel, rows),
        name="pack",
        in_specs=[ANY] * 3,
        out_specs=[VMEM] * (1 + pieces),
        out_shape=[pltpu.VMEM((3 * rows + 16, width), BF16)] + [part] * pieces,
        scratch_shapes=[
            pltpu.VMEM(pos.shape, pos.dtype),
            pltpu.SemaphoreType.DMA((4 + pieces,)),
        ],
        compiler_params=PARAMS,
    )(in_hbm(pos), in_hbm(qkv.reshape(3, -1, width)), in_hbm(own))


def place():
    me = lax.axis_index("st")
    return lax.div(me, 2), lax.rem(me, 2)


def rows_of(weight_ref, depth, chips, step, crossed):
    chip, core = place()
    owner = 2 * lax.rem(chip - step + chips, chips) + (1 - core if crossed else core)
    return weight_ref.at[pl.ds(pl.multiple_of(owner * depth, depth), depth)]


def forward_kernel(chips, groups, pos_ref, qkv_ref, weight_ref, own_ref, out_ref, total_ref, *refs):
    kept, (held, shard, buffer, rows, head_sems, sems) = refs[:-6], refs[-6:]
    heads, _, width = buffer.shape[1:]
    size = heads // groups
    gets = [pltpu.make_async_copy(pos_ref, held, head_sems.at[groups])]
    for group in range(groups):
        part = pl.ds(group * size, size)
        gets.append(
            pltpu.make_async_copy(qkv_ref.at[:, part], buffer.at[:, part], head_sems.at[group])
        )
    fetches = [
        pltpu.make_async_copy(
            rows_of(weight_ref, rows.shape[0], chips, number // 2, number % 2),
            target,
            sems.at[number],
        )
        for number, target in enumerate((rows, *kept))
    ]
    gets.append(pltpu.make_async_copy(own_ref, shard, head_sems.at[groups + 1]))
    for get in gets + fetches:
        get.start()
    gets[0].wait()
    visible = visibility(held[...])
    for head in range(heads):
        if head % size == 0:
            gets[1 + head // size].wait()
        probs = softmax(visible, buffer[0, head], buffer[1, head])
        attended = dot(probs.astype(BF16), buffer[2, head], ((0,), (0,)))
        out_ref[:, head * width : (head + 1) * width] = attended.astype(BF16)
    gets[-1].wait()
    fetches[0].wait()
    total_ref[...] = jnp.dot(shard[...], rows[...], preferred_element_type=F32)
    for fetch in fetches[1:]:
        fetch.wait()


def forward(chips, pos, qkv, weight, own):
    _, heads, seq, width = qkv.shape
    depth, columns = own.shape[1], weight.shape[1]
    count = 2 * chips - 1
    groups = max(size for size in (1, 2, 3) if heads % size == 0)
    return pl.pallas_call(
        functools.partial(forward_kernel, chips, groups),
        name="forward",
        in_specs=[ANY] * 4,
        out_specs=[VMEM] * (2 + count),
        out_shape=[
            jax.ShapeDtypeStruct((seq, heads * width), BF16),
            jax.ShapeDtypeStruct((seq, columns), F32),
        ]
        + [pltpu.VMEM((depth, columns), BF16)] * count,
        scratch_shapes=[
            pltpu.VMEM(pos.shape, pos.dtype),
            pltpu.VMEM(own.shape, BF16),
            pltpu.VMEM(qkv.shape, BF16),
            pltpu.VMEM((depth, columns), BF16),
            pltpu.SemaphoreType.DMA((groups + 2,)),
            pltpu.SemaphoreType.DMA((count + 1,)),
        ],
        compiler_params=PARAMS,
    )(in_hbm(pos), in_hbm(qkv), weight, in_hbm(own))


def head_gradients(visible, query, key, value, grad):
    scale = 1.0 / math.sqrt(query.shape[-1])
    probs = softmax(visible, query, key)
    d_value = dot(probs.astype(BF16), grad, ((1,), (0,)))
    d_probs = dot(value, grad, ((1,), (1,)))
    row_dot = jnp.sum(probs * d_probs, axis=0, keepdims=True)
    d_scores = (probs * (d_probs - row_dot)).astype(BF16)
    d_key = dot(d_scores, query, ((1,), (0,))) * scale
    d_query = dot(d_scores, key, ((0,), (0,))) * scale
    return d_query.astype(BF16), d_key.astype(BF16), d_value.astype(BF16)


def late_kernel(pos_ref, qkv_ref, grad_ref, out_ref):
    heads, _, width = out_ref.shape[1:]
    first = qkv_ref.shape[1] - heads
    visible = visibility(pos_ref[...])
    for head in range(heads):
        query, key, value = (qkv_ref[i, first + head] for i in range(3))
        grad = grad_ref[:, head * width : (head + 1) * width]
        for i, result in enumerate(head_gradients(visible, query, key, value, grad)):
            out_ref[i, head] = result


def late_backward(pos, qkv, grad):
    _, _, seq, width = qkv.shape
    heads = grad.shape[1] // width
    return pl.pallas_call(
        late_kernel,
        name="late_backward",
        in_specs=[VMEM] * 3,
        out_specs=VMEM,
        out_shape=pltpu.VMEM((3, heads, seq, width), BF16),
        compiler_params=PARAMS,
    )(pos, qkv, grad)


def fill_kernel(late_ref, whole_ref, out_ref, sems):
    late = late_ref.shape[1]
    first = out_ref.shape[1] - late
    puts = [
        pltpu.make_async_copy(late_ref.at[i], out_ref.at[i, pl.ds(first, late)], sems.at[i])
        for i in range(3)
    ]
    for put in puts:
        put.start()
    for put in puts:
        put.wait()


def fill(late, whole):
    return pl.pallas_call(
        fill_kernel,
        name="fill",
        in_specs=[VMEM, ANY],
        out_specs=ANY,
        out_shape=jax.ShapeDtypeStruct(whole.shape, whole.dtype),
        scratch_shapes=[pltpu.SemaphoreType.DMA((3,))],
        input_output_aliases={1: 0},
        compiler_params=PARAMS,
    )(late, whole)


def project_kernel(terms, splits, *refs):
    count = 1 + max(number for number, _ in terms)
    weights, grads = refs[:count], refs[count : count + len(terms)]
    refs = refs[count + len(terms) :]
    total = refs[0][...]
    for (number, start), grad in zip(terms, grads):
        rows = weights[number][start : start + grad.shape[1]]
        total = total + jnp.dot(grad[...], rows, preferred_element_type=F32)
    at = 0
    for out, size in zip(refs[1:], splits):
        out[...] = total[:, at : at + size].astype(out.dtype)
        at += size


def project(items, total, splits, dtype):
    weights, terms = [], []
    for weight, start, _ in items:
        found = [number for number, known in enumerate(weights) if known is weight]
        if not found:
            weights.append(weight)
        terms.append((found[0] if found else len(weights) - 1, start))
    grads = [grad for _, _, grad in items]
    seq = grads[0].shape[0]
    return pl.pallas_call(
        functools.partial(project_kernel, tuple(terms), splits),
        name="project",
        in_specs=[VMEM] * (len(weights) + len(grads) + 1),
        out_specs=[VMEM] * len(splits),
        out_shape=[jax.ShapeDtypeStruct((seq, size), dtype) for size in splits],
        compiler_params=PARAMS,
    )(*weights, *grads, total)


def counts(options):
    return tuple(len(pieces) for pieces in options)


def grouped(refs, sizes):
    refs = list(refs)
    return [[refs.pop(0) for _ in range(size)] for size in sizes]


def choose_kernel(per_replica, number, step, replicas, *refs):
    chips = len(refs) - 1
    chip, _ = place()
    target = lax.rem(lax.axis_index("dp") + step, replicas)
    index = lax.rem(chip - (target * per_replica + number) + chips, chips)
    for option, ref in enumerate(refs[:-1]):

        @pl.when(index == option)
        def _():
            refs[-1][...] = ref[...]


def choose(replicas, number, step, options):
    chips = len(options)
    return pl.pallas_call(
        functools.partial(choose_kernel, chips // replicas, number, step, replicas),
        name="choose",
        in_specs=[VMEM] * chips,
        out_specs=VMEM,
        out_shape=jax.ShapeDtypeStruct(options[0].shape, options[0].dtype),
        compiler_params=PARAMS,
    )(*options)


def write_rows(parity, replicas, sizes, far_sizes, slots, blocks, refs, out_ref, scratch):
    refs = list(refs)
    acts = [refs.pop(0) for _ in range(replicas)]
    options = grouped(refs, sizes)
    far = grouped(refs[sum(sizes) :], far_sizes)
    stacked, ready, sems = scratch
    seq = acts[0].shape[0]
    for number, act in enumerate(acts):
        stacked[number * seq : (number + 1) * seq] = act[...]
    chip, core = place()
    chips = len(sizes)
    size = ready.shape[1]
    spans = [(slot, block * size, size) for slot in range(slots) for block in range(blocks)]
    if parity and size % 256 == 0:
        slot, first, _ = spans.pop()
        spans += [(slot, first, size // 2), (slot, first + size // 2, size // 2)]
    puts = []
    for number, (slot, first, count) in enumerate(spans):
        index = lax.rem(chip - (lax.axis_index("dp") * slots + slot) + chips, chips)

        def part(pieces):
            piece, at = divmod(first, pieces[0].shape[1])
            return pieces[piece][:, at : at + count]

        near = None
        for option, pieces in enumerate(options):
            own = part(pieces)
            near = own if near is None else jnp.where(index == option, own, near)
        left = [near]
        for pieces in far[slot * (replicas - 1) : (slot + 1) * (replicas - 1)]:
            if len(pieces) == 2:
                left.append(jnp.where(index == 1, part(pieces), part(pieces[::-1])))
            else:
                left.append(part(pieces))
        block = dot(jnp.concatenate(left, axis=0), stacked[...], ((0,), (0,))).astype(BF16)
        if number >= 2:
            puts[number - 2].wait()
        place_in = ready.at[number % 2, pl.ds(0, count)]
        place_in[...] = block
        row = (2 * slot + lax.rem(core + parity, 2)) * (size * blocks) + first
        target = out_ref.at[pl.ds(pl.multiple_of(row, 128), count)]
        puts.append(pltpu.make_async_copy(place_in, target, sems.at[number % 2]))
        puts[-1].start()
    return puts[-2:]


def finish_kernel(setting, packed_ref, grad_ref, *refs):
    args, (out_ref, weight_ref, held, head_sems), scratch = refs[:-7], refs[-7:-3], refs[-3:]
    heads, seq, width = held.shape[1:]
    copies = []
    visible = visibility(packed_ref[3 * heads * seq :][:1])
    for head in range(heads):
        query, key, value = (
            packed_ref[(i * heads + head) * seq : (i * heads + head + 1) * seq] for i in range(3)
        )
        grad = grad_ref[:, head * width : (head + 1) * width]
        for i, result in enumerate(head_gradients(visible, query, key, value, grad)):
            held[i, head] = result
        copies.append(
            pltpu.make_async_copy(held.at[:, head], out_ref.at[:, head], head_sems.at[head])
        )
        copies[-1].start()
    copies += write_rows(0, *setting, args, weight_ref, scratch)
    for copy in copies:
        copy.wait()


def complete_kernel(setting, *refs):
    args, weight_ref, scratch = refs[:-5], refs[-4], refs[-3:]
    for copy in write_rows(1, *setting, args, weight_ref, scratch):
        copy.wait()


def weight_call(acts, options, far):
    replicas, slots = len(acts), len(far)
    far = [pieces for slot in far for pieces in slot]
    seq, columns = acts[0].shape
    features = sum(piece.shape[1] for piece in far[0])
    blocks = max(counts(options))
    args = [*acts, *[piece for pieces in options for piece in pieces]]
    args += [piece for pieces in far for piece in pieces]
    scratch = [
        pltpu.VMEM((replicas * seq, columns), BF16),
        pltpu.VMEM((2, features // blocks, columns), BF16),
        pltpu.SemaphoreType.DMA((2,)),
    ]
    setting = (replicas, counts(options), counts(far), slots, blocks)
    return setting, args, scratch, jax.ShapeDtypeStruct((2 * slots * features, columns), BF16)


def finish(packed, grad, total, acts, options, far):
    seq, width = grad.shape[0], packed.shape[1]
    heads = grad.shape[1] // width
    setting, args, scratch, shape = weight_call(acts, options, far)
    return pl.pallas_call(
        functools.partial(finish_kernel, setting),
        name="finish",
        in_specs=[VMEM] * (2 + len(args)),
        out_specs=[ANY, ANY],
        out_shape=[jax.ShapeDtypeStruct((3, total, seq, width), BF16), shape],
        scratch_shapes=[
            pltpu.VMEM((3, heads, seq, width), BF16),
            pltpu.SemaphoreType.DMA((heads,)),
            *scratch,
        ],
        compiler_params=PARAMS,
    )(packed, grad, *args)


def complete(acts, options, far, begun):
    setting, args, scratch, shape = weight_call(acts, options, far)
    return pl.pallas_call(
        functools.partial(complete_kernel, setting),
        name="complete",
        in_specs=[VMEM] * len(args) + [ANY],
        out_specs=ANY,
        out_shape=shape,
        scratch_shapes=scratch,
        input_output_aliases={len(args): 0},
        compiler_params=PARAMS,
    )(*args, begun)


def pieces_of(features):
    return 2 if features % 256 == 0 else 1


def local(saved_qkv, positions, w_out, grad_out):
    qkv = saved_qkv[0, 0].transpose(0, 2, 1, 3)
    pos = positions[0]
    weight = in_hbm(w_out[0])
    heads, _, width = qkv.shape[1:]
    early = max(1, heads * 8 // 12)
    late = heads - early
    shards = lax.axis_size("st")
    replicas = lax.axis_size("dp")
    chips = shards // 2
    per_replica = chips // replicas

    own = grad_out[0, 0]
    pieces = pieces_of(own.shape[1])
    packed, *parts = pack(pos, qkv, own, early, pieces)
    packed_above = down(packed, "section")
    same = [[own]]
    other = []
    for step in range(1, chips):
        same.append([])
        for piece in range(pieces):
            same[-1].append(rotate(parts[piece], "st", 2 * step))
    other.append([swap(own, "st")])
    for step in range(1, chips):
        other.append([])
        for piece in range(pieces):
            other[-1].append(swap(same[step][piece], "st"))

    attended, total, *far_rows = forward(chips, pos, qkv, weight, own)
    acts = [attended]
    for step in range(1, replicas):
        acts.append(rotate(attended, "dp", step))

    whole = (heads * width,)
    halves = (early * width, late * width)
    depth = own.shape[1] // pieces
    direct, crossed = [], []
    for step in range(1, chips):
        for piece in range(pieces):
            start = piece * depth
            direct.append((far_rows[2 * step - 1], start, same[step][piece]))
            crossed.append((far_rows[2 * step], start, other[step][piece]))
    mate = (far_rows[0], 0, other[0][0])
    (total,) = project([mate] + direct + crossed[:-1], total, whole, F32)
    total = project([crossed[-1]], total, halves, BF16)
    d_early, d_late = total
    d_above = down(d_early, "section")
    grads_late = late_backward(pos, qkv, d_late)
    late_above = down(grads_late, "section")

    split = chips == pieces == 2
    near_far, cross_far = [], []
    for number in range(per_replica):
        straight, swapped = [], []
        for step in range(1, replicas):
            options = [parts[1], same[1][0]] if split else [value for (value,) in same]
            chosen = choose(replicas, number, step, options)
            got = [rotate(chosen, "dp", step)]
            mates = [swap(got[0], "st")]
            if split:
                got.append(rotate(got[0], "st", 2))
                mates.append(swap(got[1], "st"))
            straight.append(got)
            swapped.append(mates)
        near_far.append(straight)
        cross_far.append(swapped)

    begun, grad_weight = finish(packed_above, d_above, heads, acts, same, near_far)
    grad_weight = complete(acts, other, cross_far, grad_weight)
    upstream = fill(late_above, begun)
    return (grad_weight[None], upstream.transpose(0, 2, 1, 3)[None, None])


def solution(mesh):
    in_specs = (
        P("section", "dp", None, None, "st", None),
        P("section", "dp", None),
        P("section", None, "st"),
        P("section", "dp", None, "st"),
    )
    out_specs = (P("section", "dp", "st"), P("section", "dp", None, None, "st", None))

    return jax.shard_map(local, mesh=mesh, in_specs=in_specs, out_specs=out_specs, check_vma=False)
```

```python
import functools
import math

import jax
import jax.numpy as jnp
from jax import lax
from jax.experimental import pallas as pl
from jax.experimental.pallas import tpu as pltpu
from jax.sharding import PartitionSpec as P


F32 = jnp.float32
BF16 = jnp.bfloat16
VMEM = pl.BlockSpec(memory_space=pltpu.VMEM)
SMEM = pl.BlockSpec(memory_space=pltpu.SMEM)
ANY = pl.BlockSpec(memory_space=pl.ANY)
PARAMS = pltpu.CompilerParams(vmem_limit_bytes=24 * 2**20)


def in_hbm(value):
    return pltpu.with_memory_space_constraint(value, pltpu.HBM)


def dot(a, b, dims):
    return lax.dot_general(a, b, ((dims[0], dims[1]), ((), ())), preferred_element_type=F32)


def rotate(value, axis, steps):
    count = lax.axis_size(axis)
    return lax.ppermute(value, axis, [(i, (i + steps) % count) for i in range(count)])


def swap(value, axis):
    count = lax.axis_size(axis)
    return lax.ppermute(value, axis, [(i, i ^ 1) for i in range(count)])


def down(value, axis):
    count = lax.axis_size(axis)
    return lax.ppermute(value, axis, [(i, i - 1) for i in range(1, count)])


def visibility(positions):
    seq = positions.shape[-1]
    queries = jnp.broadcast_to(positions.astype(F32), (seq, seq))
    return queries.T <= queries


def softmax(visible, query, key):
    scores = dot(key, query, ((1,), (1,))) * (1.0 / math.sqrt(query.shape[-1]))
    scores = jnp.where(visible, scores, -1e30)
    exponent = jnp.exp(scores - jnp.max(scores, axis=0, keepdims=True))
    return exponent * (1.0 / jnp.sum(exponent, axis=0, keepdims=True))


def pack_kernel(rows, pos_ref, qkv_ref, own_ref, out_ref, *refs):
    parts, (held, sems) = refs[:-2], refs[-2:]
    gets = [pltpu.make_async_copy(pos_ref, held, sems.at[3])]
    gets += [
        pltpu.make_async_copy(
            qkv_ref.at[i, pl.ds(0, rows)], out_ref.at[pl.ds(i * rows, rows)], sems.at[i]
        )
        for i in range(3)
    ]
    for number, part in enumerate(parts):
        size = part.shape[1]
        gets.append(
            pltpu.make_async_copy(
                own_ref.at[:, pl.ds(number * size, size)], part, sems.at[4 + number]
            )
        )
    for get in gets:
        get.start()
    gets[0].wait()
    spare = (out_ref.shape[0] - 3 * rows, out_ref.shape[1])
    out_ref[3 * rows :] = jnp.broadcast_to(held[...].astype(F32), spare).astype(BF16)
    for get in gets[1:]:
        get.wait()


def pack(pos, qkv, own, early, pieces):
    _, _, seq, width = qkv.shape
    rows = early * seq
    part = pltpu.VMEM((seq, own.shape[1] // pieces), BF16)
    return pl.pallas_call(
        functools.partial(pack_kernel, rows),
        name="pack",
        in_specs=[ANY] * 3,
        out_specs=[VMEM] * (1 + pieces),
        out_shape=[pltpu.VMEM((3 * rows + 16, width), BF16)] + [part] * pieces,
        scratch_shapes=[
            pltpu.VMEM(pos.shape, pos.dtype),
            pltpu.SemaphoreType.DMA((4 + pieces,)),
        ],
        compiler_params=PARAMS,
    )(in_hbm(pos), in_hbm(qkv.reshape(3, -1, width)), in_hbm(own))


def place():
    me = lax.axis_index("st")
    return lax.div(me, 2), lax.rem(me, 2)


def rows_of(weight_ref, depth, chips, step, crossed):
    chip, core = place()
    owner = 2 * lax.rem(chip - step + chips, chips) + (1 - core if crossed else core)
    return weight_ref.at[pl.ds(pl.multiple_of(owner * depth, depth), depth)]


def forward_kernel(chips, early, pieces, qkv_ref, weight_ref, packed_ref, *refs):
    parts, refs = refs[:pieces], refs[pieces:]
    out_ref, total_ref = refs[:2]
    kept, (buffer, rows, late_sem, sems) = refs[2:-4], refs[-4:]
    late, seq, width = buffer.shape[1:]
    fetches = [
        pltpu.make_async_copy(
            rows_of(weight_ref, rows.shape[0], chips, number // 2, number % 2),
            target,
            sems.at[number],
        )
        for number, target in enumerate((rows, *kept))
    ]
    get = pltpu.make_async_copy(qkv_ref.at[:, pl.ds(early, late)], buffer, late_sem.at[0])
    get.start()
    for fetch in fetches:
        fetch.start()
    visible = visibility(packed_ref[3 * early * seq :][:1])
    for head in range(early + late):
        if head < early:
            query, key, value = (
                packed_ref[(i * early + head) * seq : (i * early + head + 1) * seq]
                for i in range(3)
            )
        else:
            if head == early:
                get.wait()
            query, key, value = (buffer[i, head - early] for i in range(3))
        probs = softmax(visible, query, key)
        attended = dot(probs.astype(BF16), value, ((0,), (0,)))
        out_ref[:, head * width : (head + 1) * width] = attended.astype(BF16)
    fetches[0].wait()
    size = rows.shape[0] // pieces
    total = None
    for number, part in enumerate(parts):
        product = jnp.dot(
            part[...], rows[number * size : (number + 1) * size], preferred_element_type=F32
        )
        total = product if total is None else total + product
    total_ref[...] = total
    for fetch in fetches[1:]:
        fetch.wait()


def forward(chips, early, qkv, weight, packed, parts):
    _, heads, seq, width = qkv.shape
    depth, columns = len(parts) * parts[0].shape[1], weight.shape[1]
    count = 2 * chips - 1
    return pl.pallas_call(
        functools.partial(forward_kernel, chips, early, len(parts)),
        name="forward",
        in_specs=[ANY, ANY] + [VMEM] * (1 + len(parts)),
        out_specs=[VMEM] * (2 + count),
        out_shape=[
            jax.ShapeDtypeStruct((seq, heads * width), BF16),
            jax.ShapeDtypeStruct((seq, columns), F32),
        ]
        + [pltpu.VMEM((depth, columns), BF16)] * count,
        scratch_shapes=[
            pltpu.VMEM((3, heads - early, seq, width), BF16),
            pltpu.VMEM((depth, columns), BF16),
            pltpu.SemaphoreType.DMA((1,)),
            pltpu.SemaphoreType.DMA((count + 1,)),
        ],
        compiler_params=PARAMS,
    )(in_hbm(qkv), weight, packed, *parts)


def head_gradients(visible, query, key, value, grad):
    scale = 1.0 / math.sqrt(query.shape[-1])
    probs = softmax(visible, query, key)
    d_value = dot(probs.astype(BF16), grad, ((1,), (0,)))
    d_probs = dot(value, grad, ((1,), (1,)))
    row_dot = jnp.sum(probs * d_probs, axis=0, keepdims=True)
    d_scores = (probs * (d_probs - row_dot)).astype(BF16)
    d_key = dot(d_scores, query, ((1,), (0,))) * scale
    d_query = dot(d_scores, key, ((0,), (0,))) * scale
    return d_query.astype(BF16), d_key.astype(BF16), d_value.astype(BF16)


def late_kernel(pos_ref, qkv_ref, grad_ref, out_ref):
    heads, _, width = out_ref.shape[1:]
    first = qkv_ref.shape[1] - heads
    visible = visibility(pos_ref[...])
    for head in range(heads):
        query, key, value = (qkv_ref[i, first + head] for i in range(3))
        grad = grad_ref[:, head * width : (head + 1) * width]
        for i, result in enumerate(head_gradients(visible, query, key, value, grad)):
            out_ref[i, head] = result


def late_backward(pos, qkv, grad):
    _, _, seq, width = qkv.shape
    heads = grad.shape[1] // width
    return pl.pallas_call(
        late_kernel,
        name="late_backward",
        in_specs=[VMEM] * 3,
        out_specs=VMEM,
        out_shape=pltpu.VMEM((3, heads, seq, width), BF16),
        compiler_params=PARAMS,
    )(pos, qkv, grad)


def fill_kernel(late_ref, whole_ref, out_ref, sems):
    late = late_ref.shape[1]
    first = out_ref.shape[1] - late
    puts = [
        pltpu.make_async_copy(late_ref.at[i], out_ref.at[i, pl.ds(first, late)], sems.at[i])
        for i in range(3)
    ]
    for put in puts:
        put.start()
    for put in puts:
        put.wait()


def fill(late, whole):
    return pl.pallas_call(
        fill_kernel,
        name="fill",
        in_specs=[VMEM, ANY],
        out_specs=ANY,
        out_shape=jax.ShapeDtypeStruct(whole.shape, whole.dtype),
        scratch_shapes=[pltpu.SemaphoreType.DMA((3,))],
        input_output_aliases={1: 0},
        compiler_params=PARAMS,
    )(late, whole)


def project_kernel(terms, splits, *refs):
    count = 1 + max(number for number, _ in terms)
    weights, grads = refs[:count], refs[count : count + len(terms)]
    refs = refs[count + len(terms) :]
    total = refs[0][...]
    for (number, start), grad in zip(terms, grads):
        rows = weights[number][start : start + grad.shape[1]]
        total = total + jnp.dot(grad[...], rows, preferred_element_type=F32)
    at = 0
    for out, size in zip(refs[1:], splits):
        out[...] = total[:, at : at + size].astype(out.dtype)
        at += size


def project(items, total, splits, dtype):
    weights, terms = [], []
    for weight, start, _ in items:
        found = [number for number, known in enumerate(weights) if known is weight]
        if not found:
            weights.append(weight)
        terms.append((found[0] if found else len(weights) - 1, start))
    grads = [grad for _, _, grad in items]
    seq = grads[0].shape[0]
    return pl.pallas_call(
        functools.partial(project_kernel, tuple(terms), splits),
        name="project",
        in_specs=[VMEM] * (len(weights) + len(grads) + 1),
        out_specs=[VMEM] * len(splits),
        out_shape=[jax.ShapeDtypeStruct((seq, size), dtype) for size in splits],
        compiler_params=PARAMS,
    )(*weights, *grads, total)


def counts(options):
    return tuple(len(pieces) for pieces in options)


def grouped(refs, sizes):
    refs = list(refs)
    return [[refs.pop(0) for _ in range(size)] for size in sizes]


def choose_kernel(per_replica, number, step, replicas, *refs):
    chips = len(refs) - 1
    chip, _ = place()
    target = lax.rem(lax.axis_index("dp") + step, replicas)
    index = lax.rem(chip - (target * per_replica + number) + chips, chips)
    for option, ref in enumerate(refs[:-1]):

        @pl.when(index == option)
        def _():
            refs[-1][...] = ref[...]


def choose(replicas, number, step, options):
    chips = len(options)
    return pl.pallas_call(
        functools.partial(choose_kernel, chips // replicas, number, step, replicas),
        name="choose",
        in_specs=[VMEM] * chips,
        out_specs=VMEM,
        out_shape=jax.ShapeDtypeStruct(options[0].shape, options[0].dtype),
        compiler_params=PARAMS,
    )(*options)


def finish_kernel(replicas, sizes, far_sizes, slots, blocks, packed_ref, grad_ref, *refs):
    refs = list(refs)
    acts = [refs.pop(0) for _ in range(replicas)]
    options = grouped(refs, sizes)
    far = grouped(refs[sum(sizes) :], far_sizes)
    out_ref, weight_ref, held, stacked, ready, head_sems, sems = refs[-7:]
    heads, seq, width = held.shape[1:]
    copies = []
    visible = visibility(packed_ref[3 * heads * seq :][:1])
    for head in range(heads):
        query, key, value = (
            packed_ref[(i * heads + head) * seq : (i * heads + head + 1) * seq] for i in range(3)
        )
        grad = grad_ref[:, head * width : (head + 1) * width]
        for i, result in enumerate(head_gradients(visible, query, key, value, grad)):
            held[i, head] = result
        copies.append(
            pltpu.make_async_copy(held.at[:, head], out_ref.at[:, head], head_sems.at[head])
        )
        copies[-1].start()

    for number, act in enumerate(acts):
        stacked[number * seq : (number + 1) * seq] = act[...]
    chip, core = place()
    chips = len(sizes) // 2
    size = ready.shape[1]
    spans = [(turn, block * size, size) for turn in range(2 * slots) for block in range(blocks)]
    if size % 256 == 0:
        turn, first, _ = spans.pop()
        spans += [(turn, first, size // 2), (turn, first + size // 2, size // 2)]
    puts = []
    for number, (turn, first, count) in enumerate(spans):
        parity, slot = divmod(turn, slots)
        index = lax.rem(chip - (lax.axis_index("dp") * slots + slot) + chips, chips)

        def part(pieces):
            piece, at = divmod(first, pieces[0].shape[1])
            return pieces[piece][:, at : at + count]

        near = None
        for option, pieces in enumerate(options[parity * chips : (parity + 1) * chips]):
            own = part(pieces)
            near = own if near is None else jnp.where(index == option, own, near)
        left = [near]
        for pieces in far[turn * (replicas - 1) : (turn + 1) * (replicas - 1)]:
            if len(pieces) == 2:
                left.append(jnp.where(index == 1, part(pieces), part(pieces[::-1])))
            else:
                left.append(part(pieces))
        block = dot(jnp.concatenate(left, axis=0), stacked[...], ((0,), (0,))).astype(BF16)
        if number >= 2:
            puts[number - 2].wait()
        place_in = ready.at[number % 2, pl.ds(0, count)]
        place_in[...] = block
        row = (2 * slot + lax.rem(core + parity, 2)) * (size * blocks) + first
        target = weight_ref.at[pl.ds(pl.multiple_of(row, 128), count)]
        puts.append(pltpu.make_async_copy(place_in, target, sems.at[number % 2]))
        puts[-1].start()
    for copy in copies + puts[-2:]:
        copy.wait()


def finish(packed, grad, total, acts, options, far):
    seq, width = grad.shape[0], packed.shape[1]
    heads = grad.shape[1] // width
    replicas, slots = len(acts), len(far) // 2
    far = [pieces for slot in far for pieces in slot]
    columns = acts[0].shape[1]
    features = sum(piece.shape[1] for piece in far[0])
    blocks = max(counts(options))
    size = features // blocks
    args = [*acts, *[piece for pieces in options for piece in pieces]]
    args += [piece for pieces in far for piece in pieces]
    return pl.pallas_call(
        functools.partial(finish_kernel, replicas, counts(options), counts(far), slots, blocks),
        name="finish",
        in_specs=[VMEM] * (2 + len(args)),
        out_specs=[ANY, ANY],
        out_shape=[
            jax.ShapeDtypeStruct((3, total, seq, width), BF16),
            jax.ShapeDtypeStruct((2 * slots * features, columns), BF16),
        ],
        scratch_shapes=[
            pltpu.VMEM((3, heads, seq, width), BF16),
            pltpu.VMEM((replicas * seq, columns), BF16),
            pltpu.VMEM((2, size, columns), BF16),
            pltpu.SemaphoreType.DMA((heads,)),
            pltpu.SemaphoreType.DMA((2,)),
        ],
        compiler_params=PARAMS,
    )(packed, grad, *args)


def pieces_of(features):
    return 2 if features % 256 == 0 else 1


def local(saved_qkv, positions, w_out, grad_out):
    qkv = saved_qkv[0, 0].transpose(0, 2, 1, 3)
    pos = positions[0]
    weight = in_hbm(w_out[0])
    heads, _, width = qkv.shape[1:]
    early = max(1, heads * 8 // 12)
    late = heads - early
    shards = lax.axis_size("st")
    replicas = lax.axis_size("dp")
    chips = shards // 2
    per_replica = chips // replicas

    own = grad_out[0, 0]
    pieces = pieces_of(own.shape[1])
    packed, *parts = pack(pos, qkv, own, early, pieces)
    packed_above = down(packed, "section")
    same = [[own]]
    other = []
    for step in range(1, chips):
        same.append([])
        for piece in range(pieces):
            same[-1].append(rotate(parts[piece], "st", 2 * step))
    other.append([swap(own, "st")])
    for step in range(1, chips):
        other.append([])
        for piece in range(pieces):
            other[-1].append(swap(same[step][piece], "st"))

    attended, total, *far_rows = forward(chips, early, qkv, weight, packed, parts)
    acts = [attended]
    for step in range(1, replicas):
        acts.append(rotate(attended, "dp", step))

    whole = (heads * width,)
    halves = (early * width, late * width)
    depth = own.shape[1] // pieces
    direct, crossed = [], []
    for step in range(1, chips):
        for piece in range(pieces):
            start = piece * depth
            direct.append((far_rows[2 * step - 1], start, same[step][piece]))
            crossed.append((far_rows[2 * step], start, other[step][piece]))
    mate = (far_rows[0], 0, other[0][0])
    (total,) = project([mate] + direct + crossed[:-1], total, whole, F32)
    total = project([crossed[-1]], total, halves, BF16)
    d_early, d_late = total
    d_above = down(d_early, "section")
    grads_late = late_backward(pos, qkv, d_late)
    late_above = down(grads_late, "section")

    split = chips == pieces == 2
    near_far, cross_far = [], []
    for number in range(per_replica):
        straight, swapped = [], []
        for step in range(1, replicas):
            options = [parts[1], same[1][0]] if split else [value for (value,) in same]
            chosen = choose(replicas, number, step, options)
            got = [rotate(chosen, "dp", step)]
            mates = [swap(got[0], "st")]
            if split:
                got.append(rotate(got[0], "st", 2))
                mates.append(swap(got[1], "st"))
            straight.append(got)
            swapped.append(mates)
        near_far.append(straight)
        cross_far.append(swapped)

    begun, grad_weight = finish(
        packed_above, d_above, heads, acts, same + other, near_far + cross_far
    )
    upstream = fill(late_above, begun)
    return (grad_weight[None], upstream.transpose(0, 2, 1, 3)[None, None])


def solution(mesh):
    in_specs = (
        P("section", "dp", None, None, "st", None),
        P("section", "dp", None),
        P("section", None, "st"),
        P("section", "dp", None, "st"),
    )
    out_specs = (P("section", "dp", "st"), P("section", "dp", None, None, "st", None))

    return jax.shard_map(local, mesh=mesh, in_specs=in_specs, out_specs=out_specs, check_vma=False)
```

```python
import functools
import math

import jax
import jax.numpy as jnp
from jax import lax
from jax.experimental import pallas as pl
from jax.experimental.pallas import tpu as pltpu
from jax.sharding import PartitionSpec as P


F32 = jnp.float32
BF16 = jnp.bfloat16
VMEM = pl.BlockSpec(memory_space=pltpu.VMEM)
SMEM = pl.BlockSpec(memory_space=pltpu.SMEM)
ANY = pl.BlockSpec(memory_space=pl.ANY)
PARAMS = pltpu.CompilerParams(vmem_limit_bytes=24 * 2**20)


def in_hbm(value):
    return pltpu.with_memory_space_constraint(value, pltpu.HBM)


def dot(a, b, dims):
    return lax.dot_general(a, b, ((dims[0], dims[1]), ((), ())), preferred_element_type=F32)


def rotate(value, axis, steps):
    count = lax.axis_size(axis)
    return lax.ppermute(value, axis, [(i, (i + steps) % count) for i in range(count)])


def swap(value, axis):
    count = lax.axis_size(axis)
    return lax.ppermute(value, axis, [(i, i ^ 1) for i in range(count)])


def down(value, axis):
    count = lax.axis_size(axis)
    return lax.ppermute(value, axis, [(i, i - 1) for i in range(1, count)])


def visibility(positions):
    seq = positions.shape[-1]
    queries = jnp.broadcast_to(positions.astype(F32), (seq, seq))
    return queries.T <= queries


def softmax(visible, query, key):
    scores = dot(key, query, ((1,), (1,))) * (1.0 / math.sqrt(query.shape[-1]))
    scores = jnp.where(visible, scores, -1e30)
    exponent = jnp.exp(scores - jnp.max(scores, axis=0, keepdims=True))
    return exponent * (1.0 / jnp.sum(exponent, axis=0, keepdims=True))


def pack_kernel(rows, pos_ref, qkv_ref, own_ref, out_ref, *refs):
    parts, (held, sems) = refs[:-2], refs[-2:]
    gets = [pltpu.make_async_copy(pos_ref, held, sems.at[3])]
    gets += [
        pltpu.make_async_copy(
            qkv_ref.at[i, pl.ds(0, rows)], out_ref.at[pl.ds(i * rows, rows)], sems.at[i]
        )
        for i in range(3)
    ]
    for number, part in enumerate(parts):
        size = part.shape[1]
        gets.append(
            pltpu.make_async_copy(
                own_ref.at[:, pl.ds(number * size, size)], part, sems.at[4 + number]
            )
        )
    for get in gets:
        get.start()
    gets[0].wait()
    spare = (out_ref.shape[0] - 3 * rows, out_ref.shape[1])
    out_ref[3 * rows :] = jnp.broadcast_to(held[...].astype(F32), spare).astype(BF16)
    for get in gets[1:]:
        get.wait()


def pack(pos, qkv, own, early, pieces):
    _, _, seq, width = qkv.shape
    rows = early * seq
    part = pltpu.VMEM((seq, own.shape[1] // pieces), BF16)
    return pl.pallas_call(
        functools.partial(pack_kernel, rows),
        name="pack",
        in_specs=[ANY] * 3,
        out_specs=[VMEM] * (1 + pieces),
        out_shape=[pltpu.VMEM((3 * rows + 16, width), BF16)] + [part] * pieces,
        scratch_shapes=[
            pltpu.VMEM(pos.shape, pos.dtype),
            pltpu.SemaphoreType.DMA((4 + pieces,)),
        ],
        compiler_params=PARAMS,
    )(in_hbm(pos), in_hbm(qkv.reshape(3, -1, width)), in_hbm(own))


def place():
    me = lax.axis_index("st")
    return lax.div(me, 2), lax.rem(me, 2)


def rows_of(weight_ref, depth, chips, step, crossed):
    chip, core = place()
    owner = 2 * lax.rem(chip - step + chips, chips) + (1 - core if crossed else core)
    return weight_ref.at[pl.ds(pl.multiple_of(owner * depth, depth), depth)]


def forward_kernel(chips, early, pieces, qkv_ref, weight_ref, packed_ref, *refs):
    parts, refs = refs[:pieces], refs[pieces:]
    out_ref, total_ref = refs[:2]
    kept, (buffer, rows, late_sem, sems) = refs[2:-4], refs[-4:]
    late, seq, width = buffer.shape[1:]
    fetches = [
        pltpu.make_async_copy(
            rows_of(weight_ref, rows.shape[0], chips, number // 2, number % 2),
            target,
            sems.at[number],
        )
        for number, target in enumerate((rows, *kept))
    ]
    get = pltpu.make_async_copy(qkv_ref.at[:, pl.ds(early, late)], buffer, late_sem.at[0])
    get.start()
    for fetch in fetches:
        fetch.start()
    visible = visibility(packed_ref[3 * early * seq :][:1])
    chip, _ = place()

    def attend(heads):
        for head in heads:
            if head < early:
                query, key, value = (
                    packed_ref[(i * early + head) * seq : (i * early + head + 1) * seq]
                    for i in range(3)
                )
            else:
                query, key, value = (buffer[i, head - early] for i in range(3))
            probs = softmax(visible, query, key)
            attended = dot(probs.astype(BF16), value, ((0,), (0,)))
            out_ref[:, head * width : (head + 1) * width] = attended.astype(BF16)

    for first in range(0, early, 4):
        pl.when(chip >= 0)(functools.partial(attend, range(first, min(first + 4, early))))
    get.wait()
    attend(range(early, early + late))
    fetches[0].wait()
    size = rows.shape[0] // pieces
    total = None
    for number, part in enumerate(parts):
        product = jnp.dot(
            part[...], rows[number * size : (number + 1) * size], preferred_element_type=F32
        )
        total = product if total is None else total + product
    total_ref[...] = total
    for fetch in fetches[1:]:
        fetch.wait()


def forward(chips, early, qkv, weight, packed, parts):
    _, heads, seq, width = qkv.shape
    depth, columns = len(parts) * parts[0].shape[1], weight.shape[1]
    count = 2 * chips - 1
    return pl.pallas_call(
        functools.partial(forward_kernel, chips, early, len(parts)),
        name="forward",
        in_specs=[ANY, ANY] + [VMEM] * (1 + len(parts)),
        out_specs=[VMEM] * (2 + count),
        out_shape=[
            jax.ShapeDtypeStruct((seq, heads * width), BF16),
            jax.ShapeDtypeStruct((seq, columns), F32),
        ]
        + [pltpu.VMEM((depth, columns), BF16)] * count,
        scratch_shapes=[
            pltpu.VMEM((3, heads - early, seq, width), BF16),
            pltpu.VMEM((depth, columns), BF16),
            pltpu.SemaphoreType.DMA((1,)),
            pltpu.SemaphoreType.DMA((count + 1,)),
        ],
        compiler_params=PARAMS,
    )(in_hbm(qkv), weight, packed, *parts)


def head_gradients(visible, query, key, value, grad):
    scale = 1.0 / math.sqrt(query.shape[-1])
    probs = softmax(visible, query, key)
    d_value = dot(probs.astype(BF16), grad, ((1,), (0,)))
    d_probs = dot(value, grad, ((1,), (1,)))
    row_dot = jnp.sum(probs * d_probs, axis=0, keepdims=True)
    d_scores = (probs * (d_probs - row_dot)).astype(BF16)
    d_key = dot(d_scores, query, ((1,), (0,))) * scale
    d_query = dot(d_scores, key, ((0,), (0,))) * scale
    return d_query.astype(BF16), d_key.astype(BF16), d_value.astype(BF16)


def late_kernel(pos_ref, qkv_ref, grad_ref, out_ref):
    heads, _, width = out_ref.shape[1:]
    first = qkv_ref.shape[1] - heads
    visible = visibility(pos_ref[...])
    for head in range(heads):
        query, key, value = (qkv_ref[i, first + head] for i in range(3))
        grad = grad_ref[:, head * width : (head + 1) * width]
        for i, result in enumerate(head_gradients(visible, query, key, value, grad)):
            out_ref[i, head] = result


def late_backward(pos, qkv, grad):
    _, _, seq, width = qkv.shape
    heads = grad.shape[1] // width
    return pl.pallas_call(
        late_kernel,
        name="late_backward",
        in_specs=[VMEM] * 3,
        out_specs=VMEM,
        out_shape=pltpu.VMEM((3, heads, seq, width), BF16),
        compiler_params=PARAMS,
    )(pos, qkv, grad)


def fill_kernel(late_ref, whole_ref, out_ref, sems):
    late = late_ref.shape[1]
    first = out_ref.shape[1] - late
    puts = [
        pltpu.make_async_copy(late_ref.at[i], out_ref.at[i, pl.ds(first, late)], sems.at[i])
        for i in range(3)
    ]
    for put in puts:
        put.start()
    for put in puts:
        put.wait()


def fill(late, whole):
    return pl.pallas_call(
        fill_kernel,
        name="fill",
        in_specs=[VMEM, ANY],
        out_specs=ANY,
        out_shape=jax.ShapeDtypeStruct(whole.shape, whole.dtype),
        scratch_shapes=[pltpu.SemaphoreType.DMA((3,))],
        input_output_aliases={1: 0},
        compiler_params=PARAMS,
    )(late, whole)


def project_kernel(terms, splits, *refs):
    count = 1 + max(number for number, _ in terms)
    weights, grads = refs[:count], refs[count : count + len(terms)]
    refs = refs[count + len(terms) :]
    total = refs[0][...]
    for (number, start), grad in zip(terms, grads):
        rows = weights[number][start : start + grad.shape[1]]
        total = total + jnp.dot(grad[...], rows, preferred_element_type=F32)
    at = 0
    for out, size in zip(refs[1:], splits):
        out[...] = total[:, at : at + size].astype(out.dtype)
        at += size


def project(items, total, splits, dtype):
    weights, terms = [], []
    for weight, start, _ in items:
        found = [number for number, known in enumerate(weights) if known is weight]
        if not found:
            weights.append(weight)
        terms.append((found[0] if found else len(weights) - 1, start))
    grads = [grad for _, _, grad in items]
    seq = grads[0].shape[0]
    return pl.pallas_call(
        functools.partial(project_kernel, tuple(terms), splits),
        name="project",
        in_specs=[VMEM] * (len(weights) + len(grads) + 1),
        out_specs=[VMEM] * len(splits),
        out_shape=[jax.ShapeDtypeStruct((seq, size), dtype) for size in splits],
        compiler_params=PARAMS,
    )(*weights, *grads, total)


def counts(options):
    return tuple(len(pieces) for pieces in options)


def grouped(refs, sizes):
    refs = list(refs)
    return [[refs.pop(0) for _ in range(size)] for size in sizes]


def choose_kernel(per_replica, number, step, replicas, *refs):
    chips = len(refs) - 1
    chip, _ = place()
    target = lax.rem(lax.axis_index("dp") + step, replicas)
    index = lax.rem(chip - (target * per_replica + number) + chips, chips)
    for option, ref in enumerate(refs[:-1]):

        @pl.when(index == option)
        def _():
            refs[-1][...] = ref[...]


def choose(replicas, number, step, options):
    chips = len(options)
    return pl.pallas_call(
        functools.partial(choose_kernel, chips // replicas, number, step, replicas),
        name="choose",
        in_specs=[VMEM] * chips,
        out_specs=VMEM,
        out_shape=jax.ShapeDtypeStruct(options[0].shape, options[0].dtype),
        compiler_params=PARAMS,
    )(*options)


def finish_kernel(replicas, sizes, far_sizes, slots, blocks, packed_ref, grad_ref, *refs):
    refs = list(refs)
    acts = [refs.pop(0) for _ in range(replicas)]
    options = grouped(refs, sizes)
    far = grouped(refs[sum(sizes) :], far_sizes)
    out_ref, weight_ref, held, stacked, ready, head_sems, sems = refs[-7:]
    heads, seq, width = held.shape[1:]
    visible = visibility(packed_ref[3 * heads * seq :][:1])
    copies = [
        pltpu.make_async_copy(held.at[:, head], out_ref.at[:, head], head_sems.at[head])
        for head in range(heads)
    ]
    chip, core = place()

    def differentiate(group):
        for head in group:
            query, key, value = (
                packed_ref[(i * heads + head) * seq : (i * heads + head + 1) * seq]
                for i in range(3)
            )
            grad = grad_ref[:, head * width : (head + 1) * width]
            for i, result in enumerate(head_gradients(visible, query, key, value, grad)):
                held[i, head] = result
            copies[head].start()

    for first in range(0, heads, 4):
        pl.when(chip >= 0)(functools.partial(differentiate, range(first, min(first + 4, heads))))

    for number, act in enumerate(acts):
        stacked[number * seq : (number + 1) * seq] = act[...]
    chips = len(sizes) // 2
    size = ready.shape[1]
    spans = [(turn, block * size, size) for turn in range(2 * slots) for block in range(blocks)]
    if size % 256 == 0:
        turn, first, _ = spans.pop()
        spans += [(turn, first, size // 2), (turn, first + size // 2, size // 2)]
    puts = []
    for number, (turn, first, count) in enumerate(spans):
        parity, slot = divmod(turn, slots)
        index = lax.rem(chip - (lax.axis_index("dp") * slots + slot) + chips, chips)

        def part(pieces):
            piece, at = divmod(first, pieces[0].shape[1])
            return pieces[piece][:, at : at + count]

        near = None
        for option, pieces in enumerate(options[parity * chips : (parity + 1) * chips]):
            own = part(pieces)
            near = own if near is None else jnp.where(index == option, own, near)
        left = [near]
        for pieces in far[turn * (replicas - 1) : (turn + 1) * (replicas - 1)]:
            if len(pieces) == 2:
                left.append(jnp.where(index == 1, part(pieces), part(pieces[::-1])))
            else:
                left.append(part(pieces))
        block = dot(jnp.concatenate(left, axis=0), stacked[...], ((0,), (0,))).astype(BF16)
        if number >= 2:
            puts[number - 2].wait()
        place_in = ready.at[number % 2, pl.ds(0, count)]
        place_in[...] = block
        row = (2 * slot + lax.rem(core + parity, 2)) * (size * blocks) + first
        target = weight_ref.at[pl.ds(pl.multiple_of(row, 128), count)]
        puts.append(pltpu.make_async_copy(place_in, target, sems.at[number % 2]))
        puts[-1].start()
    for copy in copies + puts[-2:]:
        copy.wait()


def finish(packed, grad, total, acts, options, far):
    seq, width = grad.shape[0], packed.shape[1]
    heads = grad.shape[1] // width
    replicas, slots = len(acts), len(far) // 2
    far = [pieces for slot in far for pieces in slot]
    columns = acts[0].shape[1]
    features = sum(piece.shape[1] for piece in far[0])
    blocks = max(counts(options))
    size = features // blocks
    args = [*acts, *[piece for pieces in options for piece in pieces]]
    args += [piece for pieces in far for piece in pieces]
    return pl.pallas_call(
        functools.partial(finish_kernel, replicas, counts(options), counts(far), slots, blocks),
        name="finish",
        in_specs=[VMEM] * (2 + len(args)),
        out_specs=[ANY, ANY],
        out_shape=[
            jax.ShapeDtypeStruct((3, total, seq, width), BF16),
            jax.ShapeDtypeStruct((2 * slots * features, columns), BF16),
        ],
        scratch_shapes=[
            pltpu.VMEM((3, heads, seq, width), BF16),
            pltpu.VMEM((replicas * seq, columns), BF16),
            pltpu.VMEM((2, size, columns), BF16),
            pltpu.SemaphoreType.DMA((heads,)),
            pltpu.SemaphoreType.DMA((2,)),
        ],
        compiler_params=PARAMS,
    )(packed, grad, *args)


def pieces_of(features):
    return 2 if features % 256 == 0 else 1


def local(saved_qkv, positions, w_out, grad_out):
    qkv = saved_qkv[0, 0].transpose(0, 2, 1, 3)
    pos = positions[0]
    weight = in_hbm(w_out[0])
    heads, _, width = qkv.shape[1:]
    early = max(1, heads * 8 // 12)
    late = heads - early
    shards = lax.axis_size("st")
    replicas = lax.axis_size("dp")
    chips = shards // 2
    per_replica = chips // replicas

    own = grad_out[0, 0]
    pieces = pieces_of(own.shape[1])
    packed, *parts = pack(pos, qkv, own, early, pieces)
    packed_above = down(packed, "section")
    same = [[own]]
    other = []
    for step in range(1, chips):
        same.append([])
        for piece in range(pieces):
            same[-1].append(rotate(parts[piece], "st", 2 * step))
    other.append([swap(own, "st")])
    for step in range(1, chips):
        other.append([])
        for piece in range(pieces):
            other[-1].append(swap(same[step][piece], "st"))

    attended, total, *far_rows = forward(chips, early, qkv, weight, packed, parts)
    acts = [attended]
    for step in range(1, replicas):
        acts.append(rotate(attended, "dp", step))

    whole = (heads * width,)
    halves = (early * width, late * width)
    depth = own.shape[1] // pieces
    direct, crossed = [], []
    for step in range(1, chips):
        for piece in range(pieces):
            start = piece * depth
            direct.append((far_rows[2 * step - 1], start, same[step][piece]))
            crossed.append((far_rows[2 * step], start, other[step][piece]))
    mate = (far_rows[0], 0, other[0][0])
    (total,) = project([mate] + direct + crossed[:-1], total, whole, F32)
    total = project([crossed[-1]], total, halves, BF16)
    d_early, d_late = total
    d_above = down(d_early, "section")
    grads_late = late_backward(pos, qkv, d_late)
    late_above = down(grads_late, "section")

    split = chips == pieces == 2
    near_far, cross_far = [], []
    for number in range(per_replica):
        straight, swapped = [], []
        for step in range(1, replicas):
            options = [parts[1], same[1][0]] if split else [value for (value,) in same]
            chosen = choose(replicas, number, step, options)
            got = [rotate(chosen, "dp", step)]
            mates = [swap(got[0], "st")]
            if split:
                got.append(rotate(got[0], "st", 2))
                mates.append(swap(got[1], "st"))
            straight.append(got)
            swapped.append(mates)
        near_far.append(straight)
        cross_far.append(swapped)

    begun, grad_weight = finish(
        packed_above, d_above, heads, acts, same + other, near_far + cross_far
    )
    upstream = fill(late_above, begun)
    return (grad_weight[None], upstream.transpose(0, 2, 1, 3)[None, None])


def solution(mesh):
    in_specs = (
        P("section", "dp", None, None, "st", None),
        P("section", "dp", None),
        P("section", None, "st"),
        P("section", "dp", None, "st"),
    )
    out_specs = (P("section", "dp", "st"), P("section", "dp", None, None, "st", None))

    return jax.shard_map(local, mesh=mesh, in_specs=in_specs, out_specs=out_specs, check_vma=False)
```

```python
import functools
import math

import jax
import jax.numpy as jnp
from jax import lax
from jax.experimental import pallas as pl
from jax.experimental.pallas import tpu as pltpu
from jax.sharding import PartitionSpec as P


F32 = jnp.float32
BF16 = jnp.bfloat16
VMEM = pl.BlockSpec(memory_space=pltpu.VMEM)
SMEM = pl.BlockSpec(memory_space=pltpu.SMEM)
ANY = pl.BlockSpec(memory_space=pl.ANY)
PARAMS = pltpu.CompilerParams(vmem_limit_bytes=24 * 2**20)


def in_hbm(value):
    return pltpu.with_memory_space_constraint(value, pltpu.HBM)


def dot(a, b, dims):
    return lax.dot_general(a, b, ((dims[0], dims[1]), ((), ())), preferred_element_type=F32)


def rotate(value, axis, steps):
    count = lax.axis_size(axis)
    return lax.ppermute(value, axis, [(i, (i + steps) % count) for i in range(count)])


def swap(value, axis):
    count = lax.axis_size(axis)
    return lax.ppermute(value, axis, [(i, i ^ 1) for i in range(count)])


def down(value, axis):
    count = lax.axis_size(axis)
    return lax.ppermute(value, axis, [(i, i - 1) for i in range(1, count)])


def visibility(positions):
    seq = positions.shape[-1]
    queries = jnp.broadcast_to(positions.astype(F32), (seq, seq))
    return queries.T <= queries


def softmax(visible, query, key):
    scores = dot(key, query, ((1,), (1,))) * (1.0 / math.sqrt(query.shape[-1]))
    scores = jnp.where(visible, scores, -1e30)
    exponent = jnp.exp(scores - jnp.max(scores, axis=0, keepdims=True))
    return exponent * (1.0 / jnp.sum(exponent, axis=0, keepdims=True))


def pack_kernel(rows, pos_ref, qkv_ref, own_ref, out_ref, *refs):
    parts, (held, sems) = refs[:-2], refs[-2:]
    gets = [pltpu.make_async_copy(pos_ref, held, sems.at[3])]
    gets += [
        pltpu.make_async_copy(
            qkv_ref.at[i, pl.ds(0, rows)], out_ref.at[pl.ds(i * rows, rows)], sems.at[i]
        )
        for i in range(3)
    ]
    for number, part in enumerate(parts):
        size = part.shape[1]
        gets.append(
            pltpu.make_async_copy(
                own_ref.at[:, pl.ds(number * size, size)], part, sems.at[4 + number]
            )
        )
    for get in gets:
        get.start()
    gets[0].wait()
    spare = (out_ref.shape[0] - 3 * rows, out_ref.shape[1])
    out_ref[3 * rows :] = jnp.broadcast_to(held[...].astype(F32), spare).astype(BF16)
    for get in gets[1:]:
        get.wait()


def pack(pos, qkv, own, early, pieces):
    _, _, seq, width = qkv.shape
    rows = early * seq
    part = pltpu.VMEM((seq, own.shape[1] // pieces), BF16)
    return pl.pallas_call(
        functools.partial(pack_kernel, rows),
        name="pack",
        in_specs=[ANY] * 3,
        out_specs=[VMEM] * (1 + pieces),
        out_shape=[pltpu.VMEM((3 * rows + 16, width), BF16)] + [part] * pieces,
        scratch_shapes=[
            pltpu.VMEM(pos.shape, pos.dtype),
            pltpu.SemaphoreType.DMA((4 + pieces,)),
        ],
        compiler_params=PARAMS,
    )(in_hbm(pos), in_hbm(qkv.reshape(3, -1, width)), in_hbm(own))


def place():
    me = lax.axis_index("st")
    return lax.div(me, 2), lax.rem(me, 2)


def rows_of(weight_ref, depth, chips, step, crossed):
    chip, core = place()
    owner = 2 * lax.rem(chip - step + chips, chips) + (1 - core if crossed else core)
    return weight_ref.at[pl.ds(pl.multiple_of(owner * depth, depth), depth)]


def forward_kernel(chips, early, pieces, qkv_ref, weight_ref, packed_ref, *refs):
    parts, refs = refs[:pieces], refs[pieces:]
    out_ref, total_ref = refs[:2]
    kept, (buffer, rows, late_sem, sems) = refs[2:-4], refs[-4:]
    late, seq, width = buffer.shape[1:]
    fetches = [
        pltpu.make_async_copy(
            rows_of(weight_ref, rows.shape[0], chips, number // 2, number % 2),
            target,
            sems.at[number],
        )
        for number, target in enumerate((rows, *kept))
    ]
    get = pltpu.make_async_copy(qkv_ref.at[:, pl.ds(early, late)], buffer, late_sem.at[0])
    get.start()
    for fetch in fetches:
        fetch.start()
    visible = visibility(packed_ref[3 * early * seq :][:1])
    chip, _ = place()

    def attend(heads):
        for head in heads:
            if head < early:
                query, key, value = (
                    packed_ref[(i * early + head) * seq : (i * early + head + 1) * seq]
                    for i in range(3)
                )
            else:
                query, key, value = (buffer[i, head - early] for i in range(3))
            probs = softmax(visible, query, key)
            attended = dot(probs.astype(BF16), value, ((0,), (0,)))
            out_ref[:, head * width : (head + 1) * width] = attended.astype(BF16)

    for first in range(0, early, 4):
        pl.when(chip >= 0)(functools.partial(attend, range(first, min(first + 4, early))))
    get.wait()
    attend(range(early, early + late))
    fetches[0].wait()
    size = rows.shape[0] // pieces
    total = None
    for number, part in enumerate(parts):
        product = jnp.dot(
            part[...], rows[number * size : (number + 1) * size], preferred_element_type=F32
        )
        total = product if total is None else total + product
    total_ref[...] = total
    for fetch in fetches[1:]:
        fetch.wait()


def forward(chips, early, qkv, weight, packed, parts):
    _, heads, seq, width = qkv.shape
    depth, columns = len(parts) * parts[0].shape[1], weight.shape[1]
    count = 2 * chips - 1
    return pl.pallas_call(
        functools.partial(forward_kernel, chips, early, len(parts)),
        name="forward",
        in_specs=[ANY, ANY] + [VMEM] * (1 + len(parts)),
        out_specs=[VMEM] * (2 + count),
        out_shape=[
            jax.ShapeDtypeStruct((seq, heads * width), BF16),
            jax.ShapeDtypeStruct((seq, columns), F32),
        ]
        + [pltpu.VMEM((depth, columns), BF16)] * count,
        scratch_shapes=[
            pltpu.VMEM((3, heads - early, seq, width), BF16),
            pltpu.VMEM((depth, columns), BF16),
            pltpu.SemaphoreType.DMA((1,)),
            pltpu.SemaphoreType.DMA((count + 1,)),
        ],
        compiler_params=PARAMS,
    )(in_hbm(qkv), weight, packed, *parts)


def head_gradients(visible, query, key, value, grad):
    scale = 1.0 / math.sqrt(query.shape[-1])
    probs = softmax(visible, query, key)
    d_value = dot(probs.astype(BF16), grad, ((1,), (0,)))
    d_probs = dot(value, grad, ((1,), (1,)))
    row_dot = jnp.sum(probs * d_probs, axis=0, keepdims=True)
    d_scores = (probs * (d_probs - row_dot)).astype(BF16)
    d_key = dot(d_scores, query, ((1,), (0,))) * scale
    d_query = dot(d_scores, key, ((0,), (0,))) * scale
    return d_query.astype(BF16), d_key.astype(BF16), d_value.astype(BF16)


def late_kernel(pos_ref, qkv_ref, grad_ref, out_ref):
    heads, _, width = out_ref.shape[1:]
    first = qkv_ref.shape[1] - heads
    visible = visibility(pos_ref[...])
    for head in range(heads):
        query, key, value = (qkv_ref[i, first + head] for i in range(3))
        grad = grad_ref[:, head * width : (head + 1) * width]
        for i, result in enumerate(head_gradients(visible, query, key, value, grad)):
            out_ref[i, head] = result


def late_backward(pos, qkv, grad):
    _, _, seq, width = qkv.shape
    heads = grad.shape[1] // width
    return pl.pallas_call(
        late_kernel,
        name="late_backward",
        in_specs=[VMEM] * 3,
        out_specs=VMEM,
        out_shape=pltpu.VMEM((3, heads, seq, width), BF16),
        compiler_params=PARAMS,
    )(pos, qkv, grad)


def fill_kernel(late_ref, whole_ref, out_ref, sems):
    late = late_ref.shape[1]
    first = out_ref.shape[1] - late
    puts = [
        pltpu.make_async_copy(late_ref.at[i], out_ref.at[i, pl.ds(first, late)], sems.at[i])
        for i in range(3)
    ]
    for put in puts:
        put.start()
    for put in puts:
        put.wait()


def fill(late, whole):
    return pl.pallas_call(
        fill_kernel,
        name="fill",
        in_specs=[VMEM, ANY],
        out_specs=ANY,
        out_shape=jax.ShapeDtypeStruct(whole.shape, whole.dtype),
        scratch_shapes=[pltpu.SemaphoreType.DMA((3,))],
        input_output_aliases={1: 0},
        compiler_params=PARAMS,
    )(late, whole)


def project_kernel(terms, splits, *refs):
    count = 1 + max(number for number, _ in terms)
    weights, grads = refs[:count], refs[count : count + len(terms)]
    refs = refs[count + len(terms) :]
    total = refs[0][...]
    for (number, start), grad in zip(terms, grads):
        rows = weights[number][start : start + grad.shape[1]]
        total = total + jnp.dot(grad[...], rows, preferred_element_type=F32)
    at = 0
    for out, size in zip(refs[1:], splits):
        out[...] = total[:, at : at + size].astype(out.dtype)
        at += size


def project(items, total, splits, dtype):
    weights, terms = [], []
    for weight, start, _ in items:
        found = [number for number, known in enumerate(weights) if known is weight]
        if not found:
            weights.append(weight)
        terms.append((found[0] if found else len(weights) - 1, start))
    grads = [grad for _, _, grad in items]
    seq = grads[0].shape[0]
    return pl.pallas_call(
        functools.partial(project_kernel, tuple(terms), splits),
        name="project",
        in_specs=[VMEM] * (len(weights) + len(grads) + 1),
        out_specs=[VMEM] * len(splits),
        out_shape=[jax.ShapeDtypeStruct((seq, size), dtype) for size in splits],
        compiler_params=PARAMS,
    )(*weights, *grads, total)


def counts(options):
    return tuple(len(pieces) for pieces in options)


def grouped(refs, sizes):
    refs = list(refs)
    return [[refs.pop(0) for _ in range(size)] for size in sizes]


def choose_kernel(per_replica, number, step, replicas, *refs):
    chips = len(refs) - 1
    chip, _ = place()
    target = lax.rem(lax.axis_index("dp") + step, replicas)
    index = lax.rem(chip - (target * per_replica + number) + chips, chips)
    for option, ref in enumerate(refs[:-1]):

        @pl.when(index == option)
        def _():
            refs[-1][...] = ref[...]


def choose(replicas, number, step, options):
    chips = len(options)
    return pl.pallas_call(
        functools.partial(choose_kernel, chips // replicas, number, step, replicas),
        name="choose",
        in_specs=[VMEM] * chips,
        out_specs=VMEM,
        out_shape=jax.ShapeDtypeStruct(options[0].shape, options[0].dtype),
        compiler_params=PARAMS,
    )(*options)


def finish_kernel(replicas, sizes, far_sizes, slots, blocks, packed_ref, grad_ref, *refs):
    refs = list(refs)
    acts = [refs.pop(0) for _ in range(replicas)]
    options = grouped(refs, sizes)
    far = grouped(refs[sum(sizes) :], far_sizes)
    out_ref, weight_ref, held, stacked, ready, head_sems, sems = refs[-7:]
    heads, seq, width = held.shape[1:]
    copies = []
    visible = visibility(packed_ref[3 * heads * seq :][:1])
    for head in range(heads):
        query, key, value = (
            packed_ref[(i * heads + head) * seq : (i * heads + head + 1) * seq] for i in range(3)
        )
        grad = grad_ref[:, head * width : (head + 1) * width]
        for i, result in enumerate(head_gradients(visible, query, key, value, grad)):
            held[i, head] = result
        copies.append(
            pltpu.make_async_copy(held.at[:, head], out_ref.at[:, head], head_sems.at[head])
        )
        copies[-1].start()

    for number, act in enumerate(acts):
        stacked[number * seq : (number + 1) * seq] = act[...]
    chip, core = place()
    chips = len(sizes) // 2
    size = ready.shape[1]
    spans = [(turn, block * size, size) for turn in range(2 * slots) for block in range(blocks)]
    puts = []
    for number, (turn, first, count) in enumerate(spans):
        parity, slot = divmod(turn, slots)
        index = lax.rem(chip - (lax.axis_index("dp") * slots + slot) + chips, chips)

        def part(pieces):
            piece, at = divmod(first, pieces[0].shape[1])
            return pieces[piece][:, at : at + count]

        near = None
        for option, pieces in enumerate(options[parity * chips : (parity + 1) * chips]):
            own = part(pieces)
            near = own if near is None else jnp.where(index == option, own, near)
        left = [near]
        for pieces in far[turn * (replicas - 1) : (turn + 1) * (replicas - 1)]:
            if len(pieces) == 2:
                left.append(jnp.where(index == 1, part(pieces), part(pieces[::-1])))
            else:
                left.append(part(pieces))
        block = dot(jnp.concatenate(left, axis=0), stacked[...], ((0,), (0,))).astype(BF16)
        if number >= 2:
            puts[number - 2].wait()
        place_in = ready.at[number % 2, pl.ds(0, count)]
        place_in[...] = block
        row = (2 * slot + lax.rem(core + parity, 2)) * (size * blocks) + first
        target = weight_ref.at[pl.ds(pl.multiple_of(row, 128), count)]
        puts.append(pltpu.make_async_copy(place_in, target, sems.at[number % 2]))
        puts[-1].start()
    for copy in copies + puts[-2:]:
        copy.wait()


def finish(packed, grad, total, acts, options, far):
    seq, width = grad.shape[0], packed.shape[1]
    heads = grad.shape[1] // width
    replicas, slots = len(acts), len(far) // 2
    far = [pieces for slot in far for pieces in slot]
    columns = acts[0].shape[1]
    features = sum(piece.shape[1] for piece in far[0])
    blocks = max(counts(options))
    size = features // blocks
    args = [*acts, *[piece for pieces in options for piece in pieces]]
    args += [piece for pieces in far for piece in pieces]
    return pl.pallas_call(
        functools.partial(finish_kernel, replicas, counts(options), counts(far), slots, blocks),
        name="finish",
        in_specs=[VMEM] * (2 + len(args)),
        out_specs=[ANY, ANY],
        out_shape=[
            jax.ShapeDtypeStruct((3, total, seq, width), BF16),
            jax.ShapeDtypeStruct((2 * slots * features, columns), BF16),
        ],
        scratch_shapes=[
            pltpu.VMEM((3, heads, seq, width), BF16),
            pltpu.VMEM((replicas * seq, columns), BF16),
            pltpu.VMEM((2, size, columns), BF16),
            pltpu.SemaphoreType.DMA((heads,)),
            pltpu.SemaphoreType.DMA((2,)),
        ],
        compiler_params=PARAMS,
    )(packed, grad, *args)


def pieces_of(features):
    return 2 if features % 256 == 0 else 1


def local(saved_qkv, positions, w_out, grad_out):
    qkv = saved_qkv[0, 0].transpose(0, 2, 1, 3)
    pos = positions[0]
    weight = in_hbm(w_out[0])
    heads, _, width = qkv.shape[1:]
    early = max(1, heads * 8 // 12)
    late = heads - early
    shards = lax.axis_size("st")
    replicas = lax.axis_size("dp")
    chips = shards // 2
    per_replica = chips // replicas

    own = grad_out[0, 0]
    pieces = pieces_of(own.shape[1])
    packed, *parts = pack(pos, qkv, own, early, pieces)
    packed_above = down(packed, "section")
    same = [[own]]
    other = []
    for step in range(1, chips):
        same.append([])
        for piece in range(pieces):
            same[-1].append(rotate(parts[piece], "st", 2 * step))
    other.append([swap(own, "st")])
    for step in range(1, chips):
        other.append([])
        for piece in range(pieces):
            other[-1].append(swap(same[step][piece], "st"))

    attended, total, *far_rows = forward(chips, early, qkv, weight, packed, parts)
    acts = [attended]
    for step in range(1, replicas):
        acts.append(rotate(attended, "dp", step))

    whole = (heads * width,)
    halves = (early * width, late * width)
    depth = own.shape[1] // pieces
    direct, crossed = [], []
    for step in range(1, chips):
        for piece in range(pieces):
            start = piece * depth
            direct.append((far_rows[2 * step - 1], start, same[step][piece]))
            crossed.append((far_rows[2 * step], start, other[step][piece]))
    mate = (far_rows[0], 0, other[0][0])
    (total,) = project([mate] + direct + crossed[:-1], total, whole, F32)
    total = project([crossed[-1]], total, halves, BF16)
    d_early, d_late = total
    d_above = down(d_early, "section")
    grads_late = late_backward(pos, qkv, d_late)
    late_above = down(grads_late, "section")

    split = chips == pieces == 2
    near_far, cross_far = [], []
    for number in range(per_replica):
        straight, swapped = [], []
        for step in range(1, replicas):
            options = [parts[1], same[1][0]] if split else [value for (value,) in same]
            chosen = choose(replicas, number, step, options)
            got = [rotate(chosen, "dp", step)]
            mates = [swap(got[0], "st")]
            if split:
                got.append(rotate(got[0], "st", 2))
                mates.append(swap(got[1], "st"))
            straight.append(got)
            swapped.append(mates)
        near_far.append(straight)
        cross_far.append(swapped)

    begun, grad_weight = finish(
        packed_above, d_above, heads, acts, same + other, near_far + cross_far
    )
    upstream = fill(late_above, begun)
    return (grad_weight[None], upstream.transpose(0, 2, 1, 3)[None, None])


def solution(mesh):
    in_specs = (
        P("section", "dp", None, None, "st", None),
        P("section", "dp", None),
        P("section", None, "st"),
        P("section", "dp", None, "st"),
    )
    out_specs = (P("section", "dp", "st"), P("section", "dp", None, None, "st", None))

    return jax.shard_map(local, mesh=mesh, in_specs=in_specs, out_specs=out_specs, check_vma=False)
```
